32 devices in a mesh: rep: 2 (over x), grp: 4 (over y, core), fs: 4 (over z).
Axes of the slice: x: 2, y: 2, z: 4, core: 2. Of those that a mesh axis runs over, the one named last changes fastest.
Arguments:
- prompt_input_rows: bfloat16 [2, 4, 512, 2048], P('rep', 'fs', 'grp'), may hold values from -6 to 6
- continuation_input: bfloat16 [2, 4, 4, 256, 2048], P('rep', 'fs', 'grp'), may hold values from -6 to 6
- prompt_group_adapter: int32 [2, 4], P('rep', 'fs'), may hold values from 0 to 7
- continuation_adapter: int32 [2, 4, 4], P('rep', 'fs', 'grp'), may hold values from 0 to 7
- first_norm_scale: float32 [2048], replicated, may hold values from 0.1 to 1.9
- first_norm_bias: float32 [2048], replicated, may hold values from -1.75 to 1.75
- second_norm_scale: float32 [2048], replicated, may hold values from 0.1 to 1.9
- second_norm_bias: float32 [2048], replicated, may hold values from -1.75 to 1.75
- frozen_query_key_value: bfloat16 [2048, 6144], P(('grp', 'fs')), may hold values from -0.125 to 0.125
- frozen_output_weight: bfloat16 [2048, 2048], P(('grp', 'fs')), may hold values from -2 to 2
- frozen_up_weight: bfloat16 [2048, 8192], P(('grp', 'fs')), may hold values from -0.125 to 0.125
- frozen_down_weight: bfloat16 [8192, 2048], P(('grp', 'fs')), may hold values from -0.0625 to 0.0625
- adapter_attention_input: bfloat16 [8, 4, 2048, 16], replicated, may hold values from -0.125 to 0.125
- adapter_attention_output: bfloat16 [8, 4, 16, 2048], replicated, may hold values from -1.5 to 1.5
- adapter_up_input: bfloat16 [8, 2048, 16], replicated, may hold values from -0.125 to 0.125
- adapter_up_output: bfloat16 [8, 16, 8192], replicated, may hold values from -1 to 1
- adapter_down_input: bfloat16 [8, 8192, 16], replicated, may hold values from -0.0625 to 0.0625
- adapter_down_output: bfloat16 [8, 16, 2048], replicated, may hold values from -1.5 to 1.5
- prompt_cotangent: bfloat16 [2, 4, 512, 2048], P('rep', 'fs', 'grp'), may hold values from -6 to 6
- continuation_cotangent: bfloat16 [2, 4, 4, 256, 2048], P('rep', 'fs', 'grp'), may hold values from -6 to 6
Outputs:
- out_prompt: bfloat16 [2, 4, 512, 2048], P('rep', 'fs', 'grp')
- out_cont: bfloat16 [2, 4, 4, 256, 2048], P('rep', 'fs', 'grp')
- grad_prompt_in: bfloat16 [2, 4, 512, 2048], P('rep', 'fs', 'grp')
- grad_cont_in: bfloat16 [2, 4, 4, 256, 2048], P('rep', 'fs', 'grp')
- grad_a_attn: float32 [8, 4, 2048, 16], P('fs')
- grad_b_attn: float32 [8, 4, 16, 2048], P('fs')
- grad_a_up: float32 [8, 2048, 16], P('fs')
- grad_b_up: float32 [8, 16, 8192], P('fs')
- grad_a_down: float32 [8, 8192, 16], P('fs')
- grad_b_down: float32 [8, 16, 2048], P('fs')
The draws below stay inside these ranges and needn't reach their ends.
All inputs are finite; a program needn't handle non-finite values.
Results may differ from the reference program's by a relative error of at most 0.019.
Values may be sent and summed in bfloat16 or wider, within the bound.
A program may use at most 384 MiB of HBM per device.

```python
import jax
import jax.numpy as jnp
from jax import lax

MODEL_DIMENSION = 2048
HEADS = 16
FEEDFWD_UNITS = 8192
HDIM = 128
ADAPTER_RANK = 16
ADAPTER_COUNT = 8
CLEN = 256
PROMPT = 512
CONTS = 4
KEYS_DEV = 768
N_REP = 2
N_FS = 4


def with_ends(array, own_key, low, top_value):
    dims = array.shape
    place = [jax.random.randint(jax.random.fold_in(own_key, axis), (), 0, dims[axis]) for axis in range(len(dims))]
    array = array.at[tuple(place)].set(low)
    longest = dims.index(max(dims))
    place[longest] = (place[longest] + 1) % dims[longest]
    return array.at[tuple(place)].set(top_value)


def block_scale(key, extent, shards, low, top_value):
    def one(dim, parts):
        heights = jax.random.uniform(jax.random.fold_in(jax.random.fold_in(key, 6), dim), (parts,), jnp.float32, low / len(shards), top_value / len(shards))
        return jnp.repeat(jnp.exp(heights), extent[dim] // parts).reshape((-1,) + (1,) * (len(extent) - dim - 1))

    loudness = one(*shards[0])
    for cut in shards[1:]:
        loudness = loudness * one(*cut)
    return loudness


def noise(rng, shape, scale, most, split=(), kind=jnp.bfloat16):
    array = scale * jax.random.normal(rng, shape, jnp.float32)
    if split:
        array = array * block_scale(rng, shape, split, -0.22, 0.18)
    return jnp.clip(array, -most, most).astype(kind)


def setup_inputs(seed: int = 0) -> dict:
    seeds = jax.random.split(jax.random.key(seed), 21)
    prompt_input_rows = noise(seeds[0], (N_REP, N_FS, PROMPT, MODEL_DIMENSION), 1.0, 6.0, ((0, 2), (1, 4), (2, 4)))
    continuation_input = noise(seeds[1], (N_REP, N_FS, CONTS, CLEN, MODEL_DIMENSION), 1.0, 6.0, ((0, 2), (1, 4), (2, 4)))
    prompt_group_adapter = with_ends(jax.random.randint(seeds[2], (N_REP, N_FS), 0, ADAPTER_COUNT), jax.random.fold_in(seeds[2], 1), 0, ADAPTER_COUNT - 1).astype(jnp.int32)
    continuation_adapter = with_ends(jax.random.randint(seeds[3], (N_REP, N_FS, CONTS), 0, ADAPTER_COUNT), jax.random.fold_in(seeds[3], 1), 0, ADAPTER_COUNT - 1).astype(jnp.int32)
    first_norm_scale = jnp.clip(1.0 + 0.18 * jax.random.normal(seeds[4], (MODEL_DIMENSION,), jnp.float32), 0.1, 1.9)
    first_norm_bias = noise(seeds[5], (MODEL_DIMENSION,), 0.3, 1.75, (), jnp.float32)
    second_norm_scale = jnp.clip(1.0 + 0.18 * jax.random.normal(seeds[6], (MODEL_DIMENSION,), jnp.float32), 0.1, 1.9)
    second_norm_bias = noise(seeds[7], (MODEL_DIMENSION,), 0.3, 1.75, (), jnp.float32)
    frozen_query_key_value = noise(seeds[8], (MODEL_DIMENSION, 3 * MODEL_DIMENSION), MODEL_DIMENSION ** -0.5, 0.125, ((0, 16),))
    frozen_output_weight = noise(seeds[9], (MODEL_DIMENSION, MODEL_DIMENSION), (MODEL_DIMENSION * 4 // KEYS_DEV) ** -0.5, 2.0, ((0, 16),))
    frozen_up_weight = noise(seeds[10], (MODEL_DIMENSION, FEEDFWD_UNITS), MODEL_DIMENSION ** -0.5, 0.125, ((0, 16),))
    frozen_down_weight = noise(seeds[11], (FEEDFWD_UNITS, MODEL_DIMENSION), FEEDFWD_UNITS ** -0.5, 0.0625, ((0, 16),))
    adapter_attention_input = noise(seeds[12], (ADAPTER_COUNT, 4, MODEL_DIMENSION, ADAPTER_RANK), MODEL_DIMENSION ** -0.5, 0.125)
    adapter_attention_output = noise(seeds[13], (ADAPTER_COUNT, 4, ADAPTER_RANK, MODEL_DIMENSION), ADAPTER_RANK ** -0.5, 1.5)
    adapter_up_input = noise(seeds[14], (ADAPTER_COUNT, MODEL_DIMENSION, ADAPTER_RANK), MODEL_DIMENSION ** -0.5, 0.125)
    adapter_up_output = noise(seeds[15], (ADAPTER_COUNT, ADAPTER_RANK, FEEDFWD_UNITS), (ADAPTER_RANK * 2) ** -0.5, 1.0)
    adapter_down_input = noise(seeds[16], (ADAPTER_COUNT, FEEDFWD_UNITS, ADAPTER_RANK), FEEDFWD_UNITS ** -0.5, 0.0625)
    adapter_down_output = noise(seeds[17], (ADAPTER_COUNT, ADAPTER_RANK, MODEL_DIMENSION), ADAPTER_RANK ** -0.5, 1.5)
    prompt_cotangent = noise(seeds[18], (N_REP, N_FS, PROMPT, MODEL_DIMENSION), 1.0, 6.0, ((0, 2), (1, 4), (2, 4)))
    continuation_cotangent = noise(seeds[19], (N_REP, N_FS, CONTS, CLEN, MODEL_DIMENSION), 1.0, 6.0, ((0, 2), (1, 4), (2, 4)))
    return {"prompt_input_rows": prompt_input_rows, "continuation_input": continuation_input, "prompt_group_adapter": prompt_group_adapter, "continuation_adapter": continuation_adapter, "first_norm_scale": first_norm_scale, "first_norm_bias": first_norm_bias, "second_norm_scale": second_norm_scale, "second_norm_bias": second_norm_bias, "frozen_query_key_value": frozen_query_key_value, "frozen_output_weight": frozen_output_weight, "frozen_up_weight": frozen_up_weight, "frozen_down_weight": frozen_down_weight, "adapter_attention_input": adapter_attention_input, "adapter_attention_output": adapter_attention_output, "adapter_up_input": adapter_up_input, "adapter_up_output": adapter_up_output, "adapter_down_input": adapter_down_input, "adapter_down_output": adapter_down_output, "prompt_cotangent": prompt_cotangent, "continuation_cotangent": continuation_cotangent}


@jax.custom_vjp
def lowrank_product(v):
    return lax.optimization_barrier(v.astype(jnp.bfloat16)).astype(jnp.float32)

@jax.custom_vjp
def lowrank_pullback(v):
    return v

def low_keep(v):
    return (lowrank_product(v), None)

def low_pass(kept, grad):
    return (grad,)

def back_keep(v):
    return (v, None)

def back_low(kept, grad):
    return (lowrank_product(grad),)
lowrank_product.defvjp(low_keep, low_pass)
lowrank_pullback.defvjp(back_keep, back_low)
exact_precision = lax.Precision.HIGHEST

def layer_norm(values, gain_vec, bias_vec):
    center = values - lax.optimization_barrier(jnp.mean(values, axis=-1, keepdims=True))
    spread = lax.optimization_barrier(jnp.mean(center * center, axis=-1, keepdims=True))
    return center * lax.rsqrt(spread + 1e-05) * gain_vec + bias_vec

def adapted(prompt_rows, continuation_row_list, weight, input_map_table, output_map_table, prompt_id, continuation_identifiers):
    main_prompt = jnp.dot(prompt_rows, weight, precision=exact_precision)
    main_cont = jnp.einsum('cld,de->cle', continuation_row_list, weight, precision=exact_precision)
    low_prompt = lowrank_product(lowrank_pullback(jnp.dot(prompt_rows, input_map_table[prompt_id], precision=exact_precision)))
    lowrank_continuation = lowrank_product(lowrank_pullback(jnp.einsum('wnq,wqz->wnz', continuation_row_list, input_map_table[continuation_identifiers], precision=exact_precision)))
    extra_prompt = jnp.dot(low_prompt, output_map_table[prompt_id], precision=exact_precision)
    addition_continuation = jnp.einsum('utn,unm->utm', lowrank_continuation, output_map_table[continuation_identifiers], precision=exact_precision)
    return (main_prompt + extra_prompt, main_cont + addition_continuation)

def attend(queries, keys, values, allowed):
    row_count = queries.shape[0]
    heads_q = queries.reshape(row_count, HEADS, HDIM)
    heads_k = keys.reshape(keys.shape[0], HEADS, HDIM)
    heads_v = values.reshape(values.shape[0], HEADS, HDIM)
    scores = lowrank_pullback(jnp.einsum('qhd,khd->hqk', heads_q, heads_k, precision=exact_precision) * HDIM ** (-0.5))
    scores = jnp.where(allowed[None], scores, -1e+30)
    chances = lowrank_product(jax.nn.softmax(scores, axis=-1))
    mixture = jnp.einsum('hqk,khd->qhd', chances, heads_v, precision=exact_precision)
    return mixture.reshape(row_count, HEADS * HDIM)

def group_forward(frozen, adapter_tables, prompt_x, cont_x, prompt_id, continuation_identifiers):
    gain_one, bias_one, gain_two, bias_two, frozen_query_key_value, frozen_output_weight, frozen_up_weight, frozen_down_weight = frozen
    a_attn, b_attn, a_up, b_up, a_down, b_down = adapter_tables
    normed_prompt = lowrank_product(layer_norm(prompt_x, gain_one, bias_one))
    normed_cont = lowrank_product(layer_norm(cont_x, gain_one, bias_one))
    projected = []
    for group_membership in range(3):
        block_prompt, block_cont = adapted(normed_prompt, normed_cont, frozen_query_key_value[:, group_membership * MODEL_DIMENSION:(group_membership + 1) * MODEL_DIMENSION], a_attn[:, group_membership], b_attn[:, group_membership], prompt_id, continuation_identifiers)
        projected.append((lowrank_product(lowrank_pullback(block_prompt)), lowrank_product(lowrank_pullback(block_cont))))
    (q_prompt, q_cont), (k_prompt, k_cont), (v_prompt, v_cont) = projected
    attend_saved = jax.checkpoint(attend)
    prompt_allowed = jnp.arange(PROMPT)[:, None] >= jnp.arange(PROMPT)[None, :]
    cont_allowed = jnp.concatenate([jnp.ones((CLEN, PROMPT), dtype=jnp.bool_), jnp.arange(CLEN)[:, None] >= jnp.arange(CLEN)[None, :]], 1)
    mixed_prompt = attend_saved(q_prompt, k_prompt, v_prompt, prompt_allowed)

    def one_cont(members):
        query_rows, key_rows, value_rows = members
        return attend_saved(query_rows, jnp.concatenate([k_prompt, key_rows], 0), jnp.concatenate([v_prompt, value_rows], 0), cont_allowed)
    mixed_cont = lax.map(one_cont, (q_cont, k_cont, v_cont))
    mixed_prompt = lowrank_product(lowrank_pullback(mixed_prompt))
    mixed_cont = lowrank_product(lowrank_pullback(mixed_cont))
    attn_prompt, attn_cont = adapted(mixed_prompt, mixed_cont, frozen_output_weight, a_attn[:, 3], b_attn[:, 3], prompt_id, continuation_identifiers)
    resid_prompt = prompt_x + lowrank_pullback(attn_prompt)
    resid_cont = cont_x + lowrank_pullback(attn_cont)
    normed_two_prompt = lowrank_product(layer_norm(resid_prompt, gain_two, bias_two))
    normed_two_cont = lowrank_product(layer_norm(resid_cont, gain_two, bias_two))
    pre_prompt, pre_cont = adapted(normed_two_prompt, normed_two_cont, frozen_up_weight, a_up, b_up, prompt_id, continuation_identifiers)
    act_prompt = lowrank_product(jax.nn.gelu(lowrank_pullback(pre_prompt), approximate=False))
    act_cont = lowrank_product(jax.nn.gelu(lowrank_pullback(pre_cont), approximate=False))
    mlp_prompt, mlp_cont = adapted(act_prompt, act_cont, frozen_down_weight, a_down, b_down, prompt_id, continuation_identifiers)
    return (resid_prompt + lowrank_pullback(mlp_prompt), resid_cont + lowrank_pullback(mlp_cont))

def reference(prompt_input_rows, continuation_input, prompt_group_adapter, continuation_adapter, first_norm_scale, first_norm_bias, second_norm_scale, second_norm_bias, frozen_query_key_value, frozen_output_weight, frozen_up_weight, frozen_down_weight, adapter_attention_input, adapter_attention_output, adapter_up_input, adapter_up_output, adapter_down_input, adapter_down_output, prompt_cotangent, continuation_cotangent):
    groups = N_REP * N_FS
    frozen = tuple((group_membership.astype(jnp.float32) for group_membership in (first_norm_scale, first_norm_bias, second_norm_scale, second_norm_bias, frozen_query_key_value, frozen_output_weight, frozen_up_weight, frozen_down_weight)))
    adapter_tables = tuple((group_membership.astype(jnp.float32) for group_membership in (adapter_attention_input, adapter_attention_output, adapter_up_input, adapter_up_output, adapter_down_input, adapter_down_output)))
    prompt_x = prompt_input_rows.astype(jnp.float32).reshape(groups, PROMPT, MODEL_DIMENSION)
    cont_x = continuation_input.astype(jnp.float32).reshape(groups, CONTS, CLEN, MODEL_DIMENSION)
    prompt_ids = prompt_group_adapter.reshape(groups).astype(jnp.int32)
    continuation_identifiers = continuation_adapter.reshape(groups, CONTS).astype(jnp.int32)
    group_saved = jax.checkpoint(group_forward)

    def whole(prompt_all, cont_all, table_set):

        def one_group(members):
            return group_saved(frozen, table_set, members[0], members[1], members[2], members[3])
        return lax.map(one_group, (prompt_all, cont_all, prompt_ids, continuation_identifiers))
    outputs, pullback = jax.vjp(whole, prompt_x, cont_x, adapter_tables)
    cotangents = (prompt_cotangent.astype(jnp.float32).reshape(groups, PROMPT, MODEL_DIMENSION), continuation_cotangent.astype(jnp.float32).reshape(groups, CONTS, CLEN, MODEL_DIMENSION))
    grad_prompt, grad_cont, grad_tables = pullback(cotangents)
    return (outputs[0].reshape(N_REP, N_FS, PROMPT, MODEL_DIMENSION).astype(jnp.bfloat16), outputs[1].reshape(N_REP, N_FS, CONTS, CLEN, MODEL_DIMENSION).astype(jnp.bfloat16), grad_prompt.reshape(N_REP, N_FS, PROMPT, MODEL_DIMENSION).astype(jnp.bfloat16), grad_cont.reshape(N_REP, N_FS, CONTS, CLEN, MODEL_DIMENSION).astype(jnp.bfloat16), grad_tables[0], grad_tables[1], grad_tables[2], grad_tables[3], grad_tables[4], grad_tables[5])
```

```python
import functools
import math

import jax
import jax.numpy as jnp
from jax import lax
from jax.experimental import pallas as pl
from jax.experimental.pallas import tpu as pltpu
from jax.sharding import PartitionSpec as P

HEADS = 16
HDIM = 128
RANK = 16
NEG_FILL = -1e30
BF = jnp.bfloat16
F32 = jnp.float32
MESH = pl.DeviceIdType.MESH
BLOCK = 512


def mm(a, b):
    return jnp.dot(a, b, preferred_element_type=F32)


def mm_nt(a, b):
    return lax.dot_general(a, b, (((1,), (1,)), ((), ())), preferred_element_type=F32)


def mm_tn(a, b):
    return lax.dot_general(a, b, (((0,), (0,)), ((), ())), preferred_element_type=F32)


def norm_stats(values):
    center = values - jnp.mean(values, axis=-1, keepdims=True)
    spread = jnp.mean(center * center, axis=-1, keepdims=True)
    rstd = lax.rsqrt(spread + 1e-05)
    return center * rstd, rstd


def norm_back(hat, rstd, gain, grad):
    e = grad * gain
    return (
        e - jnp.mean(e, axis=-1, keepdims=True) - hat * jnp.mean(e * hat, axis=-1, keepdims=True)
    ) * rstd


def split_heads(block):
    return block.reshape(block.shape[0], -1, HDIM)


def masked_scores(query_part, key_part, allowed):
    scores = jnp.einsum(
        "qhd,khd->hqk",
        split_heads(query_part),
        split_heads(key_part),
        preferred_element_type=F32,
    ) * HDIM ** (-0.5)
    return jnp.where(allowed[None], scores, NEG_FILL)


def attend_forward(query_part, key_part, value_part, allowed):
    scores = masked_scores(query_part, key_part, allowed)
    row_peak = jnp.max(scores, axis=-1, keepdims=True)
    raised = jnp.exp(scores - row_peak)
    row_mass = jnp.sum(raised, axis=-1, keepdims=True)
    chances_low = (raised / row_mass).astype(BF)
    mixture = jnp.einsum(
        "hqk,khd->qhd", chances_low, split_heads(value_part), preferred_element_type=F32
    )
    return (mixture.reshape(mixture.shape[0], -1), (row_peak + jnp.log(row_mass))[:, :, 0])


def attend_backward(query_part, key_part, value_part, grad_part, logsum, allowed):
    scores = masked_scores(query_part, key_part, allowed)
    chances = jnp.exp(scores - logsum[:, :, None])
    heads_grad = split_heads(grad_part)
    grad_chances = jnp.einsum(
        "qhd,khd->hqk", heads_grad, split_heads(value_part), preferred_element_type=F32
    )
    inner_sum = jnp.sum(chances * grad_chances, axis=-1, keepdims=True)
    grad_scores = (chances * (grad_chances - inner_sum)).astype(BF)
    factor = HDIM ** (-0.5)
    grad_query = (
        jnp.einsum("hqk,khd->qhd", grad_scores, split_heads(key_part), preferred_element_type=F32)
        * factor
    )
    grad_key = (
        jnp.einsum("hqk,qhd->khd", grad_scores, split_heads(query_part), preferred_element_type=F32)
        * factor
    )
    grad_value = jnp.einsum(
        "hqk,qhd->khd", chances.astype(BF), heads_grad, preferred_element_type=F32
    )
    return (
        grad_query.reshape(grad_query.shape[0], -1),
        grad_key.reshape(grad_key.shape[0], -1),
        grad_value.reshape(grad_value.shape[0], -1),
    )


def pick_rows(table, ids):
    return jnp.concatenate(
        [lax.dynamic_index_in_dim(table, i, 0, keepdims=False) for i in ids], 0
    )


def spread_rows(grads, order, ids):
    owner = jnp.repeat(jnp.stack(ids), RANK)
    rank = jnp.arange(RANK * len(ids)) % RANK
    hot = (order[:, None] == (owner * RANK + rank)[None, :]).astype(BF)
    return mm(hot, grads.astype(BF)).astype(BF)


class Gather:
    def __init__(self, n_fs, count, src, dst, sems, lag=2, away=48):
        (self.zs, self.zr, self.ys, self.yr, self.xs, self.xr) = sems[:6]
        (self.cs, self.cr, self.ds, self.dr, self.loc) = sems[6:]
        self.nz, self.count, self.src, self.dst = n_fs, count, src, dst
        self.lag, self.slots, self.last = lag, 2 * lag, n_fs + 2
        self.rows = src.shape[1]
        rep, grp = lax.axis_index("rep"), lax.axis_index("grp")
        self.z = lax.axis_index("fs")
        self.y, self.c, plane = grp // 2, grp % 2, rep % 2
        self.far_rep = rep + 1 - 2 * plane
        self.far_core = self.y * 2 + 1 - self.c
        self.far_row = (1 - self.y) * 2 + self.c
        self.own = grp * n_fs + self.z
        self.away, self.stay = away, self.rows - away
        self.in_first = pl.multiple_of(away * plane, 8)
        self.out_first = pl.multiple_of(self.stay * plane, 8)
        self.far_first = pl.multiple_of(self.stay * (1 - plane), 8)

    @staticmethod
    def semaphores(n_fs, lag=2):
        slots, dma = 2 * lag, pltpu.SemaphoreType.DMA
        return (
            [dma((2 * slots, 2, n_fs)), dma((2 * slots, n_fs))]
            + [dma((slots, n_fs))] * 2
            + [dma((slots, 2 * n_fs))] * 6
            + [dma((slots,))]
        )

    def barrier(self):
        sem = pltpu.get_barrier_semaphore()

        def greet(**where):
            pl.semaphore_signal(sem, 1, device_id=where, device_id_type=MESH)

        greet(rep=self.far_rep)
        greet(grp=self.far_core)
        greet(grp=self.far_row)
        below, above = self.z > 0, self.z < self.nz - 1
        pl.when(below)(lambda: greet(fs=self.z - 1))
        pl.when(above)(lambda: greet(fs=self.z + 1))
        pl.semaphore_wait(sem, 3 + below.astype(jnp.int32) + above.astype(jnp.int32))

    def at_distance(self, d):
        if d < 0 or d >= self.nz:
            return []
        if d == 0:
            return [(None, self.z, 0)]
        return [(self.z >= d, self.z - d, 1), (self.z < self.nz - d, self.z + d, -1)]

    def shard(self, other, fs, core):
        row = 1 - self.y if other else self.y
        return (row * 2 + core) * self.nz + fs

    def send(self, j, shard, first, size, sems, own=False, **where):
        rows = pl.ds(first, size)
        return pltpu.make_async_remote_copy(
            self.src.at[j, rows] if own else self.dst.at[j, shard, rows],
            self.dst.at[j, shard, rows],
            *sems,
            device_id=where,
            device_id_type=MESH,
        )

    def keep(self, j, t):
        sem = self.loc.at[lax.rem(t, self.slots)]
        return pltpu.make_async_copy(self.src.at[j], self.dst.at[j, self.own], sem)

    def sends(self, a, j, t):
        todo, nz, k, kz = [], self.nz, lax.rem(t, self.slots), lax.rem(t, 2 * self.slots)
        inner, outer, far = (self.in_first, self.stay), (self.out_first, self.away), self.far_first

        def both(left, right):
            return right if left is None else jnp.logical_and(left, right)

        for ok, fs, way in self.at_distance(a):
            shard, own = self.shard(0, fs, self.c), a == 0
            if way >= 0:
                sems = (self.zs.at[kz, 0, fs], self.zr.at[kz, fs])
                up = self.send(j, shard, *inner, sems, own, fs=self.z + 1)
                todo.append((both(ok, self.z < nz - 1), up))
            if way <= 0:
                sems = (self.zs.at[kz, 1, fs], self.zr.at[kz, fs])
                down = self.send(j, shard, *inner, sems, own, fs=self.z - 1)
                todo.append((both(ok, self.z > 0), down))
            sems = (self.ys.at[k, fs], self.yr.at[k, fs])
            todo.append((ok, self.send(j, shard, *inner, sems, own, grp=self.far_row)))
            if not own:
                sems = (self.xs.at[k, fs], self.xr.at[k, fs])
                todo.append((ok, self.send(j, shard, *outer, sems, rep=self.far_rep)))
            sems = (self.cs.at[k, fs], self.cr.at[k, fs])
            size = (0, self.rows) if own else inner
            todo.append((ok, self.send(j, shard, *size, sems, own, grp=self.far_core)))
        for ok, fs, _ in self.at_distance(a - 1):
            shard = self.shard(1, fs, self.c)
            sems = (self.xs.at[k, nz + fs], self.xr.at[k, nz + fs])
            todo.append((ok, self.send(j, shard, *outer, sems, rep=self.far_rep)))
            sems = (self.cs.at[k, nz + fs], self.cr.at[k, nz + fs])
            todo.append((ok, self.send(j, shard, *inner, sems, grp=self.far_core)))
        for other in (0, 1):
            for ok, fs, way in self.at_distance(a - 1 - other):
                if way or other:
                    i = other * nz + fs
                    sems = (self.ds.at[k, i], self.dr.at[k, i])
                    shard = self.shard(other, fs, self.c)
                    core = self.send(j, shard, far, self.away, sems, grp=self.far_core)
                    todo.append((ok, core))
        return todo

    def arrivals(self, a, j, t):
        todo, nz, k, kz = [], self.nz, lax.rem(t, self.slots), lax.rem(t, 2 * self.slots)
        inner, far = (self.in_first, self.stay), (self.far_first, self.away)

        def expect(ok, shard, first, size, sem):
            ref = self.dst.at[j, shard, pl.ds(first, size)]
            todo.append((ok, pltpu.make_async_copy(ref, ref, sem)))

        for ok, fs, way in self.at_distance(a):
            if way:
                expect(ok, self.shard(0, fs, self.c), *inner, self.zr.at[kz, fs])
        for ok, fs, _ in self.at_distance(a - 1):
            expect(ok, self.shard(1, fs, self.c), *inner, self.yr.at[k, fs])
        for other in (0, 1):
            for ok, fs, way in self.at_distance(a - 1 - other):
                i = other * nz + fs
                if way or other:
                    expect(ok, self.shard(other, fs, self.c), *far, self.xr.at[k, i])
                size = inner if way or other else (0, self.rows)
                expect(ok, self.shard(other, fs, 1 - self.c), *size, self.cr.at[k, i])
            for ok, fs, way in self.at_distance(a - 2 - other):
                if way or other:
                    i = other * nz + fs
                    expect(ok, self.shard(other, fs, 1 - self.c), *far, self.dr.at[k, i])
        return todo

    def run(self, early=None, compute=None):
        lag = self.lag

        def act(ok, fn):
            if ok is None:
                fn()
            else:
                pl.when(ok)(fn)

        def finish(a, j, t):
            for ok, copy in self.sends(a - 1, j, t):
                act(ok, copy.wait_send)
            for ok, copy in self.arrivals(a, j, t):
                act(ok, copy.wait)
            if a == 1:
                self.keep(j, t).wait()

        def begin(a, j, t):
            for ok, copy in self.sends(a, j, t):
                act(ok, copy.start)
            if a == 0:
                self.keep(j, t).start()

        def tick(t, carry):
            for a in range(self.last, 0, -1):
                j = t - lag * a
                pl.when((j >= 0) & (j < self.count))(functools.partial(finish, a, j, t - lag))
            for a in range(self.last - 1, -1, -1):
                j = t - lag * a
                pl.when((j >= 0) & (j < self.count))(functools.partial(begin, a, j, t))
            if early is not None:
                early(t)
            if compute is not None:
                j = t - lag * self.last
                pl.when(j >= 0)(functools.partial(compute, j))
            return carry

        lax.fori_loop(0, self.count + lag * self.last + (compute is not None), tick, 0)


def gather_blocks(blocks, n_fs, n_shard, name):
    count, rows, width = blocks.shape

    def kernel(src, dst, *sems):
        engine = Gather(n_fs, count, src, dst, sems)
        engine.barrier()
        engine.run()

    return pl.pallas_call(
        kernel,
        out_shape=jax.ShapeDtypeStruct((count, n_shard, rows, width), BF),
        in_specs=[pl.BlockSpec(memory_space=pl.ANY)],
        out_specs=pl.BlockSpec(memory_space=pl.ANY),
        scratch_shapes=Gather.semaphores(n_fs),
        compiler_params=pltpu.CompilerParams(collective_id=0, has_side_effects=True),
        name=name,
    )(blocks)


def make_body(sizes):
    n_rep, n_grp, n_fs = sizes
    n_shard = n_grp * n_fs

    def reduce_tables(grads, ids, count):
        per, r_lo, width = count // n_fs, RANK // n_grp, grads.shape[1]
        order = jnp.arange(count * RANK).reshape(n_fs, per, n_grp, r_lo)
        v = spread_rows(grads, order.transpose(2, 0, 1, 3).reshape(-1), ids)
        v = lax.psum_scatter(v, ("grp", "fs"), scatter_dimension=0, tiled=True)
        v = lax.psum(v, "rep")
        v = lax.all_gather(v, "grp", axis=0, tiled=True)
        v = v.reshape(n_grp, per, r_lo, width).transpose(1, 0, 2, 3)
        return v.reshape(per, RANK, width).astype(F32)

    def body(
        prompt_input_rows,
        continuation_input,
        prompt_group_adapter,
        continuation_adapter,
        first_norm_scale,
        first_norm_bias,
        second_norm_scale,
        second_norm_bias,
        frozen_query_key_value,
        frozen_output_weight,
        frozen_up_weight,
        frozen_down_weight,
        adapter_attention_input,
        adapter_attention_output,
        adapter_up_input,
        adapter_up_output,
        adapter_down_input,
        adapter_down_output,
        prompt_cotangent,
        continuation_cotangent,
    ):
        prompt_len, width = prompt_input_rows.shape[2:]
        cont_len = continuation_input.shape[3]
        rows = prompt_len + cont_len
        count = adapter_up_input.shape[0]
        hidden = frozen_up_weight.shape[1]

        inputs = jnp.concatenate(
            [
                prompt_input_rows.reshape(prompt_len, width),
                continuation_input.reshape(cont_len, width),
            ],
            0,
        ).astype(F32)
        cot_low = jnp.concatenate(
            [
                prompt_cotangent.reshape(prompt_len, width),
                continuation_cotangent.reshape(cont_len, width),
            ],
            0,
        )
        ids = [prompt_group_adapter.reshape(()), continuation_adapter.reshape(())]
        a_attn = adapter_attention_input.swapaxes(2, 3)
        b_attn = adapter_attention_output
        a_up, b_up = adapter_up_input.swapaxes(1, 2), adapter_up_output
        a_dn, b_dn = adapter_down_input.swapaxes(1, 2), adapter_down_output

        mask2 = (jnp.arange(rows) >= prompt_len)[:, None] == (jnp.arange(2 * RANK) >= RANK)[None, :]

        def low_of(product):
            return jnp.where(mask2, product, 0.0).astype(BF)

        shard_rows = frozen_query_key_value.shape[0]
        parts = hidden // n_shard // shard_rows
        wide = shard_rows * (BLOCK // shard_rows)

        def columns(w):
            return w.reshape(shard_rows, -1, BLOCK).swapaxes(0, 1)

        up_blocks = frozen_up_weight.reshape(
            shard_rows, n_shard * shard_rows // BLOCK, BLOCK // shard_rows, parts, shard_rows
        )
        up_blocks = up_blocks.transpose(3, 1, 0, 2, 4).reshape(-1, shard_rows, BLOCK)
        dn_blocks = frozen_down_weight.reshape(parts, shard_rows, -1, BLOCK).swapaxes(1, 2)
        dn_blocks = dn_blocks.reshape(-1, shard_rows, BLOCK)
        all_blocks = jnp.concatenate(
            [columns(frozen_query_key_value), columns(frozen_output_weight), dn_blocks, up_blocks], 0
        )
        got = gather_blocks(all_blocks, n_fs, n_shard, "gather_all")
        got = got.reshape(-1, n_shard * shard_rows, BLOCK)
        n_qkv, n_out = 3 * width // BLOCK, width // BLOCK
        w_qkv, w_out = got[:n_qkv], got[n_qkv : n_qkv + n_out]
        n_dn = dn_blocks.shape[0]
        w_dn = got[n_qkv + n_out : n_qkv + n_out + n_dn]
        w_up = got[n_qkv + n_out + n_dn :]

        def times(u, w):
            return jnp.einsum("rk,bkc->rbc", u, w, preferred_element_type=F32).reshape(u.shape[0], -1)

        def times_t(g, w):
            g = g.reshape(g.shape[0], w.shape[0], BLOCK)
            return jnp.einsum("rbc,bkc->rk", g, w, preferred_element_type=F32)

        def hidden_order(v):
            v = v.reshape(-1, n_shard, parts, shard_rows)
            return v.transpose(0, 2, 1, 3).reshape(-1, hidden)

        def hidden_back(v):
            v = v.reshape(-1, parts, n_shard, shard_rows)
            return v.transpose(0, 2, 1, 3).reshape(-1, hidden)

        hat_one, rstd_one = norm_stats(inputs)
        normed_one = (hat_one * first_norm_scale + first_norm_bias).astype(BF)
        a_sel = [pick_rows(a_attn[:, n], ids) for n in range(4)]
        b_sel = [pick_rows(b_attn[:, n], ids) for n in range(4)]
        lows = [low_of(mm_nt(normed_one, a_sel[n])) for n in range(3)]
        merged = times(normed_one, w_qkv)
        queries, keys_local, values_local = [
            (merged[:, n * width : (n + 1) * width] + mm(lows[n], b_sel[n])).astype(BF)
            for n in range(3)
        ]
        prompt_keys = lax.all_gather(keys_local[:prompt_len], "grp", axis=0, tiled=True)
        prompt_values = lax.all_gather(values_local[:prompt_len], "grp", axis=0, tiled=True)
        prompt_total = prompt_keys.shape[0]
        all_keys = jnp.concatenate([prompt_keys, keys_local[prompt_len:]], 0)
        all_values = jnp.concatenate([prompt_values, values_local[prompt_len:]], 0)
        query_row = jnp.arange(rows)[:, None]
        key_col = jnp.arange(all_keys.shape[0])[None, :]
        prompt_sees = key_col <= lax.axis_index("grp") * prompt_len + query_row
        cont_sees = key_col - prompt_total <= query_row - prompt_len
        allowed = jnp.where(
            query_row < prompt_len, prompt_sees & (key_col < prompt_total), cont_sees
        )
        block_width = 512
        mixtures, logsums = [], []
        for first in range(0, width, block_width):
            cut = slice(first, first + block_width)
            mixture, logsum = attend_forward(
                queries[:, cut], all_keys[:, cut], all_values[:, cut], allowed
            )
            mixtures.append(mixture)
            logsums.append(logsum)
        mixed = jnp.concatenate(mixtures, 1).astype(BF)

        lows.append(low_of(mm_nt(mixed, a_sel[3])))
        resid = inputs + (times(mixed, w_out) + mm(lows[3], b_sel[3]))
        hat_two, rstd_two = norm_stats(resid)
        normed_two = (hat_two * second_norm_scale + second_norm_bias).astype(BF)

        a_up2, b_up2 = pick_rows(a_up, ids), hidden_order(pick_rows(b_up, ids))
        a_dn2, b_dn2 = hidden_order(pick_rows(a_dn, ids)), pick_rows(b_dn, ids)
        low_up = low_of(mm_nt(normed_two, a_up2))
        dlow_dn = low_of(mm_nt(cot_low, b_dn2))
        size = n_shard * shard_rows
        out_part = back_part = low_dn = dlow_up = 0.0
        g_b_up, g_a_dn = [], []
        for n in range(parts):
            cut = slice(n * size, (n + 1) * size)
            per = width // BLOCK
            w_up_n, w_dn_n = w_up[n * size // BLOCK : (n + 1) * size // BLOCK], w_dn[n * per : (n + 1) * per]
            pre = times(normed_two, w_up_n) + mm(low_up, b_up2[:, cut])
            cdf = 0.5 * (1.0 + lax.erf(pre * math.sqrt(0.5)))
            act = (pre * cdf).astype(BF)
            slope = cdf + pre * jnp.exp(-0.5 * pre * pre) * (1.0 / math.sqrt(2.0 * math.pi))
            grad_act = times_t(cot_low, w_dn_n) + mm(dlow_dn, a_dn2[:, cut])
            grad_pre = (grad_act * slope).astype(BF)
            out_part = out_part + times(act, w_dn_n)
            back_part = back_part + times_t(grad_pre, w_up_n)
            low_dn = low_dn + mm_nt(act, a_dn2[:, cut])
            dlow_up = dlow_up + mm_nt(grad_pre, b_up2[:, cut])
            g_b_up.append(mm_tn(low_up, grad_pre))
            g_a_dn.append(mm_tn(dlow_dn, act))
        g_b_up = hidden_back(jnp.concatenate(g_b_up, 1))
        g_a_dn = hidden_back(jnp.concatenate(g_a_dn, 1))
        low_dn, dlow_up = low_of(low_dn), low_of(dlow_up)
        result = resid + (out_part + mm(low_dn, b_dn2))
        grad_two = back_part + mm(dlow_up, a_up2)
        g_a_up = mm_tn(dlow_up, normed_two)
        g_b_dn = mm_tn(low_dn, cot_low)

        cot = cot_low.astype(F32)
        grad_resid = cot + norm_back(hat_two, rstd_two, second_norm_scale, grad_two)
        grad_attn = grad_resid.astype(BF)
        dlows = [None] * 4
        dlows[3] = low_of(mm_nt(grad_attn, b_sel[3]))
        grad_mixed = (times_t(grad_attn, w_out) + mm(dlows[3], a_sel[3])).astype(BF)

        g_q, g_k, g_v = [], [], []
        for n, first in enumerate(range(0, width, block_width)):
            cut = slice(first, first + block_width)
            a, b, c = attend_backward(
                queries[:, cut],
                all_keys[:, cut],
                all_values[:, cut],
                grad_mixed[:, cut],
                logsums[n],
                allowed,
            )
            g_q.append(a)
            g_k.append(b)
            g_v.append(c)
        grad_all_keys = jnp.concatenate(g_k, 1)
        grad_all_values = jnp.concatenate(g_v, 1)

        def share(v):
            mine = lax.psum_scatter(
                v[:prompt_total].astype(BF), "grp", scatter_dimension=0, tiled=True
            )
            return jnp.concatenate([mine, v[prompt_total:].astype(BF)], 0)

        grads = [
            jnp.concatenate(g_q, 1).astype(BF),
            share(grad_all_keys),
            share(grad_all_values),
        ]
        grad_one = times_t(jnp.concatenate(grads, 1), w_qkv)
        for n in range(3):
            dlows[n] = low_of(mm_nt(grads[n], b_sel[n]))
            grad_one = grad_one + mm(dlows[n], a_sel[n])
        grad_inputs = grad_resid + norm_back(hat_one, rstd_one, first_norm_scale, grad_one)

        g_a = [mm_tn(dlows[n], normed_one) for n in range(3)] + [mm_tn(dlows[3], mixed)]
        g_b = [mm_tn(lows[n], grads[n]) for n in range(3)] + [mm_tn(lows[3], grad_attn)]

        slim = reduce_tables(jnp.concatenate([g_b_up, g_a_dn] + g_a + g_b + [g_a_up, g_b_dn], 1), ids, count)
        both = [slim[:, :, :hidden], slim[:, :, hidden : 2 * hidden]]
        slim = slim[:, :, 2 * hidden :].reshape(slim.shape[0], RANK, 10, width).transpose(0, 2, 1, 3)

        return (
            result[:prompt_len].reshape(prompt_input_rows.shape).astype(BF),
            result[prompt_len:].reshape(continuation_input.shape).astype(BF),
            grad_inputs[:prompt_len].reshape(prompt_input_rows.shape).astype(BF),
            grad_inputs[prompt_len:].reshape(continuation_input.shape).astype(BF),
            slim[:, :4].swapaxes(2, 3),
            slim[:, 4:8],
            slim[:, 8].swapaxes(1, 2),
            both[0],
            both[1].swapaxes(1, 2),
            slim[:, 9],
        )

    return body


def solution(mesh):
    sizes = (mesh.shape["rep"], mesh.shape["grp"], mesh.shape["fs"])
    rows_in = P("rep", "fs", "grp", None)
    conts_in = P("rep", "fs", "grp", None, None)
    weight = P(("grp", "fs"), None)
    return jax.shard_map(
        make_body(sizes),
        mesh=mesh,
        in_specs=(
            rows_in,
            conts_in,
            P("rep", "fs"),
            P("rep", "fs", "grp"),
            P(),
            P(),
            P(),
            P(),
            weight,
            weight,
            weight,
            weight,
            P(),
            P(),
            P(),
            P(),
            P(),
            P(),
            rows_in,
            conts_in,
        ),
        out_specs=(
            rows_in,
            conts_in,
            rows_in,
            conts_in,
            P("fs", None, None, None),
            P("fs", None, None, None),
            P("fs", None, None),
            P("fs", None, None),
            P("fs", None, None),
            P("fs", None, None),
        ),
        check_vma=False,
    )
```

```python
import functools
import math

import jax
import jax.numpy as jnp
from jax import lax
from jax.experimental import pallas as pl
from jax.experimental.pallas import tpu as pltpu
from jax.sharding import PartitionSpec as P

HDIM = 128
RANK = 16
BLOCK = 512
SCALE = HDIM ** (-0.5)
NEG_FILL = -1e30
BF = jnp.bfloat16
F32 = jnp.float32
MESH = pl.DeviceIdType.MESH
ANY = pl.BlockSpec(memory_space=pl.ANY)
WHOLE = pl.BlockSpec(memory_space=pltpu.VMEM)
SCALARS = pl.BlockSpec(memory_space=pltpu.SMEM)
ROOM = 62 * 2**20


def mm(a, b):
    return jnp.dot(a, b, preferred_element_type=F32)


def mm_nt(a, b):
    return lax.dot_general(a, b, (((1,), (1,)), ((), ())), preferred_element_type=F32)


def mm_tn(a, b):
    return lax.dot_general(a, b, (((0,), (0,)), ((), ())), preferred_element_type=F32)


def norm_stats(values):
    center = values - jnp.mean(values, axis=-1, keepdims=True)
    spread = jnp.mean(center * center, axis=-1, keepdims=True)
    rstd = lax.rsqrt(spread + 1e-05)
    return center * rstd, rstd


def norm_back(values, gain, grad):
    hat, rstd = norm_stats(values)
    e = grad * gain
    return (
        e - jnp.mean(e, axis=-1, keepdims=True) - hat * jnp.mean(e * hat, axis=-1, keepdims=True)
    ) * rstd


def low_of(product, prompt_len):
    row = lax.broadcasted_iota(jnp.int32, product.shape, 0)
    col = lax.broadcasted_iota(jnp.int32, product.shape, 1)
    return jnp.where((row < prompt_len) == (col < RANK), product, 0.0).astype(BF)


def spread_rows(grads, order, ids):
    owner = jnp.repeat(jnp.stack(ids), RANK)
    rank = jnp.arange(RANK * len(ids)) % RANK
    hot = (order[:, None] == (owner * RANK + rank)[None, :]).astype(BF)
    return mm(hot, grads.astype(BF)).astype(BF)


class Gather:
    def __init__(self, n_fs, count, src, dst, sems, lag=2, away=48):
        (self.zs, self.zr, self.ys, self.yr, self.xs, self.xr) = sems[:6]
        (self.cs, self.cr, self.ds, self.dr, self.loc) = sems[6:]
        self.nz, self.count, self.src, self.dst = n_fs, count, src, dst
        self.lag, self.slots, self.last = lag, 2 * lag, n_fs + 2
        self.rows = src.shape[1]
        rep, grp = lax.axis_index("rep"), lax.axis_index("grp")
        self.z = lax.axis_index("fs")
        self.y, self.c, plane = grp // 2, grp % 2, rep % 2
        self.far_rep = rep + 1 - 2 * plane
        self.far_core = self.y * 2 + 1 - self.c
        self.far_row = (1 - self.y) * 2 + self.c
        self.own = grp * n_fs + self.z
        self.away, self.stay = away, self.rows - away
        self.in_first = pl.multiple_of(away * plane, 8)
        self.out_first = pl.multiple_of(self.stay * plane, 8)
        self.far_first = pl.multiple_of(self.stay * (1 - plane), 8)

    @staticmethod
    def semaphores(n_fs, lag=2):
        slots, dma = 2 * lag, pltpu.SemaphoreType.DMA
        return (
            [dma((2 * slots, 2, n_fs)), dma((2 * slots, n_fs))]
            + [dma((slots, n_fs))] * 2
            + [dma((slots, 2 * n_fs))] * 6
            + [dma((slots,))]
        )

    def barrier(self):
        sem = pltpu.get_barrier_semaphore()

        def greet(**where):
            pl.semaphore_signal(sem, 1, device_id=where, device_id_type=MESH)

        greet(rep=self.far_rep)
        greet(grp=self.far_core)
        greet(grp=self.far_row)
        below, above = self.z > 0, self.z < self.nz - 1
        pl.when(below)(lambda: greet(fs=self.z - 1))
        pl.when(above)(lambda: greet(fs=self.z + 1))
        pl.semaphore_wait(sem, 3 + below.astype(jnp.int32) + above.astype(jnp.int32))

    def at_distance(self, d):
        if d < 0 or d >= self.nz:
            return []
        if d == 0:
            return [(None, self.z, 0)]
        return [(self.z >= d, self.z - d, 1), (self.z < self.nz - d, self.z + d, -1)]

    def shard(self, other, fs, core):
        row = 1 - self.y if other else self.y
        return (row * 2 + core) * self.nz + fs

    def send(self, j, shard, first, size, sems, own=False, **where):
        rows = pl.ds(first, size)
        return pltpu.make_async_remote_copy(
            self.src.at[j, rows] if own else self.dst.at[j, shard, rows],
            self.dst.at[j, shard, rows],
            *sems,
            device_id=where,
            device_id_type=MESH,
        )

    def keep(self, j, t):
        sem = self.loc.at[lax.rem(t, self.slots)]
        return pltpu.make_async_copy(self.src.at[j], self.dst.at[j, self.own], sem)

    def sends(self, a, j, t):
        todo, nz, k, kz = [], self.nz, lax.rem(t, self.slots), lax.rem(t, 2 * self.slots)
        inner, outer, far = (self.in_first, self.stay), (self.out_first, self.away), self.far_first

        def both(left, right):
            return right if left is None else jnp.logical_and(left, right)

        for ok, fs, way in self.at_distance(a):
            shard, own = self.shard(0, fs, self.c), a == 0
            if way >= 0:
                sems = (self.zs.at[kz, 0, fs], self.zr.at[kz, fs])
                up = self.send(j, shard, *inner, sems, own, fs=self.z + 1)
                todo.append((both(ok, self.z < nz - 1), up))
            if way <= 0:
                sems = (self.zs.at[kz, 1, fs], self.zr.at[kz, fs])
                down = self.send(j, shard, *inner, sems, own, fs=self.z - 1)
                todo.append((both(ok, self.z > 0), down))
            sems = (self.ys.at[k, fs], self.yr.at[k, fs])
            todo.append((ok, self.send(j, shard, *inner, sems, own, grp=self.far_row)))
            if not own:
                sems = (self.xs.at[k, fs], self.xr.at[k, fs])
                todo.append((ok, self.send(j, shard, *outer, sems, rep=self.far_rep)))
            sems = (self.cs.at[k, fs], self.cr.at[k, fs])
            size = (0, self.rows) if own else inner
            todo.append((ok, self.send(j, shard, *size, sems, own, grp=self.far_core)))
        for ok, fs, _ in self.at_distance(a - 1):
            shard = self.shard(1, fs, self.c)
            sems = (self.xs.at[k, nz + fs], self.xr.at[k, nz + fs])
            todo.append((ok, self.send(j, shard, *outer, sems, rep=self.far_rep)))
            sems = (self.cs.at[k, nz + fs], self.cr.at[k, nz + fs])
            todo.append((ok, self.send(j, shard, *inner, sems, grp=self.far_core)))
        for other in (0, 1):
            for ok, fs, way in self.at_distance(a - 1 - other):
                if way or other:
                    i = other * nz + fs
                    sems = (self.ds.at[k, i], self.dr.at[k, i])
                    shard = self.shard(other, fs, self.c)
                    core = self.send(j, shard, far, self.away, sems, grp=self.far_core)
                    todo.append((ok, core))
        return todo

    def arrivals(self, a, j, t):
        todo, nz, k, kz = [], self.nz, lax.rem(t, self.slots), lax.rem(t, 2 * self.slots)
        inner, far = (self.in_first, self.stay), (self.far_first, self.away)

        def expect(ok, shard, first, size, sem):
            ref = self.dst.at[j, shard, pl.ds(first, size)]
            todo.append((ok, pltpu.make_async_copy(ref, ref, sem)))

        for ok, fs, way in self.at_distance(a):
            if way:
                expect(ok, self.shard(0, fs, self.c), *inner, self.zr.at[kz, fs])
        for ok, fs, _ in self.at_distance(a - 1):
            expect(ok, self.shard(1, fs, self.c), *inner, self.yr.at[k, fs])
        for other in (0, 1):
            for ok, fs, way in self.at_distance(a - 1 - other):
                i = other * nz + fs
                if way or other:
                    expect(ok, self.shard(other, fs, self.c), *far, self.xr.at[k, i])
                size = inner if way or other else (0, self.rows)
                expect(ok, self.shard(other, fs, 1 - self.c), *size, self.cr.at[k, i])
            for ok, fs, way in self.at_distance(a - 2 - other):
                if way or other:
                    i = other * nz + fs
                    expect(ok, self.shard(other, fs, 1 - self.c), *far, self.dr.at[k, i])
        return todo

    def run(self, early=None, compute=None):
        lag = self.lag

        def act(ok, fn):
            if ok is None:
                fn()
            else:
                pl.when(ok)(fn)

        def finish(a, j, t):
            for ok, copy in self.sends(a - 1, j, t):
                act(ok, copy.wait_send)
            for ok, copy in self.arrivals(a, j, t):
                act(ok, copy.wait)
            if a == 1:
                self.keep(j, t).wait()

        def begin(a, j, t):
            for ok, copy in self.sends(a, j, t):
                act(ok, copy.start)
            if a == 0:
                self.keep(j, t).start()

        def tick(t, carry):
            for a in range(self.last, 0, -1):
                j = t - lag * a
                pl.when((j >= 0) & (j < self.count))(functools.partial(finish, a, j, t - lag))
            for a in range(self.last - 1, -1, -1):
                j = t - lag * a
                pl.when((j >= 0) & (j < self.count))(functools.partial(begin, a, j, t))
            if early is not None:
                early(t)
            if compute is not None:
                j = t - lag * self.last
                pl.when(j >= 0)(functools.partial(compute, j))
            return carry

        lax.fori_loop(0, self.count + lag * self.last + (compute is not None), tick, 0)


def head_columns(ref, rows, part, h, width):
    first = pl.multiple_of(part * width + h * HDIM, HDIM)
    return ref[rows, pl.ds(first, HDIM)]


def seen(shape, first):
    row = lax.broadcasted_iota(jnp.int32, shape, 0)
    return lax.broadcasted_iota(jnp.int32, shape, 1) <= first + row


def head_chances(qkv, kp, h, prompt_len, width, first):
    own, cont = slice(0, prompt_len), slice(prompt_len, None)
    q_p = head_columns(qkv, own, 0, h, width)
    q_c = head_columns(qkv, cont, 0, h, width)
    k_c = head_columns(qkv, cont, 1, h, width)
    v_c = head_columns(qkv, cont, 2, h, width)
    lanes = pl.ds(pl.multiple_of(h * HDIM, HDIM), HDIM)
    k_p = kp[:, :, lanes].reshape(-1, HDIM)
    lanes = pl.ds(pl.multiple_of(width + h * HDIM, HDIM), HDIM)
    v_p = kp[:, :, lanes].reshape(-1, HDIM)
    s_p = mm_nt(q_p, k_p) * SCALE
    s_p = jnp.where(seen(s_p.shape, first), s_p, NEG_FILL)
    e_p = jnp.exp(s_p - jnp.max(s_p, axis=-1, keepdims=True))
    c_p = e_p * (1.0 / jnp.sum(e_p, axis=-1, keepdims=True))
    s_1 = mm_nt(q_c, k_p) * SCALE
    s_2 = mm_nt(q_c, k_c) * SCALE
    s_2 = jnp.where(seen(s_2.shape, 0), s_2, NEG_FILL)
    peak = jnp.maximum(
        jnp.max(s_1, axis=-1, keepdims=True), jnp.max(s_2, axis=-1, keepdims=True)
    )
    e_1, e_2 = jnp.exp(s_1 - peak), jnp.exp(s_2 - peak)
    mass = jnp.sum(e_1, axis=-1, keepdims=True) + jnp.sum(e_2, axis=-1, keepdims=True)
    inv = 1.0 / mass
    return (q_p, q_c, k_p, k_c, v_p, v_c), (c_p, e_1 * inv, e_2 * inv)


def project_call(x, gain, bias, ids, a_tab, b_tab, blocks, n_fs, n_shard, prompt_len):
    count, shard_rows, _ = blocks.shape
    rows, width = x.shape
    per = width // BLOCK

    def kernel(
        x, gain, bias, ids, a_tab, b_tab, src, dst, qkv, normed, lows, a_ext, b_ext, wbuf, wsem, *sems
    ):
        engine = Gather(n_fs, count, src, dst, sems)
        engine.barrier()

        def load(j):
            return pltpu.make_async_copy(dst.at[j], wbuf.at[lax.rem(j, 2)], wsem.at[lax.rem(j, 2)])

        def early(t):
            @pl.when(t == 0)
            def _():
                for i in range(2):
                    part = slice(i * RANK, (i + 1) * RANK)
                    for n in range(3):
                        a_ext[n, part] = a_tab[ids[i], n]
                        b_ext[n, part] = b_tab[ids[i], n]
                hat, _ = norm_stats(x[...].astype(F32))
                normed[...] = (hat * gain[...] + bias[...]).astype(BF)
                for n in range(3):
                    lows[n] = low_of(mm_nt(normed[...], a_ext[n]), prompt_len)

        def compute(j):
            @pl.when(j < count)
            def _():
                load(j).start()

            @pl.when(j > 0)
            def _():
                i = j - 1
                load(i).wait()
                n = i // per
                w = wbuf[lax.rem(i, 2)].reshape(-1, BLOCK)
                inside = pl.ds(pl.multiple_of(lax.rem(i, per) * BLOCK, BLOCK), BLOCK)
                extra = mm(lows[n], b_ext[n, :, inside])
                cols = pl.ds(pl.multiple_of(i * BLOCK, BLOCK), BLOCK)
                qkv[:, cols] = (mm(normed[...], w) + extra).astype(BF)

        engine.run(early, compute)

    return pl.pallas_call(
        kernel,
        out_shape=[
            jax.ShapeDtypeStruct((count, n_shard, shard_rows, BLOCK), BF),
            jax.ShapeDtypeStruct((rows, 3 * width), BF),
            jax.ShapeDtypeStruct((rows, width), BF),
            jax.ShapeDtypeStruct((3, rows, 2 * RANK), BF),
        ],
        in_specs=[WHOLE, WHOLE, WHOLE, SCALARS, WHOLE, WHOLE, ANY],
        out_specs=[ANY, WHOLE, WHOLE, WHOLE],
        scratch_shapes=[
            pltpu.VMEM((3, 2 * RANK, width), BF),
            pltpu.VMEM((3, 2 * RANK, width), BF),
            pltpu.VMEM((2, n_shard, shard_rows, BLOCK), BF),
            pltpu.SemaphoreType.DMA((2,)),
        ]
        + Gather.semaphores(n_fs),
        compiler_params=pltpu.CompilerParams(
            collective_id=0, has_side_effects=True, vmem_limit_bytes=ROOM
        ),
        name="project",
    )(x, gain, bias, ids, a_tab, b_tab, blocks)


def middle_call(x, cot, qkv, gain, bias, ids, tables, blocks, counts, n_fs, n_shard, prompt_len):
    rows, width = x.shape
    shard_rows = blocks.shape[1]
    n_out, n_dn, n_up = counts
    count = n_out + n_dn + n_up
    hidden = n_up * BLOCK
    n_grp = n_shard // n_fs
    parts = n_dn // n_out
    heads = width // HDIM
    go, first_head = 4, 5
    first_out = first_head + heads
    a_o, b_o, a_u, b_u, a_d, b_d = range(6)

    def kernel(
        x,
        cot,
        qkv,
        gain,
        bias,
        ids,
        *refs,
    ):
        tabs, refs = refs[:6], refs[6:]
        src, refs = refs[0], refs[1:]
        (dst, kp, mixed, normed, result, resid_back, grad_attn), refs = refs[:7], refs[7:]
        (low_o, g_a_up, g_b_up, g_a_dn, g_b_dn), refs = refs[:5], refs[5:]
        ext, refs = refs[:6], refs[6:]
        (resid, out_acc, low_up, dlow_dn, low_dn, dlow_up), refs = refs[:6], refs[6:]
        (wbuf, dbuf, wsem, dsem, ksend, krecv, kloc), sems = refs[:7], refs[7:]
        engine = Gather(n_fs, count, src, dst, sems)
        engine.barrier()
        grp = lax.axis_index("grp")

        def pass_on(n, whose, to):
            return pltpu.make_async_remote_copy(
                kp.at[whose],
                kp.at[whose],
                ksend.at[n],
                krecv.at[n],
                device_id={"grp": to},
                device_id_type=MESH,
            )

        def landed(n, whose):
            return pltpu.make_async_copy(kp.at[whose], kp.at[whose], krecv.at[n])

        to_row = pass_on(0, grp, engine.far_row)
        to_core = pass_on(1, grp, engine.far_core)
        onward = pass_on(2, engine.far_row, engine.far_core)
        diagonal = (1 - engine.y) * 2 + 1 - engine.c

        def load_out(b):
            return pltpu.make_async_copy(dst.at[b], wbuf.at[lax.rem(b, 2)], wsem.at[lax.rem(b, 2)])

        def early(t):
            @pl.when(t == 0)
            def _():
                kp[grp] = qkv[:prompt_len, width:]
                to_row.start()
                to_core.start()
                for n, tab in enumerate(tabs):
                    for i in range(2):
                        ext[n][i * RANK : (i + 1) * RANK] = tab[ids[i]]
                dlow_dn[...] = low_of(mm_nt(cot[...], ext[b_d][...]), prompt_len)

            @pl.when(t == go)
            def _():
                landed(0, engine.far_row).wait()
                onward.start()

            @pl.when(t == first_head)
            def _():
                landed(1, engine.far_core).wait()
                landed(2, diagonal).wait()
                to_row.wait_send()
                to_core.wait_send()
                onward.wait_send()

            @pl.when((t >= first_head) & (t < first_out))
            def _():
                h = t - first_head
                (_, _, _, _, v_p, v_c), (c_p, c_1, c_2) = head_chances(
                    qkv, kp, h, prompt_len, width, grp * prompt_len
                )
                lanes = pl.ds(pl.multiple_of(h * HDIM, HDIM), HDIM)
                mixed[:prompt_len, lanes] = mm(c_p.astype(BF), v_p).astype(BF)
                mixed[prompt_len:, lanes] = (
                    mm(c_1.astype(BF), v_p) + mm(c_2.astype(BF), v_c)
                ).astype(BF)

            @pl.when(t == first_out - 1)
            def _():
                load_out(0).start()

            @pl.when((t >= first_out) & (t < first_out + n_out))
            def _():
                b = t - first_out

                @pl.when(b == 0)
                def _():
                    low_o[...] = low_of(mm_nt(mixed[...], ext[a_o][...]), prompt_len)

                load_out(b).wait()

                @pl.when(b + 1 < n_out)
                def _():
                    load_out(b + 1).start()

                cols = pl.ds(pl.multiple_of(b * BLOCK, BLOCK), BLOCK)
                w = wbuf[lax.rem(b, 2)].reshape(-1, BLOCK)
                branch = mm(mixed[...], w) + mm(low_o[...], ext[b_o][:, cols])
                resid[:, cols] = x[:, cols].astype(F32) + branch

            @pl.when(t == first_out + n_out)
            def _():
                hat, _ = norm_stats(resid[...])
                normed[...] = (hat * gain[...] + bias[...]).astype(BF)
                low_up[...] = low_of(mm_nt(normed[...], ext[a_u][...]), prompt_len)
                out_acc[...] = resid[...]
                resid_back[...] = jnp.zeros_like(resid_back)
                low_dn[...] = jnp.zeros_like(low_dn)
                dlow_up[...] = jnp.zeros_like(dlow_up)

        def load_up(n):
            k = lax.rem(n, 2)
            up = pltpu.make_async_copy(dst.at[n_out + n_dn + n], wbuf.at[k], wsem.at[k])
            down = pltpu.make_async_copy(dst.at[pl.ds(n_out, n_dn), n], dbuf.at[k], dsem.at[k])
            return up, down

        def compute(j):
            n = j - (n_out + n_dn)

            @pl.when((n >= 0) & (n < n_up))
            def _():
                for copy in load_up(n):
                    copy.start()

            @pl.when(n > 0)
            def _():
                i = n - 1
                for copy in load_up(i):
                    copy.wait()
                k = lax.rem(i, 2)
                cols = pl.ds(pl.multiple_of(i * BLOCK, BLOCK), BLOCK)
                w_up = wbuf[k].reshape(-1, BLOCK)
                a_dn, b_up = ext[a_d][:, cols], ext[b_u][:, cols]
                pre = mm(normed[...], w_up) + mm(low_up[...], b_up)
                cdf = 0.5 * (1.0 + lax.erf(pre * math.sqrt(0.5)))
                act = (pre * cdf).astype(BF)
                slope = cdf + pre * jnp.exp(-0.5 * pre * pre) * (1.0 / math.sqrt(2.0 * math.pi))
                grad_act = mm(dlow_dn[...], a_dn)
                for b in range(n_out):
                    w_dn = dbuf[k, b * parts : (b + 1) * parts].reshape(BLOCK, BLOCK)
                    span = slice(b * BLOCK, (b + 1) * BLOCK)
                    grad_act = grad_act + mm_nt(cot[:, span], w_dn)
                    out_acc[:, span] += mm(act, w_dn)
                grad_pre = (grad_act * slope).astype(BF)
                resid_back[...] += mm_nt(grad_pre, w_up)
                low_dn[...] += mm_nt(act, a_dn)
                dlow_up[...] += mm_nt(grad_pre, b_up)
                g_b_up[:, cols] = mm_tn(low_up[...], grad_pre).astype(BF)
                g_a_dn[:, cols] = mm_tn(dlow_dn[...], act).astype(BF)

        engine.run(early, compute)
        low = low_of(low_dn[...], prompt_len)
        result[...] = (out_acc[...] + mm(low, ext[b_d][...])).astype(BF)
        g_b_dn[...] = mm_tn(low, cot[...]).astype(BF)
        dlow = low_of(dlow_up[...], prompt_len)
        g_a_up[...] = mm_tn(dlow, normed[...]).astype(BF)
        grad = resid_back[...] + mm(dlow, ext[a_u][...])
        grad = cot[...].astype(F32) + norm_back(resid[...], gain[...], grad)
        resid_back[...] = grad
        grad_attn[...] = grad.astype(BF)

    like = jax.ShapeDtypeStruct
    two = 2 * RANK
    return pl.pallas_call(
        kernel,
        out_shape=[
            like((count, n_shard, shard_rows, BLOCK), BF),
            like((n_grp, prompt_len, 2 * width), BF),
            like((rows, width), BF),
            like((rows, width), BF),
            like((rows, width), BF),
            like((rows, width), F32),
            like((rows, width), BF),
            like((rows, two), BF),
            like((two, width), BF),
            like((two, hidden), BF),
            like((two, hidden), BF),
            like((two, width), BF),
        ],
        in_specs=[WHOLE] * 5 + [SCALARS] + [WHOLE] * 6 + [ANY],
        out_specs=[ANY] + [WHOLE] * 11,
        scratch_shapes=[
            pltpu.VMEM((two, w), BF) for w in (width, width, width, hidden, hidden, width)
        ]
        + [
            pltpu.VMEM((rows, width), F32),
            pltpu.VMEM((rows, width), F32),
            pltpu.VMEM((rows, two), BF),
            pltpu.VMEM((rows, two), BF),
            pltpu.VMEM((rows, two), F32),
            pltpu.VMEM((rows, two), F32),
            pltpu.VMEM((2, n_shard, shard_rows, BLOCK), BF),
            pltpu.VMEM((2, n_dn, shard_rows, BLOCK), BF),
            pltpu.SemaphoreType.DMA((2,)),
            pltpu.SemaphoreType.DMA((2,)),
            pltpu.SemaphoreType.DMA((3,)),
            pltpu.SemaphoreType.DMA((3,)),
            pltpu.SemaphoreType.DMA((1,)),
        ]
        + Gather.semaphores(n_fs),
        compiler_params=pltpu.CompilerParams(
            collective_id=1, has_side_effects=True, vmem_limit_bytes=ROOM
        ),
        name="middle",
    )(x, cot, qkv, gain, bias, ids, *tables, blocks)


def attention_back_call(grad_attn, mixed, low_o, qkv, kp, ids, a_tab, b_tab, w_out, n_out, prompt_len):
    rows, width = grad_attn.shape
    heads = width // HDIM
    total = kp.shape[0] * prompt_len
    n_shard, shard_rows = w_out.shape[1:3]

    def kernel(
        grad_attn, mixed, low_o, qkv, kp, ids, a_tab, b_tab, w, g_q, g_own, g_far, g_a, g_b, a_ext, b_ext, dlow, acc, gm
    ):
        step = pl.program_id(0)

        @pl.when(step == 0)
        def _():
            for i in range(2):
                part = slice(i * RANK, (i + 1) * RANK)
                a_ext[part] = a_tab[ids[i]]
                b_ext[part] = b_tab[ids[i]]
            dlow[...] = low_of(mm_nt(grad_attn[...], b_ext[...]), prompt_len)
            acc[...] = mm(dlow[...], a_ext[...])
            g_a[...] = mm_tn(dlow[...], mixed[...]).astype(BF)
            g_b[...] = mm_tn(low_o[...], grad_attn[...]).astype(BF)

        @pl.when(step < n_out)
        def _():
            cols = pl.ds(pl.multiple_of(step * BLOCK, BLOCK), BLOCK)
            acc[...] += mm_nt(grad_attn[:, cols], w[0].reshape(-1, BLOCK))

        @pl.when(step == n_out - 1)
        def _():
            gm[...] = acc[...].astype(BF)

        @pl.when(step >= n_out)
        def _():
            h = step - n_out
            first = lax.axis_index("grp") * prompt_len
            (q_p, q_c, k_p, k_c, v_p, v_c), (c_p, c_1, c_2) = head_chances(
                qkv, kp, h, prompt_len, width, first
            )
            lanes = pl.ds(pl.multiple_of(h * HDIM, HDIM), HDIM)
            far = pl.ds(pl.multiple_of(width + h * HDIM, HDIM), HDIM)
            gm_p, gm_c = gm[:prompt_len, lanes], gm[prompt_len:, lanes]
            d_p = mm_nt(gm_p, v_p)
            d_1, d_2 = mm_nt(gm_c, v_p), mm_nt(gm_c, v_c)
            s_p = (c_p * (d_p - jnp.sum(c_p * d_p, axis=-1, keepdims=True))).astype(BF)
            inner = jnp.sum(c_1 * d_1, axis=-1, keepdims=True) + jnp.sum(
                c_2 * d_2, axis=-1, keepdims=True
            )
            s_1 = (c_1 * (d_1 - inner)).astype(BF)
            s_2 = (c_2 * (d_2 - inner)).astype(BF)
            g_q[:prompt_len, lanes] = (mm(s_p, k_p) * SCALE).astype(BF)
            g_q[prompt_len:, lanes] = ((mm(s_1, k_p) + mm(s_2, k_c)) * SCALE).astype(BF)
            g_own[:, lanes] = (mm_tn(s_2, q_c) * SCALE).astype(BF)
            g_own[:, far] = mm_tn(c_2.astype(BF), gm_c).astype(BF)
            g_far[:, lanes] = ((mm_tn(s_p, q_p) + mm_tn(s_1, q_c)) * SCALE).astype(BF)
            g_far[:, far] = (mm_tn(c_p.astype(BF), gm_p) + mm_tn(c_1.astype(BF), gm_c)).astype(BF)

    like = jax.ShapeDtypeStruct
    two = 2 * RANK
    return pl.pallas_call(
        kernel,
        grid=(n_out + heads,),
        out_shape=[
            like((rows, width), BF),
            like((rows - prompt_len, 2 * width), BF),
            like((total, 2 * width), BF),
            like((two, width), BF),
            like((two, width), BF),
        ],
        in_specs=[WHOLE] * 5
        + [SCALARS, WHOLE, WHOLE]
        + [
            pl.BlockSpec(
                (1, n_shard, shard_rows, BLOCK), lambda i: (jnp.minimum(i, n_out - 1), 0, 0, 0)
            )
        ],
        out_specs=[WHOLE] * 5,
        scratch_shapes=[
            pltpu.VMEM((two, width), BF),
            pltpu.VMEM((two, width), BF),
            pltpu.VMEM((rows, two), BF),
            pltpu.VMEM((rows, width), F32),
            pltpu.VMEM((rows, width), BF),
        ],
        compiler_params=pltpu.CompilerParams(vmem_limit_bytes=ROOM),
        name="attention_back",
    )(grad_attn, mixed, low_o, qkv, kp, ids, a_tab, b_tab, w_out)


def project_back_call(grads, x, normed, lows, grad_resid, gain, ids, a_tab, b_tab, w_qkv, prompt_len):
    rows, width = x.shape
    count, n_shard, shard_rows, _ = w_qkv.shape
    per = width // BLOCK

    def kernel(
        grads, x, normed, lows, grad_resid, gain, ids, a_tab, b_tab, w, out, g_a, g_b, a_ext, b_ext, dlow, acc
    ):
        j = pl.program_id(0)
        n = j // per

        @pl.when(j == 0)
        def _():
            for i in range(2):
                part = slice(i * RANK, (i + 1) * RANK)
                for m in range(3):
                    a_ext[m, part] = a_tab[ids[i], m]
                    b_ext[m, part] = b_tab[ids[i], m]
            acc[...] = jnp.zeros_like(acc)
            dlow[...] = jnp.zeros_like(dlow)

        inside = pl.ds(pl.multiple_of(lax.rem(j, per) * BLOCK, BLOCK), BLOCK)
        part = grads[...]
        acc[...] += mm_nt(part, w[0].reshape(-1, BLOCK))
        dlow[n] += mm_nt(part, b_ext[n, :, inside])
        g_b[...] = mm_tn(lows[n], part).astype(BF)

        @pl.when(j == count - 1)
        def _():
            for m in range(3):
                low = low_of(dlow[m], prompt_len)
                acc[...] += mm(low, a_ext[m])
                g_a[m] = mm_tn(low, normed[...]).astype(BF)
            back = norm_back(x[...].astype(F32), gain[...], acc[...])
            out[...] = (grad_resid[...] + back).astype(BF)

    like = jax.ShapeDtypeStruct
    two = 2 * RANK
    return pl.pallas_call(
        kernel,
        grid=(count,),
        out_shape=[like((rows, width), BF), like((3, two, width), BF), like((two, 3 * width), BF)],
        in_specs=[pl.BlockSpec((rows, BLOCK), lambda j: (0, j))]
        + [WHOLE] * 5
        + [SCALARS, WHOLE, WHOLE]
        + [pl.BlockSpec((1, n_shard, shard_rows, BLOCK), lambda j: (j, 0, 0, 0))],
        out_specs=[WHOLE, WHOLE, pl.BlockSpec((two, BLOCK), lambda j: (0, j))],
        scratch_shapes=[
            pltpu.VMEM((3, two, width), BF),
            pltpu.VMEM((3, two, width), BF),
            pltpu.VMEM((3, rows, two), F32),
            pltpu.VMEM((rows, width), F32),
        ],
        compiler_params=pltpu.CompilerParams(vmem_limit_bytes=ROOM),
        name="project_back",
    )(grads, x, normed, lows, grad_resid, gain, ids, a_tab, b_tab, w_qkv)


def make_body(sizes):
    n_rep, n_grp, n_fs = sizes
    n_shard = n_grp * n_fs

    def reduce_tables(grads, ids, count):
        per, r_lo, width = count // n_fs, RANK // n_grp, grads.shape[1]
        order = jnp.arange(count * RANK).reshape(n_fs, per, n_grp, r_lo)
        v = spread_rows(grads, order.transpose(2, 0, 1, 3).reshape(-1), ids)
        v = lax.psum_scatter(v, ("grp", "fs"), scatter_dimension=0, tiled=True)
        v = lax.psum(v, "rep")
        v = lax.all_gather(v, "grp", axis=0, tiled=True)
        v = v.reshape(n_grp, per, r_lo, width).transpose(1, 0, 2, 3)
        return v.reshape(per, RANK, width).astype(F32)

    def body(
        prompt_input_rows,
        continuation_input,
        prompt_group_adapter,
        continuation_adapter,
        first_norm_scale,
        first_norm_bias,
        second_norm_scale,
        second_norm_bias,
        frozen_query_key_value,
        frozen_output_weight,
        frozen_up_weight,
        frozen_down_weight,
        adapter_attention_input,
        adapter_attention_output,
        adapter_up_input,
        adapter_up_output,
        adapter_down_input,
        adapter_down_output,
        prompt_cotangent,
        continuation_cotangent,
    ):
        prompt_len, width = prompt_input_rows.shape[2:]
        cont_len = continuation_input.shape[3]
        count = adapter_up_input.shape[0]
        hidden = frozen_up_weight.shape[1]
        shard_rows = frozen_query_key_value.shape[0]
        parts = frozen_down_weight.shape[0] // shard_rows
        assert hidden == n_shard * BLOCK and parts * shard_rows == BLOCK

        def tokens(prompt, cont):
            return jnp.concatenate(
                [prompt.reshape(prompt_len, width), cont.reshape(cont_len, width)], 0
            )

        def columns(w):
            return w.reshape(shard_rows, -1, BLOCK).swapaxes(0, 1)

        x = tokens(prompt_input_rows, continuation_input)
        cot = tokens(prompt_cotangent, continuation_cotangent)
        ids = jnp.concatenate(
            [prompt_group_adapter.reshape(1), continuation_adapter.reshape(1)]
        )
        a_attn = adapter_attention_input.swapaxes(2, 3)
        b_attn = adapter_attention_output
        a_up, b_up = adapter_up_input.swapaxes(1, 2), adapter_up_output
        a_dn, b_dn = adapter_down_input.swapaxes(1, 2), adapter_down_output
        gain_one, bias_one, gain_two, bias_two = [
            v[None, :]
            for v in (first_norm_scale, first_norm_bias, second_norm_scale, second_norm_bias)
        ]
        w_qkv, qkv, normed_one, lows = project_call(
            x,
            gain_one,
            bias_one,
            ids,
            a_attn,
            b_attn,
            columns(frozen_query_key_value),
            n_fs,
            n_shard,
            prompt_len,
        )
        dn_blocks = frozen_down_weight.reshape(parts, shard_rows, -1, BLOCK).transpose(2, 0, 1, 3)
        blocks = [
            columns(frozen_output_weight),
            dn_blocks.reshape(-1, shard_rows, BLOCK),
            columns(frozen_up_weight),
        ]
        counts = [b.shape[0] for b in blocks]
        tables = (a_attn[:, 3], b_attn[:, 3], a_up, b_up, a_dn, b_dn)
        (
            w_rest,
            kp,
            mixed,
            normed_two,
            result,
            grad_resid,
            grad_attn,
            low_o,
            g_a_up,
            g_b_up,
            g_a_dn,
            g_b_dn,
        ) = middle_call(
            x,
            cot,
            qkv,
            gain_two,
            bias_two,
            ids,
            tables,
            jnp.concatenate(blocks, 0),
            counts,
            n_fs,
            n_shard,
            prompt_len,
        )
        g_q, g_own, g_far, g_a_o, g_b_o = attention_back_call(
            grad_attn,
            mixed,
            low_o,
            qkv,
            kp,
            ids,
            tables[0],
            tables[1],
            w_rest,
            counts[0],
            prompt_len,
        )
        g_mine = lax.psum_scatter(g_far, "grp", scatter_dimension=0, tiled=True)
        grads = jnp.concatenate([g_q, jnp.concatenate([g_mine, g_own], 0)], 1)
        grad_inputs, g_a, g_b = project_back_call(
            grads, x, normed_one, lows, grad_resid, gain_one, ids, a_attn, b_attn, w_qkv, prompt_len
        )
        flat = [g_b_up, g_a_dn, g_a[0], g_a[1], g_a[2], g_a_o, g_b, g_b_o, g_a_up, g_b_dn]
        slim = reduce_tables(jnp.concatenate(flat, 1), [ids[0], ids[1]], count)
        both = [slim[:, :, :hidden], slim[:, :, hidden : 2 * hidden]]
        slim = slim[:, :, 2 * hidden :].reshape(slim.shape[0], RANK, 10, width).transpose(0, 2, 1, 3)

        return (
            result[:prompt_len].reshape(prompt_input_rows.shape),
            result[prompt_len:].reshape(continuation_input.shape),
            grad_inputs[:prompt_len].reshape(prompt_input_rows.shape),
            grad_inputs[prompt_len:].reshape(continuation_input.shape),
            slim[:, :4].swapaxes(2, 3),
            slim[:, 4:8],
            slim[:, 8].swapaxes(1, 2),
            both[0],
            both[1].swapaxes(1, 2),
            slim[:, 9],
        )

    return body


def solution(mesh):
    sizes = (mesh.shape["rep"], mesh.shape["grp"], mesh.shape["fs"])
    rows_in = P("rep", "fs", "grp", None)
    conts_in = P("rep", "fs", "grp", None, None)
    weight = P(("grp", "fs"), None)
    return jax.shard_map(
        make_body(sizes),
        mesh=mesh,
        in_specs=(
            rows_in,
            conts_in,
            P("rep", "fs"),
            P("rep", "fs", "grp"),
            P(),
            P(),
            P(),
            P(),
            weight,
            weight,
            weight,
            weight,
            P(),
            P(),
            P(),
            P(),
            P(),
            P(),
            rows_in,
            conts_in,
        ),
        out_specs=(
            rows_in,
            conts_in,
            rows_in,
            conts_in,
            P("fs", None, None, None),
            P("fs", None, None, None),
            P("fs", None, None),
            P("fs", None, None),
            P("fs", None, None),
            P("fs", None, None),
        ),
        check_vma=False,
    )
```

```python
import functools
import math

import jax
import jax.numpy as jnp
from jax import lax
from jax.experimental import pallas as pl
from jax.experimental.pallas import tpu as pltpu
from jax.sharding import PartitionSpec as P

HDIM = 128
RANK = 16
BLOCK = 512
SCALE = HDIM ** (-0.5)
NEG_FILL = -1e30
BF = jnp.bfloat16
F32 = jnp.float32
MESH = pl.DeviceIdType.MESH
ANY = pl.BlockSpec(memory_space=pl.ANY)
WHOLE = pl.BlockSpec(memory_space=pltpu.VMEM)
SCALARS = pl.BlockSpec(memory_space=pltpu.SMEM)
ROOM = 62 * 2**20


def mm(a, b):
    return jnp.dot(a, b, preferred_element_type=F32)


def mm_nt(a, b):
    return lax.dot_general(a, b, (((1,), (1,)), ((), ())), preferred_element_type=F32)


def mm_tn(a, b):
    return lax.dot_general(a, b, (((0,), (0,)), ((), ())), preferred_element_type=F32)


def norm_stats(values):
    center = values - jnp.mean(values, axis=-1, keepdims=True)
    spread = jnp.mean(center * center, axis=-1, keepdims=True)
    rstd = lax.rsqrt(spread + 1e-05)
    return center * rstd, rstd


def norm_back(values, gain, grad):
    hat, rstd = norm_stats(values)
    e = grad * gain
    return (
        e - jnp.mean(e, axis=-1, keepdims=True) - hat * jnp.mean(e * hat, axis=-1, keepdims=True)
    ) * rstd


def low_of(product, prompt_len):
    row = lax.broadcasted_iota(jnp.int32, product.shape, 0)
    col = lax.broadcasted_iota(jnp.int32, product.shape, 1)
    return jnp.where((row < prompt_len) == (col < RANK), product, 0.0).astype(BF)


class Gather:
    def __init__(self, n_fs, sources, dst, sems, lag=2, away=48):
        (self.zs, self.zr, self.ys, self.yr, self.xs, self.xr) = sems[:6]
        (self.cs, self.cr, self.ds, self.dr, self.loc) = sems[6:]
        self.nz, self.sources, self.dst = n_fs, sources, dst
        self.count, self.rows = dst.shape[0], dst.shape[2]
        self.lag, self.slots, self.last = lag, 2 * lag, n_fs + 2
        rep, grp = lax.axis_index("rep"), lax.axis_index("grp")
        self.z = lax.axis_index("fs")
        self.y, self.c, plane = grp // 2, grp % 2, rep % 2
        self.far_rep = rep + 1 - 2 * plane
        self.far_core = self.y * 2 + 1 - self.c
        self.far_row = (1 - self.y) * 2 + self.c
        self.own = grp * n_fs + self.z
        self.away, self.stay = away, self.rows - away
        self.in_first = pl.multiple_of(away * plane, 8)
        self.out_first = pl.multiple_of(self.stay * plane, 8)
        self.far_first = pl.multiple_of(self.stay * (1 - plane), 8)

    @staticmethod
    def semaphores(n_fs, lag=2):
        slots, dma = 2 * lag, pltpu.SemaphoreType.DMA
        return (
            [dma((2 * slots, 2, n_fs)), dma((2 * slots, n_fs))]
            + [dma((slots, n_fs))] * 2
            + [dma((slots, 2 * n_fs))] * 6
            + [dma((slots,))]
        )

    def barrier(self):
        sem = pltpu.get_barrier_semaphore()

        def greet(**where):
            pl.semaphore_signal(sem, 1, device_id=where, device_id_type=MESH)

        greet(rep=self.far_rep)
        greet(grp=self.far_core)
        greet(grp=self.far_row)
        below, above = self.z > 0, self.z < self.nz - 1
        pl.when(below)(lambda: greet(fs=self.z - 1))
        pl.when(above)(lambda: greet(fs=self.z + 1))
        pl.semaphore_wait(sem, 3 + below.astype(jnp.int32) + above.astype(jnp.int32))

    def at_distance(self, d):
        if d < 0 or d >= self.nz:
            return []
        if d == 0:
            return [(None, self.z, 0)]
        return [(self.z >= d, self.z - d, 1), (self.z < self.nz - d, self.z + d, -1)]

    def shard(self, other, fs, core):
        row = 1 - self.y if other else self.y
        return (row * 2 + core) * self.nz + fs

    def send(self, j, shard, first, size, sems, src=None, **where):
        rows = pl.ds(first, size)
        return pltpu.make_async_remote_copy(
            self.dst.at[j, shard, rows] if src is None else src(first, size),
            self.dst.at[j, shard, rows],
            *sems,
            device_id=where,
            device_id_type=MESH,
        )

    def own_blocks(self, j):
        start = 0
        for count, ref in self.sources:
            ok = (j >= start) & (j < start + count) if len(self.sources) > 1 else None
            yield ok, functools.partial(ref, j - start)
            start += count

    def keeps(self, j, t):
        sem = self.loc.at[lax.rem(t, self.slots)]
        for ok, src in self.own_blocks(j):
            yield ok, pltpu.make_async_copy(src(0, self.rows), self.dst.at[j, self.own], sem)

    def sends(self, a, j, t):
        todo, nz, k, kz = [], self.nz, lax.rem(t, self.slots), lax.rem(t, 2 * self.slots)
        inner, outer, far = (self.in_first, self.stay), (self.out_first, self.away), self.far_first

        def both(left, right):
            return right if left is None else jnp.logical_and(left, right)

        def column(ok, fs, way, src):
            shard = self.shard(0, fs, self.c)
            if way >= 0:
                sems = (self.zs.at[kz, 0, fs], self.zr.at[kz, fs])
                up = self.send(j, shard, *inner, sems, src, fs=self.z + 1)
                todo.append((both(ok, self.z < nz - 1), up))
            if way <= 0:
                sems = (self.zs.at[kz, 1, fs], self.zr.at[kz, fs])
                down = self.send(j, shard, *inner, sems, src, fs=self.z - 1)
                todo.append((both(ok, self.z > 0), down))
            sems = (self.ys.at[k, fs], self.yr.at[k, fs])
            todo.append((ok, self.send(j, shard, *inner, sems, src, grp=self.far_row)))
            if way:
                sems = (self.xs.at[k, fs], self.xr.at[k, fs])
                todo.append((ok, self.send(j, shard, *outer, sems, rep=self.far_rep)))
            sems = (self.cs.at[k, fs], self.cr.at[k, fs])
            size = inner if way else (0, self.rows)
            todo.append((ok, self.send(j, shard, *size, sems, src, grp=self.far_core)))

        if a == 0:
            for ok, src in self.own_blocks(j):
                column(ok, self.z, 0, src)
        else:
            for ok, fs, way in self.at_distance(a):
                column(ok, fs, way, None)
        for ok, fs, _ in self.at_distance(a - 1):
            shard = self.shard(1, fs, self.c)
            sems = (self.xs.at[k, nz + fs], self.xr.at[k, nz + fs])
            todo.append((ok, self.send(j, shard, *outer, sems, rep=self.far_rep)))
            sems = (self.cs.at[k, nz + fs], self.cr.at[k, nz + fs])
            todo.append((ok, self.send(j, shard, *inner, sems, grp=self.far_core)))
        for other in (0, 1):
            for ok, fs, way in self.at_distance(a - 1 - other):
                if way or other:
                    i = other * nz + fs
                    sems = (self.ds.at[k, i], self.dr.at[k, i])
                    shard = self.shard(other, fs, self.c)
                    core = self.send(j, shard, far, self.away, sems, grp=self.far_core)
                    todo.append((ok, core))
        return todo

    def arrivals(self, a, j, t):
        todo, nz, k, kz = [], self.nz, lax.rem(t, self.slots), lax.rem(t, 2 * self.slots)
        inner, far = (self.in_first, self.stay), (self.far_first, self.away)

        def expect(ok, shard, first, size, sem):
            ref = self.dst.at[j, shard, pl.ds(first, size)]
            todo.append((ok, pltpu.make_async_copy(ref, ref, sem)))

        for ok, fs, way in self.at_distance(a):
            if way:
                expect(ok, self.shard(0, fs, self.c), *inner, self.zr.at[kz, fs])
        for ok, fs, _ in self.at_distance(a - 1):
            expect(ok, self.shard(1, fs, self.c), *inner, self.yr.at[k, fs])
        for other in (0, 1):
            for ok, fs, way in self.at_distance(a - 1 - other):
                i = other * nz + fs
                if way or other:
                    expect(ok, self.shard(other, fs, self.c), *far, self.xr.at[k, i])
                size = inner if way or other else (0, self.rows)
                expect(ok, self.shard(other, fs, 1 - self.c), *size, self.cr.at[k, i])
            for ok, fs, way in self.at_distance(a - 2 - other):
                if way or other:
                    i = other * nz + fs
                    expect(ok, self.shard(other, fs, 1 - self.c), *far, self.dr.at[k, i])
        return todo

    def run(self, early=None, compute=None):
        lag = self.lag

        def act(ok, fn):
            if ok is None:
                fn()
            else:
                pl.when(ok)(fn)

        def finish(a, j, t):
            for ok, copy in self.sends(a - 1, j, t):
                act(ok, copy.wait_send)
            for ok, copy in self.arrivals(a, j, t):
                act(ok, copy.wait)
            if a == 1:
                for ok, copy in self.keeps(j, t):
                    act(ok, copy.wait)

        def begin(a, j, t):
            for ok, copy in self.sends(a, j, t):
                act(ok, copy.start)
            if a == 0:
                for ok, copy in self.keeps(j, t):
                    act(ok, copy.start)

        def tick(t, carry):
            for a in range(self.last, 0, -1):
                j = t - lag * a
                pl.when((j >= 0) & (j < self.count))(functools.partial(finish, a, j, t - lag))
            for a in range(self.last - 1, -1, -1):
                j = t - lag * a
                pl.when((j >= 0) & (j < self.count))(functools.partial(begin, a, j, t))
            if early is not None:
                early(t)
            if compute is not None:
                j = t - lag * self.last
                pl.when(j >= 0)(functools.partial(compute, j))
            return carry

        lax.fori_loop(0, self.count + lag * self.last + (compute is not None), tick, 0)


def head_columns(ref, rows, part, h, width):
    first = pl.multiple_of(part * width + h * HDIM, HDIM)
    return ref[rows, pl.ds(first, HDIM)]


def seen(shape, first):
    row = lax.broadcasted_iota(jnp.int32, shape, 0)
    return lax.broadcasted_iota(jnp.int32, shape, 1) <= first + row


def head_chances(qkv, kp, h, prompt_len, width, first):
    own, cont = slice(0, prompt_len), slice(prompt_len, None)
    q_p = head_columns(qkv, own, 0, h, width)
    q_c = head_columns(qkv, cont, 0, h, width)
    k_c = head_columns(qkv, cont, 1, h, width)
    v_c = head_columns(qkv, cont, 2, h, width)
    lanes = pl.ds(pl.multiple_of(h * HDIM, HDIM), HDIM)
    k_p = kp[:, :, lanes].reshape(-1, HDIM)
    lanes = pl.ds(pl.multiple_of(width + h * HDIM, HDIM), HDIM)
    v_p = kp[:, :, lanes].reshape(-1, HDIM)
    s_p = mm_nt(q_p, k_p) * SCALE
    s_p = jnp.where(seen(s_p.shape, first), s_p, NEG_FILL)
    e_p = jnp.exp(s_p - jnp.max(s_p, axis=-1, keepdims=True))
    c_p = e_p * (1.0 / jnp.sum(e_p, axis=-1, keepdims=True))
    s_1 = mm_nt(q_c, k_p) * SCALE
    s_2 = mm_nt(q_c, k_c) * SCALE
    s_2 = jnp.where(seen(s_2.shape, 0), s_2, NEG_FILL)
    peak = jnp.maximum(
        jnp.max(s_1, axis=-1, keepdims=True), jnp.max(s_2, axis=-1, keepdims=True)
    )
    e_1, e_2 = jnp.exp(s_1 - peak), jnp.exp(s_2 - peak)
    mass = jnp.sum(e_1, axis=-1, keepdims=True) + jnp.sum(e_2, axis=-1, keepdims=True)
    inv = 1.0 / mass
    return (q_p, q_c, k_p, k_c, v_p, v_c), (c_p, e_1 * inv, e_2 * inv)


def columns_of(ref):
    return lambda j, first, size: ref.at[
        pl.ds(first, size), pl.ds(pl.multiple_of(j * BLOCK, BLOCK), BLOCK)
    ]


def tiles_of(ref, shard_rows, parts):
    def tile(j, first, size):
        row = pl.multiple_of(lax.rem(j, parts) * shard_rows + first, 8)
        return ref.at[pl.ds(row, size), pl.ds(pl.multiple_of(j // parts * BLOCK, BLOCK), BLOCK)]

    return tile


def select_call(ids, tables):
    def kernel(ids, *refs):
        for src, dst in zip(refs[: len(tables)], refs[len(tables) :]):
            dst[...] = src[0]

    def spec_in(t):
        return pl.BlockSpec((1,) + t.shape[1:], lambda i, ids: (ids[i],) + (0,) * (t.ndim - 1))

    def spec_out(t):
        lead = t.ndim - 3
        return pl.BlockSpec(t.shape[1:], lambda i, ids: (0,) * lead + (i, 0))

    return pl.pallas_call(
        kernel,
        grid_spec=pltpu.PrefetchScalarGridSpec(
            num_scalar_prefetch=1,
            grid=(2,),
            in_specs=[spec_in(t) for t in tables],
            out_specs=[spec_out(t) for t in tables],
        ),
        out_shape=[
            jax.ShapeDtypeStruct(t.shape[1:-2] + (2 * RANK, t.shape[-1]), BF) for t in tables
        ],
        name="select",
    )(ids, *tables)


def project_call(x_p, x_c, gain, bias, a_ext, b_ext, weight, n_fs, n_shard):
    prompt_len, width = x_p.shape
    rows = prompt_len + x_c.shape[0]
    shard_rows, count = weight.shape[0], weight.shape[1] // BLOCK
    per = width // BLOCK

    def kernel(
        x_p, x_c, gain, bias, a_ext, b_ext, src, dst, qkv, normed, lows, wbuf, wsem, *sems
    ):
        engine = Gather(n_fs, [(count, columns_of(src))], dst, sems)
        engine.barrier()

        def load(j):
            return pltpu.make_async_copy(dst.at[j], wbuf.at[lax.rem(j, 2)], wsem.at[lax.rem(j, 2)])

        def early(t):
            @pl.when(t == 0)
            def _():
                for x, part in ((x_p, slice(0, prompt_len)), (x_c, slice(prompt_len, None))):
                    hat, _ = norm_stats(x[...].astype(F32))
                    normed[part] = (hat * gain[...] + bias[...]).astype(BF)
                for n in range(3):
                    lows[n] = low_of(mm_nt(normed[...], a_ext[n]), prompt_len)

        def compute(j):
            @pl.when(j < count)
            def _():
                load(j).start()

            @pl.when(j > 0)
            def _():
                i = j - 1
                load(i).wait()
                n = i // per
                w = wbuf[lax.rem(i, 2)].reshape(-1, BLOCK)
                inside = pl.ds(pl.multiple_of(lax.rem(i, per) * BLOCK, BLOCK), BLOCK)
                extra = mm(lows[n], b_ext[n, :, inside])
                cols = pl.ds(pl.multiple_of(i * BLOCK, BLOCK), BLOCK)
                qkv[:, cols] = (mm(normed[...], w) + extra).astype(BF)

        engine.run(early, compute)

    return pl.pallas_call(
        kernel,
        out_shape=[
            jax.ShapeDtypeStruct((count, n_shard, shard_rows, BLOCK), BF),
            jax.ShapeDtypeStruct((rows, 3 * width), BF),
            jax.ShapeDtypeStruct((rows, width), BF),
            jax.ShapeDtypeStruct((3, rows, 2 * RANK), BF),
        ],
        in_specs=[WHOLE] * 6 + [ANY],
        out_specs=[ANY, WHOLE, WHOLE, WHOLE],
        scratch_shapes=[
            pltpu.VMEM((2, n_shard, shard_rows, BLOCK), BF),
            pltpu.SemaphoreType.DMA((2,)),
        ]
        + Gather.semaphores(n_fs),
        compiler_params=pltpu.CompilerParams(
            collective_id=0, has_side_effects=True, vmem_limit_bytes=ROOM
        ),
        name="project",
    )(x_p, x_c, gain, bias, a_ext, b_ext, weight)


def middle_call(x_p, x_c, cot_p, cot_c, qkv, gain, bias, tables, weights, n_fs, n_shard):
    prompt_len, width = x_p.shape
    rows = prompt_len + x_c.shape[0]
    shard_rows, hidden = weights[2].shape
    parts = weights[1].shape[0] // shard_rows
    n_out, n_up = width // BLOCK, hidden // BLOCK
    n_dn = n_out * parts
    count = n_out + n_dn + n_up
    n_grp = n_shard // n_fs
    heads = width // HDIM
    go, first_head = 4, 5
    first_out = first_head + heads
    a_o, b_o, a_u, b_u, a_d, b_d = range(6)

    def kernel(x_p, x_c, cot_p, cot_c, qkv, gain, bias, *refs):
        ext, src, refs = refs[:6], refs[6:9], refs[9:]
        (dst, kp, mixed, normed, res_p, res_c, resid_back, grad_attn), refs = refs[:8], refs[8:]
        (low_o, g_a_up, g_b_up, g_a_dn, g_b_dn), refs = refs[:5], refs[5:]
        (cot, resid, out_acc, low_up, dlow_dn, low_dn, dlow_up), refs = refs[:7], refs[7:]
        (wbuf, dbuf, wsem, dsem, ksend, krecv), sems = refs[:6], refs[6:]
        own, rest = slice(0, prompt_len), slice(prompt_len, None)
        sources = [
            (n_out, columns_of(src[0])),
            (n_dn, tiles_of(src[1], shard_rows, parts)),
            (n_up, columns_of(src[2])),
        ]
        engine = Gather(n_fs, sources, dst, sems)
        engine.barrier()
        grp = lax.axis_index("grp")

        def pass_on(n, whose, to):
            return pltpu.make_async_remote_copy(
                kp.at[whose],
                kp.at[whose],
                ksend.at[n],
                krecv.at[n],
                device_id={"grp": to},
                device_id_type=MESH,
            )

        def landed(n, whose):
            return pltpu.make_async_copy(kp.at[whose], kp.at[whose], krecv.at[n])

        to_row = pass_on(0, grp, engine.far_row)
        to_core = pass_on(1, grp, engine.far_core)
        onward = pass_on(2, engine.far_row, engine.far_core)
        diagonal = (1 - engine.y) * 2 + 1 - engine.c

        def load_out(b):
            return pltpu.make_async_copy(dst.at[b], wbuf.at[lax.rem(b, 2)], wsem.at[lax.rem(b, 2)])

        def early(t):
            @pl.when(t == 0)
            def _():
                kp[grp] = qkv[:prompt_len, width:]
                to_row.start()
                to_core.start()
                cot[own] = cot_p[...]
                cot[rest] = cot_c[...]
                dlow_dn[...] = low_of(mm_nt(cot[...], ext[b_d][...]), prompt_len)

            @pl.when(t == go)
            def _():
                landed(0, engine.far_row).wait()
                onward.start()

            @pl.when(t == first_head)
            def _():
                landed(1, engine.far_core).wait()
                landed(2, diagonal).wait()
                to_row.wait_send()
                to_core.wait_send()
                onward.wait_send()

            @pl.when((t >= first_head) & (t < first_out))
            def _():
                h = t - first_head
                (_, _, _, _, v_p, v_c), (c_p, c_1, c_2) = head_chances(
                    qkv, kp, h, prompt_len, width, grp * prompt_len
                )
                lanes = pl.ds(pl.multiple_of(h * HDIM, HDIM), HDIM)
                mixed[:prompt_len, lanes] = mm(c_p.astype(BF), v_p).astype(BF)
                mixed[prompt_len:, lanes] = (
                    mm(c_1.astype(BF), v_p) + mm(c_2.astype(BF), v_c)
                ).astype(BF)

            @pl.when(t == first_out - 1)
            def _():
                load_out(0).start()

            @pl.when((t >= first_out) & (t < first_out + n_out))
            def _():
                b = t - first_out

                @pl.when(b == 0)
                def _():
                    low_o[...] = low_of(mm_nt(mixed[...], ext[a_o][...]), prompt_len)

                load_out(b).wait()

                @pl.when(b + 1 < n_out)
                def _():
                    load_out(b + 1).start()

                cols = pl.ds(pl.multiple_of(b * BLOCK, BLOCK), BLOCK)
                w = wbuf[lax.rem(b, 2)].reshape(-1, BLOCK)
                branch = mm(mixed[...], w) + mm(low_o[...], ext[b_o][:, cols])
                resid[own, cols] = x_p[:, cols].astype(F32) + branch[own]
                resid[rest, cols] = x_c[:, cols].astype(F32) + branch[rest]

            @pl.when(t == first_out + n_out)
            def _():
                hat, _ = norm_stats(resid[...])
                normed[...] = (hat * gain[...] + bias[...]).astype(BF)
                low_up[...] = low_of(mm_nt(normed[...], ext[a_u][...]), prompt_len)
                out_acc[...] = resid[...]
                resid_back[...] = jnp.zeros_like(resid_back)
                low_dn[...] = jnp.zeros_like(low_dn)
                dlow_up[...] = jnp.zeros_like(dlow_up)

        def load_up(n):
            k = lax.rem(n, 2)
            up = pltpu.make_async_copy(dst.at[n_out + n_dn + n], wbuf.at[k], wsem.at[k])
            down = pltpu.make_async_copy(dst.at[pl.ds(n_out, n_dn), n], dbuf.at[k], dsem.at[k])
            return up, down

        def compute(j):
            n = j - (n_out + n_dn)

            @pl.when((n >= 0) & (n < n_up))
            def _():
                for copy in load_up(n):
                    copy.start()

            @pl.when(n > 0)
            def _():
                i = n - 1
                for copy in load_up(i):
                    copy.wait()
                k = lax.rem(i, 2)
                cols = pl.ds(pl.multiple_of(i * BLOCK, BLOCK), BLOCK)
                w_up = wbuf[k].reshape(-1, BLOCK)
                a_dn, b_up = ext[a_d][:, cols], ext[b_u][:, cols]
                pre = mm(normed[...], w_up) + mm(low_up[...], b_up)
                cdf = 0.5 * (1.0 + lax.erf(pre * math.sqrt(0.5)))
                act = (pre * cdf).astype(BF)
                slope = cdf + pre * jnp.exp(-0.5 * pre * pre) * (1.0 / math.sqrt(2.0 * math.pi))
                grad_act = mm(dlow_dn[...], a_dn)
                for b in range(n_out):
                    w_dn = dbuf[k, b * parts : (b + 1) * parts].reshape(BLOCK, BLOCK)
                    span = slice(b * BLOCK, (b + 1) * BLOCK)
                    grad_act = grad_act + mm_nt(cot[:, span], w_dn)
                    out_acc[:, span] += mm(act, w_dn)
                grad_pre = (grad_act * slope).astype(BF)
                resid_back[...] += mm_nt(grad_pre, w_up)
                low_dn[...] += mm_nt(act, a_dn)
                dlow_up[...] += mm_nt(grad_pre, b_up)
                g_b_up[:, cols] = mm_tn(low_up[...], grad_pre).astype(BF)
                g_a_dn[:, cols] = mm_tn(dlow_dn[...], act).astype(BF)

        engine.run(early, compute)
        low = low_of(low_dn[...], prompt_len)
        result = (out_acc[...] + mm(low, ext[b_d][...])).astype(BF)
        res_p[...] = result[own]
        res_c[...] = result[rest]
        g_b_dn[...] = mm_tn(low, cot[...]).astype(BF)
        dlow = low_of(dlow_up[...], prompt_len)
        g_a_up[...] = mm_tn(dlow, normed[...]).astype(BF)
        grad = resid_back[...] + mm(dlow, ext[a_u][...])
        grad = cot[...].astype(F32) + norm_back(resid[...], gain[...], grad)
        resid_back[...] = grad
        grad_attn[...] = grad.astype(BF)

    like = jax.ShapeDtypeStruct
    two = 2 * RANK
    return pl.pallas_call(
        kernel,
        out_shape=[
            like((count, n_shard, shard_rows, BLOCK), BF),
            like((n_grp, prompt_len, 2 * width), BF),
            like((rows, width), BF),
            like((rows, width), BF),
            like(x_p.shape, BF),
            like(x_c.shape, BF),
            like((rows, width), F32),
            like((rows, width), BF),
            like((rows, two), BF),
            like((two, width), BF),
            like((two, hidden), BF),
            like((two, hidden), BF),
            like((two, width), BF),
        ],
        in_specs=[WHOLE] * 13 + [ANY] * 3,
        out_specs=[ANY] + [WHOLE] * 12,
        scratch_shapes=[
            pltpu.VMEM((rows, width), BF),
            pltpu.VMEM((rows, width), F32),
            pltpu.VMEM((rows, width), F32),
            pltpu.VMEM((rows, two), BF),
            pltpu.VMEM((rows, two), BF),
            pltpu.VMEM((rows, two), F32),
            pltpu.VMEM((rows, two), F32),
            pltpu.VMEM((2, n_shard, shard_rows, BLOCK), BF),
            pltpu.VMEM((2, n_dn, shard_rows, BLOCK), BF),
            pltpu.SemaphoreType.DMA((2,)),
            pltpu.SemaphoreType.DMA((2,)),
            pltpu.SemaphoreType.DMA((3,)),
            pltpu.SemaphoreType.DMA((3,)),
        ]
        + Gather.semaphores(n_fs),
        compiler_params=pltpu.CompilerParams(
            collective_id=1, has_side_effects=True, vmem_limit_bytes=ROOM
        ),
        name="middle",
    )(x_p, x_c, cot_p, cot_c, qkv, gain, bias, *tables, *weights)


PIECES = 8


class TableSum:
    def __init__(self, n_fs, hots, units, bufs, sems):
        self.n_fs, self.hots, self.units = n_fs, hots, units
        self.out, self.got, self.dense, self.parts, self.sums = bufs
        (self.s1, self.r1, self.s2, self.r2, self.s3, self.r3) = sems
        rep, self.grp = lax.axis_index("rep"), lax.axis_index("grp")
        self.z = lax.axis_index("fs")
        plane = rep % 2
        y, c = self.grp // 2, self.grp % 2
        self.me = plane * 4 + self.grp
        self.peers = []
        for q in range(1, PIECES):
            x_to = 1 - plane if q // 4 else plane
            y_to = 1 - y if q // 2 % 2 else y
            c_to = 1 - c if q % 2 else c
            where = {"grp": y_to * 2 + c_to}
            if q // 4:
                where["rep"] = rep + 1 - 2 * plane
            self.peers.append((q, x_to * 4 + y_to * 2 + c_to, where))
        self.piece = self.out.shape[2] // units

    @staticmethod
    def scratch(n_fs, units, piece, count):
        two, wide = 2 * RANK, units * piece
        rows = count * RANK // n_fs
        bufs = [
            pltpu.VMEM((PIECES, two, wide), BF),
            pltpu.VMEM((PIECES, two, wide), BF),
            pltpu.VMEM((n_fs, rows, wide), BF),
            pltpu.VMEM((n_fs, rows, wide), BF),
            pltpu.VMEM((PIECES, rows, wide), BF),
        ]
        dma = pltpu.SemaphoreType.DMA
        return bufs, [dma((PIECES,))] * 2 + [dma((n_fs,))] * 2 + [dma((PIECES,))] * 2

    def pack(self, unit, value, first=0):
        value = value.astype(BF)
        cols = slice(unit * self.piece, (unit + 1) * self.piece)
        for n in range(value.shape[1] // self.piece):
            self.out[first + n, :, cols] = value[:, n * self.piece : (n + 1) * self.piece]

    def exchange(self):
        return [
            pltpu.make_async_remote_copy(
                self.out.at[to],
                self.got.at[self.me],
                self.s1.at[q],
                self.r1.at[q],
                device_id=where,
                device_id_type=MESH,
            )
            for q, to, where in self.peers
        ]

    def along_fs(self):
        copies = []
        for d in range(1, self.n_fs):
            to = lax.rem(self.z + d, self.n_fs)
            copies.append(
                pltpu.make_async_remote_copy(
                    self.dense.at[to],
                    self.parts.at[self.z],
                    self.s2.at[d],
                    self.r2.at[d],
                    device_id={"fs": to},
                    device_id_type=MESH,
                )
            )
        return copies

    def hand_out(self):
        return [
            pltpu.make_async_remote_copy(
                self.sums.at[self.me],
                self.sums.at[self.me],
                self.s3.at[q],
                self.r3.at[q],
                device_id=where,
                device_id_type=MESH,
            )
            for q, _, where in self.peers
        ]

    def first(self):
        for copy in self.exchange():
            copy.start()
        self.got[self.me] = self.out[self.me]

    def second(self):
        for q, whose, _ in self.peers:
            ref = self.got.at[whose]
            pltpu.make_async_copy(ref, ref, self.r1.at[q]).wait()
        for copy in self.exchange():
            copy.wait_send()
        wide = self.out.shape[2]
        hots = self.hots[...].reshape(PIECES * 2 * RANK, -1)
        dense = mm_tn(hots, self.got[...].reshape(PIECES * 2 * RANK, wide))
        self.dense[...] = dense.astype(BF).reshape(self.dense.shape)
        for copy in self.along_fs():
            copy.start()
        self.parts[self.z] = self.dense[self.z]

    def third(self):
        for d in range(1, self.n_fs):
            ref = self.parts.at[lax.rem(self.z + self.n_fs - d, self.n_fs)]
            pltpu.make_async_copy(ref, ref, self.r2.at[d]).wait()
        for copy in self.along_fs():
            copy.wait_send()
        total = self.parts[0].astype(F32)
        for n in range(1, self.n_fs):
            total = total + self.parts[n].astype(F32)
        self.sums[self.me] = total.astype(BF)
        for copy in self.hand_out():
            copy.start()

    def last(self, places):
        for q, whose, _ in self.peers:
            ref = self.sums.at[whose]
            pltpu.make_async_copy(ref, ref, self.r3.at[q]).wait()
        for copy in self.hand_out():
            copy.wait_send()
        for unit, place in enumerate(places):
            for k in range(PIECES):
                cols = slice(unit * self.piece, (unit + 1) * self.piece)
                for a in range(self.sums.shape[1] // RANK):
                    value = self.sums[k, a * RANK : (a + 1) * RANK, cols]
                    place(a, k * self.piece, value)


def back_call(
    grad_attn, mixed, low_o, lows, gain, a_ext, b_ext, hot, mid, qkv, kp, x_p, x_c, normed, grad_resid, w_rest, w_qkv, n_fs, count
):
    rows, width = grad_attn.shape
    prompt_len, cont_len = x_p.shape[0], x_c.shape[0]
    heads = width // HDIM
    n_grp = kp.shape[0]
    n_shard, shard_rows = w_qkv.shape[1:3]
    per = width // BLOCK
    n_qkv = w_qkv.shape[0]
    hidden = mid[1].shape[1]
    adapters = count // n_fs
    half_heads = heads // 2
    half = half_heads * HDIM
    two = 2 * RANK
    wide_units = hidden // width
    first_units = 2 * wide_units + 4
    last_units = 6
    piece = width // PIECES

    def kernel(*refs):
        (grad_attn, mixed, low_o, lows, gain, a_ext, b_ext, hot), refs = refs[:8], refs[8:]
        (g_a_up, g_b_up, g_a_dn, g_b_dn), refs = refs[:4], refs[4:]
        (qkv, kp, x_p, x_c, normed, grad_resid, w_rest, w_qkv), refs = refs[:8], refs[8:]
        (out_p, out_c, t_a, t_b, t_a_up, t_b_up, t_a_dn, t_b_dn), refs = refs[:8], refs[8:]
        (grads, keep, late, x, normed_here, wbuf, gm, acc, dlow, dlow_o), refs = refs[:10], refs[10:]
        (far, far_core, far_row, hots), refs = refs[:4], refs[4:]
        bufs_one, bufs_two, refs = refs[:5], refs[5:10], refs[10:]
        sems_one, sems_two, refs = refs[:6], refs[6:12], refs[12:]
        lsem, wsem, csend, crecv, rsend, rrecv, hsend, hrecv = refs
        grp = lax.axis_index("grp")
        y, c = grp // 2, grp % 2
        own, rest = slice(0, prompt_len), slice(prompt_len, None)
        one = TableSum(n_fs, hots, first_units, bufs_one, sems_one)
        two_ = TableSum(n_fs, hots, last_units, bufs_two, sems_two)
        barrier = pltpu.get_barrier_semaphore()
        for _, _, where in one.peers:
            pl.semaphore_signal(barrier, 1, device_id=where, device_id_type=MESH)
        for d in range(1, n_fs):
            to = lax.rem(one.z + d, n_fs)
            pl.semaphore_signal(barrier, 1, device_id={"fs": to}, device_id_type=MESH)

        loads = [
            pltpu.make_async_copy(src, dst, lsem.at[n])
            for n, (src, dst) in enumerate(
                [
                    (qkv, grads),
                    (kp, keep),
                    (grad_resid, late),
                    (normed, normed_here),
                    (x_p, x.at[pl.ds(0, prompt_len)]),
                    (x_c, x.at[pl.ds(prompt_len, cont_len)]),
                ]
            )
        ]
        for copy in loads:
            copy.start()

        def load_w(ref, i, k):
            return pltpu.make_async_copy(ref.at[i], wbuf.at[k], wsem.at[k])

        load_w(w_rest, 0, 0).start()
        pl.semaphore_wait(barrier, len(one.peers) + n_fs - 1)

        hots[one.me] = hot[...]
        hot_sends = [
            pltpu.make_async_remote_copy(
                hots.at[one.me],
                hots.at[one.me],
                hsend.at[q],
                hrecv.at[q],
                device_id=where,
                device_id_type=MESH,
            )
            for q, _, where in one.peers
        ]
        for copy in hot_sends:
            copy.start()
        for n in range(wide_units):
            one.pack(n, g_b_up[:, n * width : (n + 1) * width])
            one.pack(wide_units + n, g_a_dn[:, n * width : (n + 1) * width])
        one.pack(2 * wide_units, g_a_up[...])
        one.pack(2 * wide_units + 1, g_b_dn[...])
        dlow_o[...] = low_of(mm_nt(grad_attn[...], b_ext[3]), prompt_len)
        one.pack(2 * wide_units + 2, mm_tn(dlow_o[...], mixed[...]))
        one.pack(2 * wide_units + 3, mm_tn(low_o[...], grad_attn[...]))
        one.first()

        acc[...] = mm(dlow_o[...], a_ext[3])
        for n in range(per):
            load_w(w_rest, n, n % 2).wait()
            if n + 1 < per:
                load_w(w_rest, n + 1, (n + 1) % 2).start()
            w = wbuf[n % 2].reshape(-1, BLOCK)
            acc[...] += mm_nt(grad_attn[:, n * BLOCK : (n + 1) * BLOCK], w)
        gm[...] = acc[...].astype(BF)
        load_w(w_qkv, 0, 0).start()
        load_w(w_qkv, 1, 1).start()

        loads[0].wait()
        loads[1].wait()

        def head(part, n, carry):
            h = part * half_heads + n
            first = grp * prompt_len
            (q_p, q_c, k_p, k_c, v_p, v_c), (c_p, c_1, c_2) = head_chances(
                grads, keep, h, prompt_len, width, first
            )
            lanes = [
                pl.ds(pl.multiple_of(i * width + h * HDIM, HDIM), HDIM) for i in range(3)
            ]
            gm_p, gm_c = gm[own, lanes[0]], gm[rest, lanes[0]]
            d_p = mm_nt(gm_p, v_p)
            d_1, d_2 = mm_nt(gm_c, v_p), mm_nt(gm_c, v_c)
            s_p = (c_p * (d_p - jnp.sum(c_p * d_p, axis=-1, keepdims=True))).astype(BF)
            inner = jnp.sum(c_1 * d_1, axis=-1, keepdims=True) + jnp.sum(
                c_2 * d_2, axis=-1, keepdims=True
            )
            s_1 = (c_1 * (d_1 - inner)).astype(BF)
            s_2 = (c_2 * (d_2 - inner)).astype(BF)
            grads[own, lanes[0]] = (mm(s_p, k_p) * SCALE).astype(BF)
            grads[rest, lanes[0]] = ((mm(s_1, k_p) + mm(s_2, k_c)) * SCALE).astype(BF)
            grads[rest, lanes[1]] = (mm_tn(s_2, q_c) * SCALE).astype(BF)
            grads[rest, lanes[2]] = mm_tn(c_2.astype(BF), gm_c).astype(BF)
            g_k = ((mm_tn(s_p, q_p) + mm_tn(s_1, q_c)) * SCALE).astype(BF)
            g_v = (mm_tn(c_p.astype(BF), gm_p) + mm_tn(c_1.astype(BF), gm_c)).astype(BF)
            into = [pl.ds(pl.multiple_of(i * half + n * HDIM, HDIM), HDIM) for i in range(2)]
            far[part, :, :, into[0]] = g_k.reshape(n_grp, prompt_len, HDIM)
            far[part, :, :, into[1]] = g_v.reshape(n_grp, prompt_len, HDIM)
            return carry

        def to_core(part):
            return [
                pltpu.make_async_remote_copy(
                    far.at[part, row * 2 + 1 - c],
                    far_core.at[part, row],
                    csend.at[part, row],
                    crecv.at[part, row],
                    device_id={"grp": y * 2 + 1 - c},
                    device_id_type=MESH,
                )
                for row in range(2)
            ]

        def to_row(part):
            return pltpu.make_async_remote_copy(
                far.at[part, (1 - y) * 2 + c],
                far_row.at[part],
                rsend.at[part],
                rrecv.at[part],
                device_id={"grp": (1 - y) * 2 + c},
                device_id_type=MESH,
            )

        def add_core(part):
            for copy in to_core(part):
                copy.wait()
            for row in range(2):
                total = far[part, row * 2 + c].astype(F32) + far_core[part, row].astype(F32)
                far[part, row * 2 + c] = total.astype(BF)
            to_row(part).start()

        def add_row(part):
            to_row(part).wait()
            total = far[part, grp].astype(F32) + far_row[part].astype(F32)
            total = total.astype(BF)
            for i in range(2):
                cols = slice((i + 1) * width + part * half, (i + 1) * width + (part + 1) * half)
                grads[own, cols] = total[:, i * half : (i + 1) * half]

        lax.fori_loop(0, half_heads, functools.partial(head, 0), 0)
        for copy in to_core(0):
            copy.start()
        for copy in hot_sends:
            copy.wait_send()
        for q, whose, _ in one.peers:
            pltpu.make_async_copy(hots.at[whose], hots.at[whose], hrecv.at[q]).wait()
        one.second()
        lax.fori_loop(0, half_heads // 2, functools.partial(head, 1), 0)
        add_core(0)
        lax.fori_loop(half_heads // 2, half_heads, functools.partial(head, 1), 0)
        for copy in to_core(1):
            copy.start()
        one.third()

        acc[...] = jnp.zeros_like(acc)
        dlow[...] = jnp.zeros_like(dlow)

        def project(i, m, carry):
            n = i * per + m
            k = lax.rem(n, 2)
            load_w(w_qkv, n, k).wait()
            part = grads[:, pl.ds(pl.multiple_of(n * BLOCK, BLOCK), BLOCK)]
            acc[...] += mm_nt(part, wbuf[k].reshape(-1, BLOCK))
            dlow[i] += mm_nt(part, b_ext[i, :, pl.ds(pl.multiple_of(m * BLOCK, BLOCK), BLOCK)])
            two_.pack(3 + i, mm_tn(lows[i], part), m * (BLOCK // piece))

            @pl.when(n + 2 < n_qkv)
            def _():
                load_w(w_qkv, n + 2, k).start()

            return carry

        lax.fori_loop(0, 1, functools.partial(project, 0), 0)
        add_core(1)
        lax.fori_loop(1, per, functools.partial(project, 0), 0)
        add_row(0)
        add_row(1)
        for i in (1, 2):
            lax.fori_loop(0, per, functools.partial(project, i), 0)

        for copy in loads[2:]:
            copy.wait()
        for i in range(3):
            low = low_of(dlow[i], prompt_len)
            acc[...] += mm(low, a_ext[i])
            two_.pack(i, mm_tn(low, normed_here[...]))
        two_.first()
        back = late[...] + norm_back(x[...].astype(F32), gain[...], acc[...])
        back = back.astype(BF)
        out_p[...] = back[own]
        out_c[...] = back[rest]

        def whole(ref, first):
            def place(a, col, value):
                ref[a, :, first + col : first + col + piece] = value

            return place

        def one_map(ref, n):
            def place(a, col, value):
                ref[a, n, :, col : col + piece] = value

            return place

        one.last(
            [whole(t_b_up, n * width) for n in range(wide_units)]
            + [whole(t_a_dn, n * width) for n in range(wide_units)]
            + [whole(t_a_up, 0), whole(t_b_dn, 0), one_map(t_a, 3), one_map(t_b, 3)]
        )
        two_.second()
        two_.third()
        two_.last([one_map(t_a, n) for n in range(3)] + [one_map(t_b, n) for n in range(3)])

    like = jax.ShapeDtypeStruct
    bufs_one, sems_one = TableSum.scratch(n_fs, first_units, piece, count)
    bufs_two, sems_two = TableSum.scratch(n_fs, last_units, piece, count)
    dma = pltpu.SemaphoreType.DMA
    return pl.pallas_call(
        kernel,
        out_shape=[
            like(x_p.shape, BF),
            like(x_c.shape, BF),
            like((adapters, 4, RANK, width), BF),
            like((adapters, 4, RANK, width), BF),
            like((adapters, RANK, width), BF),
            like((adapters, RANK, hidden), BF),
            like((adapters, RANK, hidden), BF),
            like((adapters, RANK, width), BF),
        ],
        in_specs=[WHOLE] * 12 + [ANY] * 8,
        out_specs=[WHOLE] * 8,
        scratch_shapes=[
            pltpu.VMEM((rows, 3 * width), BF),
            pltpu.VMEM(kp.shape, BF),
            pltpu.VMEM((rows, width), F32),
            pltpu.VMEM((rows, width), BF),
            pltpu.VMEM((rows, width), BF),
            pltpu.VMEM((2, n_shard, shard_rows, BLOCK), BF),
            pltpu.VMEM((rows, width), BF),
            pltpu.VMEM((rows, width), F32),
            pltpu.VMEM((3, rows, two), F32),
            pltpu.VMEM((rows, two), BF),
            pltpu.VMEM((2, n_grp, prompt_len, 2 * half), BF),
            pltpu.VMEM((2, 2, prompt_len, 2 * half), BF),
            pltpu.VMEM((2, prompt_len, 2 * half), BF),
            pltpu.VMEM((PIECES,) + hot.shape, BF),
        ]
        + bufs_one
        + bufs_two
        + sems_one
        + sems_two
        + [dma((6,)), dma((2,)), dma((2, 2)), dma((2, 2)), dma((2,)), dma((2,))]
        + [dma((PIECES,)), dma((PIECES,))],
        compiler_params=pltpu.CompilerParams(
            collective_id=2, has_side_effects=True, vmem_limit_bytes=ROOM
        ),
        name="back",
    )(
        grad_attn, mixed, low_o, lows, gain, a_ext, b_ext, hot, *mid,
        qkv, kp, x_p, x_c, normed, grad_resid, w_rest, w_qkv,
    )


def make_body(sizes):
    n_rep, n_grp, n_fs = sizes
    n_shard = n_grp * n_fs

    def other_pairs(v):
        step = 2
        while step < n_rep:
            far = lax.ppermute(v, "rep", [(i, i ^ step) for i in range(n_rep)])
            v = (v.astype(F32) + far.astype(F32)).astype(BF)
            step *= 2
        return v.astype(F32)

    def body(
        prompt_input_rows,
        continuation_input,
        prompt_group_adapter,
        continuation_adapter,
        first_norm_scale,
        first_norm_bias,
        second_norm_scale,
        second_norm_bias,
        frozen_query_key_value,
        frozen_output_weight,
        frozen_up_weight,
        frozen_down_weight,
        adapter_attention_input,
        adapter_attention_output,
        adapter_up_input,
        adapter_up_output,
        adapter_down_input,
        adapter_down_output,
        prompt_cotangent,
        continuation_cotangent,
    ):
        prompt_len, width = prompt_input_rows.shape[2:]
        count = adapter_up_input.shape[0]
        hidden = frozen_up_weight.shape[1]
        shard_rows = frozen_query_key_value.shape[0]
        assert n_grp == 4 and hidden == n_shard * BLOCK
        assert frozen_down_weight.shape[0] == BLOCK and BLOCK % shard_rows == 0

        def flat(v):
            return v.reshape(v.shape[-2:])

        x_p, x_c = flat(prompt_input_rows), flat(continuation_input)
        cot_p, cot_c = flat(prompt_cotangent), flat(continuation_cotangent)
        ids = jnp.concatenate([prompt_group_adapter.reshape(1), continuation_adapter.reshape(1)])
        a_ext, b_ext, a_up, b_up, a_dn, b_dn = select_call(
            ids,
            [
                adapter_attention_input.swapaxes(2, 3),
                adapter_attention_output,
                adapter_up_input.swapaxes(1, 2),
                adapter_up_output,
                adapter_down_input.swapaxes(1, 2),
                adapter_down_output,
            ],
        )
        place = jnp.repeat(ids, RANK) * RANK + jnp.arange(2 * RANK) % RANK
        hot = (place[:, None] == jnp.arange(count * RANK)[None, :]).astype(BF)
        gain_one, bias_one, gain_two, bias_two = [
            v[None, :]
            for v in (first_norm_scale, first_norm_bias, second_norm_scale, second_norm_bias)
        ]
        w_qkv, qkv, normed_one, lows = project_call(
            x_p, x_c, gain_one, bias_one, a_ext, b_ext, frozen_query_key_value, n_fs, n_shard
        )
        (
            w_rest,
            kp,
            mixed,
            normed_two,
            res_p,
            res_c,
            grad_resid,
            grad_attn,
            low_o,
            *mid,
        ) = middle_call(
            x_p,
            x_c,
            cot_p,
            cot_c,
            qkv,
            gain_two,
            bias_two,
            (a_ext[3], b_ext[3], a_up, b_up, a_dn, b_dn),
            (frozen_output_weight, frozen_down_weight, frozen_up_weight),
            n_fs,
            n_shard,
        )
        grad_p, grad_c, t_a, t_b, t_a_up, t_b_up, t_a_dn, t_b_dn = back_call(
            grad_attn,
            mixed,
            low_o,
            lows,
            gain_one,
            a_ext,
            b_ext,
            hot,
            mid,
            qkv,
            kp,
            x_p,
            x_c,
            normed_one,
            grad_resid,
            w_rest,
            w_qkv,
            n_fs,
            count,
        )
        return (
            res_p.reshape(prompt_input_rows.shape),
            res_c.reshape(continuation_input.shape),
            grad_p.reshape(prompt_input_rows.shape),
            grad_c.reshape(continuation_input.shape),
            other_pairs(t_a).swapaxes(2, 3),
            other_pairs(t_b),
            other_pairs(t_a_up).swapaxes(1, 2),
            other_pairs(t_b_up),
            other_pairs(t_a_dn).swapaxes(1, 2),
            other_pairs(t_b_dn),
        )

    return body


def solution(mesh):
    sizes = (mesh.shape["rep"], mesh.shape["grp"], mesh.shape["fs"])
    rows_in = P("rep", "fs", "grp", None)
    conts_in = P("rep", "fs", "grp", None, None)
    weight = P(("grp", "fs"), None)
    return jax.shard_map(
        make_body(sizes),
        mesh=mesh,
        in_specs=(
            rows_in,
            conts_in,
            P("rep", "fs"),
            P("rep", "fs", "grp"),
            P(),
            P(),
            P(),
            P(),
            weight,
            weight,
            weight,
            weight,
            P(),
            P(),
            P(),
            P(),
            P(),
            P(),
            rows_in,
            conts_in,
        ),
        out_specs=(
            rows_in,
            conts_in,
            rows_in,
            conts_in,
            P("fs", None, None, None),
            P("fs", None, None, None),
            P("fs", None, None),
            P("fs", None, None),
            P("fs", None, None),
            P("fs", None, None),
        ),
        check_vma=False,
    )
```

```python
import functools
import math

import jax
import jax.numpy as jnp
from jax import lax
from jax.experimental import pallas as pl
from jax.experimental.pallas import tpu as pltpu
from jax.sharding import PartitionSpec as P

HDIM = 128
RANK = 16
BLOCK = 512
PART = 256
SCALE = HDIM ** (-0.5)
NEG_FILL = -1e30
BF = jnp.bfloat16
F32 = jnp.float32
MESH = pl.DeviceIdType.MESH
ANY = pl.BlockSpec(memory_space=pl.ANY)
WHOLE = pl.BlockSpec(memory_space=pltpu.VMEM)
ROOM = 62 * 2**20


def mm(a, b):
    return jnp.dot(a, b, preferred_element_type=F32)


def mm_nt(a, b):
    return lax.dot_general(a, b, (((1,), (1,)), ((), ())), preferred_element_type=F32)


def mm_tn(a, b):
    return lax.dot_general(a, b, (((0,), (0,)), ((), ())), preferred_element_type=F32)


def norm_stats(values):
    center = values - jnp.mean(values, axis=-1, keepdims=True)
    spread = jnp.mean(center * center, axis=-1, keepdims=True)
    rstd = lax.rsqrt(spread + 1e-05)
    return center * rstd, rstd


def norm_back(values, gain, grad):
    hat, rstd = norm_stats(values)
    e = grad * gain
    return (
        e - jnp.mean(e, axis=-1, keepdims=True) - hat * jnp.mean(e * hat, axis=-1, keepdims=True)
    ) * rstd


def low_of(product, prompt_len):
    row = lax.broadcasted_iota(jnp.int32, product.shape, 0)
    col = lax.broadcasted_iota(jnp.int32, product.shape, 1)
    return jnp.where((row < prompt_len) == (col < RANK), product, 0.0).astype(BF)


class Gather:
    def __init__(self, n_fs, sources, dst, sems, lag=2, away=48):
        (self.zs, self.zr, self.ys, self.yr, self.xs, self.xr) = sems[:6]
        (self.cs, self.cr, self.ds, self.dr, self.loc) = sems[6:]
        self.nz, self.sources, self.dst = n_fs, sources, dst
        self.count, self.rows = dst.shape[0], dst.shape[2]
        self.lag, self.slots, self.last = lag, 2 * lag, n_fs + 2
        rep, grp = lax.axis_index("rep"), lax.axis_index("grp")
        self.z = lax.axis_index("fs")
        self.y, self.c, plane = grp // 2, grp % 2, rep % 2
        self.far_rep = rep + 1 - 2 * plane
        self.far_core = self.y * 2 + 1 - self.c
        self.far_row = (1 - self.y) * 2 + self.c
        self.own = grp * n_fs + self.z
        self.away, self.stay = away, self.rows - away
        self.in_first = pl.multiple_of(away * plane, 8)
        self.out_first = pl.multiple_of(self.stay * plane, 8)
        self.far_first = pl.multiple_of(self.stay * (1 - plane), 8)

    @staticmethod
    def semaphores(n_fs, lag=2):
        slots, dma = 2 * lag, pltpu.SemaphoreType.DMA
        return (
            [dma((2 * slots, 2, n_fs)), dma((2 * slots, n_fs))]
            + [dma((slots, n_fs))] * 2
            + [dma((slots, 2 * n_fs))] * 6
            + [dma((slots,))]
        )

    def barrier(self):
        sem = pltpu.get_barrier_semaphore()

        def greet(**where):
            pl.semaphore_signal(sem, 1, device_id=where, device_id_type=MESH)

        greet(rep=self.far_rep)
        greet(grp=self.far_core)
        greet(grp=self.far_row)
        below, above = self.z > 0, self.z < self.nz - 1
        pl.when(below)(lambda: greet(fs=self.z - 1))
        pl.when(above)(lambda: greet(fs=self.z + 1))
        pl.semaphore_wait(sem, 3 + below.astype(jnp.int32) + above.astype(jnp.int32))

    def at_distance(self, d):
        if d < 0 or d >= self.nz:
            return []
        if d == 0:
            return [(None, self.z, 0)]
        return [(self.z >= d, self.z - d, 1), (self.z < self.nz - d, self.z + d, -1)]

    def shard(self, other, fs, core):
        row = 1 - self.y if other else self.y
        return (row * 2 + core) * self.nz + fs

    def send(self, j, shard, first, size, sems, src=None, **where):
        rows = pl.ds(first, size)
        return pltpu.make_async_remote_copy(
            self.dst.at[j, shard, rows] if src is None else src(first, size),
            self.dst.at[j, shard, rows],
            *sems,
            device_id=where,
            device_id_type=MESH,
        )

    def own_blocks(self, j):
        start = 0
        for count, ref in self.sources:
            ok = (j >= start) & (j < start + count) if len(self.sources) > 1 else None
            yield ok, functools.partial(ref, j - start)
            start += count

    def keeps(self, j, t):
        sem = self.loc.at[lax.rem(t, self.slots)]
        for ok, src in self.own_blocks(j):
            yield ok, pltpu.make_async_copy(src(0, self.rows), self.dst.at[j, self.own], sem)

    def sends(self, a, j, t):
        todo, nz, k, kz = [], self.nz, lax.rem(t, self.slots), lax.rem(t, 2 * self.slots)
        inner, outer, far = (self.in_first, self.stay), (self.out_first, self.away), self.far_first

        def both(left, right):
            return right if left is None else jnp.logical_and(left, right)

        def column(ok, fs, way, src):
            shard = self.shard(0, fs, self.c)
            if way >= 0:
                sems = (self.zs.at[kz, 0, fs], self.zr.at[kz, fs])
                up = self.send(j, shard, *inner, sems, src, fs=self.z + 1)
                todo.append((both(ok, self.z < nz - 1), up))
            if way <= 0:
                sems = (self.zs.at[kz, 1, fs], self.zr.at[kz, fs])
                down = self.send(j, shard, *inner, sems, src, fs=self.z - 1)
                todo.append((both(ok, self.z > 0), down))
            sems = (self.ys.at[k, fs], self.yr.at[k, fs])
            todo.append((ok, self.send(j, shard, *inner, sems, src, grp=self.far_row)))
            if way:
                sems = (self.xs.at[k, fs], self.xr.at[k, fs])
                todo.append((ok, self.send(j, shard, *outer, sems, rep=self.far_rep)))
            sems = (self.cs.at[k, fs], self.cr.at[k, fs])
            size = inner if way else (0, self.rows)
            todo.append((ok, self.send(j, shard, *size, sems, src, grp=self.far_core)))

        if a == 0:
            for ok, src in self.own_blocks(j):
                column(ok, self.z, 0, src)
        else:
            for ok, fs, way in self.at_distance(a):
                column(ok, fs, way, None)
        for ok, fs, _ in self.at_distance(a - 1):
            shard = self.shard(1, fs, self.c)
            sems = (self.xs.at[k, nz + fs], self.xr.at[k, nz + fs])
            todo.append((ok, self.send(j, shard, *outer, sems, rep=self.far_rep)))
            sems = (self.cs.at[k, nz + fs], self.cr.at[k, nz + fs])
            todo.append((ok, self.send(j, shard, *inner, sems, grp=self.far_core)))
        for other in (0, 1):
            for ok, fs, way in self.at_distance(a - 1 - other):
                if way or other:
                    i = other * nz + fs
                    sems = (self.ds.at[k, i], self.dr.at[k, i])
                    shard = self.shard(other, fs, self.c)
                    core = self.send(j, shard, far, self.away, sems, grp=self.far_core)
                    todo.append((ok, core))
        return todo

    def arrivals(self, a, j, t):
        todo, nz, k, kz = [], self.nz, lax.rem(t, self.slots), lax.rem(t, 2 * self.slots)
        inner, far = (self.in_first, self.stay), (self.far_first, self.away)

        def expect(ok, shard, first, size, sem):
            ref = self.dst.at[j, shard, pl.ds(first, size)]
            todo.append((ok, pltpu.make_async_copy(ref, ref, sem)))

        for ok, fs, way in self.at_distance(a):
            if way:
                expect(ok, self.shard(0, fs, self.c), *inner, self.zr.at[kz, fs])
        for ok, fs, _ in self.at_distance(a - 1):
            expect(ok, self.shard(1, fs, self.c), *inner, self.yr.at[k, fs])
        for other in (0, 1):
            for ok, fs, way in self.at_distance(a - 1 - other):
                i = other * nz + fs
                if way or other:
                    expect(ok, self.shard(other, fs, self.c), *far, self.xr.at[k, i])
                size = inner if way or other else (0, self.rows)
                expect(ok, self.shard(other, fs, 1 - self.c), *size, self.cr.at[k, i])
            for ok, fs, way in self.at_distance(a - 2 - other):
                if way or other:
                    i = other * nz + fs
                    expect(ok, self.shard(other, fs, 1 - self.c), *far, self.dr.at[k, i])
        return todo

    def run(self, early=None, compute=None):
        lag = self.lag

        def act(ok, fn):
            if ok is None:
                fn()
            else:
                pl.when(ok)(fn)

        def finish(a, j, t):
            for ok, copy in self.sends(a - 1, j, t):
                act(ok, copy.wait_send)
            for ok, copy in self.arrivals(a, j, t):
                act(ok, copy.wait)
            if a == 1:
                for ok, copy in self.keeps(j, t):
                    act(ok, copy.wait)

        def begin(a, j, t):
            for ok, copy in self.sends(a, j, t):
                act(ok, copy.start)
            if a == 0:
                for ok, copy in self.keeps(j, t):
                    act(ok, copy.start)

        def tick(t, carry):
            for a in range(self.last, 0, -1):
                j = t - lag * a
                pl.when((j >= 0) & (j < self.count))(functools.partial(finish, a, j, t - lag))
            for a in range(self.last - 1, -1, -1):
                j = t - lag * a
                pl.when((j >= 0) & (j < self.count))(functools.partial(begin, a, j, t))
            if early is not None:
                early(t)
            if compute is not None:
                j = t - lag * self.last
                pl.when(j >= 0)(functools.partial(compute, j))
            return carry

        lax.fori_loop(0, self.count + lag * self.last + (compute is not None), tick, 0)


def head_columns(ref, rows, part, h, width):
    first = pl.multiple_of(part * width + h * HDIM, HDIM)
    return ref[rows, pl.ds(first, HDIM)]


def seen(shape, first):
    row = lax.broadcasted_iota(jnp.int32, shape, 0)
    return lax.broadcasted_iota(jnp.int32, shape, 1) <= first + row


def head_chances(qkv, kp, h, prompt_len, width, first):
    own, cont = slice(0, prompt_len), slice(prompt_len, None)
    q_p = head_columns(qkv, own, 0, h, width)
    q_c = head_columns(qkv, cont, 0, h, width)
    k_c = head_columns(qkv, cont, 1, h, width)
    v_c = head_columns(qkv, cont, 2, h, width)
    lanes = pl.ds(pl.multiple_of(h * HDIM, HDIM), HDIM)
    k_p = kp[:, :, lanes].reshape(-1, HDIM)
    lanes = pl.ds(pl.multiple_of(width + h * HDIM, HDIM), HDIM)
    v_p = kp[:, :, lanes].reshape(-1, HDIM)
    s_p = mm_nt(q_p, k_p) * SCALE
    s_p = jnp.where(seen(s_p.shape, first), s_p, NEG_FILL)
    e_p = jnp.exp(s_p - jnp.max(s_p, axis=-1, keepdims=True))
    c_p = e_p * (1.0 / jnp.sum(e_p, axis=-1, keepdims=True))
    s_1 = mm_nt(q_c, k_p) * SCALE
    s_2 = mm_nt(q_c, k_c) * SCALE
    s_2 = jnp.where(seen(s_2.shape, 0), s_2, NEG_FILL)
    peak = jnp.maximum(
        jnp.max(s_1, axis=-1, keepdims=True), jnp.max(s_2, axis=-1, keepdims=True)
    )
    e_1, e_2 = jnp.exp(s_1 - peak), jnp.exp(s_2 - peak)
    mass = jnp.sum(e_1, axis=-1, keepdims=True) + jnp.sum(e_2, axis=-1, keepdims=True)
    inv = 1.0 / mass
    return (q_p, q_c, k_p, k_c, v_p, v_c), (c_p, e_1 * inv, e_2 * inv)


def select_call(ids, tables):
    def kernel(ids, *refs):
        for src, dst in zip(refs[: len(tables)], refs[len(tables) :]):
            dst[...] = src[0]

    def spec_in(t):
        return pl.BlockSpec((1,) + t.shape[1:], lambda i, ids: (ids[i],) + (0,) * (t.ndim - 1))

    def spec_out(t):
        lead = t.ndim - 3
        return pl.BlockSpec(t.shape[1:], lambda i, ids: (0,) * lead + (i, 0))

    return pl.pallas_call(
        kernel,
        grid_spec=pltpu.PrefetchScalarGridSpec(
            num_scalar_prefetch=1,
            grid=(2,),
            in_specs=[spec_in(t) for t in tables],
            out_specs=[spec_out(t) for t in tables],
        ),
        out_shape=[
            jax.ShapeDtypeStruct(t.shape[1:-2] + (2 * RANK, t.shape[-1]), BF) for t in tables
        ],
        name="select",
    )(ids, *tables)


def columns_of(ref):
    return lambda j, first, size: ref.at[
        pl.ds(first, size), pl.ds(pl.multiple_of(j * PART, PART), PART)
    ]


def tiles_of(ref, shard_rows, parts):
    def tile(j, first, size):
        row = pl.multiple_of(lax.rem(j, parts) * shard_rows + first, 8)
        return ref.at[pl.ds(row, size), pl.ds(pl.multiple_of(j // parts * PART, PART), PART)]

    return tile


def pair_loads(blocks, first, wbuf, wsem, k):
    return [
        pltpu.make_async_copy(
            blocks.at[first + i], wbuf.at[k, :, :, pl.ds(i * PART, PART)], wsem.at[k, i]
        )
        for i in range(2)
    ]


def forward_call(x_p, x_c, cot_p, cot_c, norms, tables, weights, n_fs, n_shard):
    prompt_len, width = x_p.shape
    rows = prompt_len + x_c.shape[0]
    shard_rows, hidden = weights[3].shape
    parts = weights[2].shape[0] // shard_rows
    n_qkv, n_out, n_up = 3 * width // PART, width // PART, hidden // PART
    n_dn = n_out * parts
    before_up = n_qkv + n_out + n_dn
    count = before_up + n_up
    n_grp = n_shard // n_fs
    heads = width // HDIM
    per = width // BLOCK
    lag = 2
    t_share = n_qkv + lag * (n_fs + 2) + 1
    t_onward = t_share + 10
    t_head = t_onward + 1
    t_out = t_head + heads
    t_norm = t_out + per

    def kernel(x_p, x_c, gain_one, bias_one, gain_two, bias_two, *refs):
        (a_ext, b_ext, a_up, b_up, a_dn, b_dn), refs = refs[:6], refs[6:]
        (cot_p, cot_c), src, refs = refs[:2], refs[2:6], refs[6:]
        (dst, qkv_out, kp_out, normed_out, mixed_out), refs = refs[:5], refs[5:]
        (lows, res_p, res_c, resid_back, grad_attn, low_o), refs = refs[:6], refs[6:]
        (g_a_up, g_b_up, g_a_dn, g_b_dn), refs = refs[:4], refs[4:]
        (qkv, kp, normed_one, normed, mixed, cot, resid, out_acc), refs = refs[:8], refs[8:]
        (low_up, dlow_dn, low_dn, dlow_up, wbuf, dbuf), refs = refs[:6], refs[6:]
        (wsem, dsem, ksend, krecv, lsem), sems = refs[:5], refs[5:]
        own, rest = slice(0, prompt_len), slice(prompt_len, None)
        sources = [
            (n_qkv, columns_of(src[0])),
            (n_out, columns_of(src[1])),
            (n_dn, tiles_of(src[2], shard_rows, parts)),
            (n_up, columns_of(src[3])),
        ]
        engine = Gather(n_fs, sources, dst, sems, lag)
        engine.barrier()
        grp = lax.axis_index("grp")
        loads = [
            pltpu.make_async_copy(cot_p, cot.at[pl.ds(0, prompt_len)], lsem.at[0]),
            pltpu.make_async_copy(cot_c, cot.at[pl.ds(prompt_len, rows - prompt_len)], lsem.at[1]),
        ]
        stores = [
            pltpu.make_async_copy(qkv, qkv_out, lsem.at[2]),
            pltpu.make_async_copy(kp, kp_out, lsem.at[3]),
            pltpu.make_async_copy(normed_one, normed_out, lsem.at[4]),
            pltpu.make_async_copy(mixed, mixed_out, lsem.at[5]),
        ]

        def pass_on(n, whose, to):
            return pltpu.make_async_remote_copy(
                kp.at[whose],
                kp.at[whose],
                ksend.at[n],
                krecv.at[n],
                device_id={"grp": to},
                device_id_type=MESH,
            )

        def landed(n, whose):
            return pltpu.make_async_copy(kp.at[whose], kp.at[whose], krecv.at[n])

        to_row = pass_on(0, grp, engine.far_row)
        to_core = pass_on(1, grp, engine.far_core)
        onward = pass_on(2, engine.far_row, engine.far_core)
        diagonal = (1 - engine.y) * 2 + 1 - engine.c

        def early(t):
            @pl.when(t == 0)
            def _():
                for copy in loads:
                    copy.start()
                for x, part in ((x_p, own), (x_c, rest)):
                    hat, _ = norm_stats(x[...].astype(F32))
                    normed_one[part] = (hat * gain_one[...] + bias_one[...]).astype(BF)
                for n in range(3):
                    lows[n] = low_of(mm_nt(normed_one[...], a_ext[n]), prompt_len)
                for copy in loads:
                    copy.wait()
                dlow_dn[...] = low_of(mm_nt(cot[...], b_dn[...]), prompt_len)

            @pl.when(t == t_share)
            def _():
                kp[grp] = qkv[:prompt_len, width:]
                to_row.start()
                to_core.start()
                stores[0].start()
                stores[2].start()

            @pl.when(t == t_onward)
            def _():
                landed(0, engine.far_row).wait()
                onward.start()

            @pl.when(t == t_head)
            def _():
                landed(1, engine.far_core).wait()
                landed(2, diagonal).wait()
                to_row.wait_send()
                to_core.wait_send()
                onward.wait_send()
                stores[1].start()

            @pl.when((t >= t_head) & (t < t_out))
            def _():
                h = t - t_head
                (_, _, _, _, v_p, v_c), (c_p, c_1, c_2) = head_chances(
                    qkv, kp, h, prompt_len, width, grp * prompt_len
                )
                lanes = pl.ds(pl.multiple_of(h * HDIM, HDIM), HDIM)
                mixed[own, lanes] = mm(c_p.astype(BF), v_p).astype(BF)
                mixed[rest, lanes] = (mm(c_1.astype(BF), v_p) + mm(c_2.astype(BF), v_c)).astype(BF)

            def load_out(b):
                return pair_loads(dst, n_qkv + 2 * b, wbuf, wsem, lax.rem(b, 2))

            @pl.when(t == t_out - 1)
            def _():
                for copy in load_out(0):
                    copy.start()

            @pl.when((t >= t_out) & (t < t_norm))
            def _():
                b = t - t_out

                @pl.when(b == 0)
                def _():
                    stores[3].start()
                    low_o[...] = low_of(mm_nt(mixed[...], a_ext[3]), prompt_len)

                for copy in load_out(b):
                    copy.wait()

                @pl.when(b + 1 < per)
                def _():
                    for copy in load_out(b + 1):
                        copy.start()

                cols = pl.ds(pl.multiple_of(b * BLOCK, BLOCK), BLOCK)
                w = wbuf[lax.rem(b, 2)].reshape(-1, BLOCK)
                branch = mm(mixed[...], w) + mm(low_o[...], b_ext[3, :, cols])
                resid[own, cols] = x_p[:, cols].astype(F32) + branch[own]
                resid[rest, cols] = x_c[:, cols].astype(F32) + branch[rest]

            @pl.when(t == t_norm)
            def _():
                hat, _ = norm_stats(resid[...])
                normed[...] = (hat * gain_two[...] + bias_two[...]).astype(BF)
                low_up[...] = low_of(mm_nt(normed[...], a_up[...]), prompt_len)
                out_acc[...] = resid[...]
                resid_back[...] = jnp.zeros_like(resid_back)
                low_dn[...] = jnp.zeros_like(low_dn)
                dlow_up[...] = jnp.zeros_like(dlow_up)

        def load(j):
            k, i = lax.rem(j // 2, 2), lax.rem(j, 2)
            into = wbuf.at[k, :, :, pl.ds(pl.multiple_of(i * PART, PART), PART)]
            return pltpu.make_async_copy(dst.at[j], into, wsem.at[k, i])

        def load_down(n):
            k = lax.rem(n, 2)
            return [
                pltpu.make_async_copy(
                    dst.at[pl.ds(n_qkv + n_out + b * parts, parts), n],
                    dbuf.at[k, :, :, pl.ds(b * PART, PART)],
                    dsem.at[k, b],
                )
                for b in range(n_out)
            ]

        def compute(j):
            n = j - before_up

            @pl.when((j < n_qkv) | ((n >= 0) & (n < n_up)))
            def _():
                load(j).start()

            @pl.when((n >= 0) & (n < n_up) & (lax.rem(j, 2) == 0))
            def _():
                for copy in load_down(n // 2):
                    copy.start()

            @pl.when((j > 0) & (j <= n_qkv) & (lax.rem(j, 2) == 0))
            def _():
                i = j // 2 - 1
                for first in (j - 2, j - 1):
                    load(first).wait()
                w = wbuf[lax.rem(i, 2)].reshape(-1, BLOCK)
                m = i // per
                inside = pl.ds(pl.multiple_of(lax.rem(i, per) * BLOCK, BLOCK), BLOCK)
                cols = pl.ds(pl.multiple_of(i * BLOCK, BLOCK), BLOCK)
                extra = mm(lows[m], b_ext[m, :, inside])
                qkv[:, cols] = (mm(normed_one[...], w) + extra).astype(BF)

            @pl.when((n > 0) & (lax.rem(j, 2) == 0))
            def _():
                i = n // 2 - 1
                for first in (j - 2, j - 1):
                    load(first).wait()
                for copy in load_down(i):
                    copy.wait()
                cols = pl.ds(pl.multiple_of(i * BLOCK, BLOCK), BLOCK)
                w_up = wbuf[lax.rem(j // 2 - 1, 2)].reshape(-1, BLOCK)
                w_dn = dbuf[lax.rem(i, 2)].reshape(BLOCK, width)
                a_d, b_u = a_dn[:, cols], b_up[:, cols]
                pre = mm(normed[...], w_up) + mm(low_up[...], b_u)
                cdf = 0.5 * (1.0 + lax.erf(pre * math.sqrt(0.5)))
                act = (pre * cdf).astype(BF)
                slope = cdf + pre * jnp.exp(-0.5 * pre * pre) * (1.0 / math.sqrt(2.0 * math.pi))
                grad_act = mm_nt(cot[...], w_dn) + mm(dlow_dn[...], a_d)
                grad_pre = (grad_act * slope).astype(BF)
                out_acc[...] += mm(act, w_dn)
                resid_back[...] += mm_nt(grad_pre, w_up)
                low_dn[...] += mm_nt(act, a_d)
                dlow_up[...] += mm_nt(grad_pre, b_u)
                g_b_up[:, cols] = mm_tn(low_up[...], grad_pre).astype(BF)
                g_a_dn[:, cols] = mm_tn(dlow_dn[...], act).astype(BF)

        engine.run(early, compute)
        dlow = low_of(dlow_up[...], prompt_len)
        g_a_up[...] = mm_tn(dlow, normed[...]).astype(BF)
        grad = resid_back[...] + mm(dlow, a_up[...])
        grad = cot[...].astype(F32) + norm_back(resid[...], gain_two[...], grad)
        resid_back[...] = grad
        grad_attn[...] = grad.astype(BF)
        low = low_of(low_dn[...], prompt_len)
        result = (out_acc[...] + mm(low, b_dn[...])).astype(BF)
        res_p[...] = result[own]
        res_c[...] = result[rest]
        g_b_dn[...] = mm_tn(low, cot[...]).astype(BF)
        for copy in stores:
            copy.wait()

    like = jax.ShapeDtypeStruct
    two = 2 * RANK
    dma = pltpu.SemaphoreType.DMA
    share = (n_grp, prompt_len, 2 * width)
    return pl.pallas_call(
        kernel,
        out_shape=[
            like((count, n_shard, shard_rows, PART), BF),
            like((rows, 3 * width), BF),
            like(share, BF),
            like((rows, width), BF),
            like((rows, width), BF),
            like((3, rows, two), BF),
            like(x_p.shape, BF),
            like(x_c.shape, BF),
            like((rows, width), F32),
            like((rows, width), BF),
            like((rows, two), BF),
            like((two, width), BF),
            like((two, hidden), BF),
            like((two, hidden), BF),
            like((two, width), BF),
        ],
        in_specs=[WHOLE] * 12 + [ANY] * 6,
        out_specs=[ANY] * 5 + [WHOLE] * 10,
        scratch_shapes=[
            pltpu.VMEM((rows, 3 * width), BF),
            pltpu.VMEM(share, BF),
            pltpu.VMEM((rows, width), BF),
            pltpu.VMEM((rows, width), BF),
            pltpu.VMEM((rows, width), BF),
            pltpu.VMEM((rows, width), BF),
            pltpu.VMEM((rows, width), F32),
            pltpu.VMEM((rows, width), F32),
            pltpu.VMEM((rows, two), BF),
            pltpu.VMEM((rows, two), BF),
            pltpu.VMEM((rows, two), F32),
            pltpu.VMEM((rows, two), F32),
            pltpu.VMEM((2, n_shard, shard_rows, BLOCK), BF),
            pltpu.VMEM((2, parts, shard_rows, width), BF),
            dma((2, 2)),
            dma((2, n_out)),
            dma((3,)),
            dma((3,)),
            dma((6,)),
        ]
        + Gather.semaphores(n_fs, lag),
        compiler_params=pltpu.CompilerParams(
            collective_id=0, has_side_effects=True, vmem_limit_bytes=ROOM
        ),
        name="forward",
    )(x_p, x_c, *norms, *tables, cot_p, cot_c, *weights)


PIECES = 8


class TableSum:
    def __init__(self, n_fs, hots, units, bufs, sems, stepwise):
        self.n_fs, self.hots, self.units, self.stepwise = n_fs, hots, units, stepwise
        self.out, self.got, self.dense, self.parts, self.sums = bufs
        (self.s1, self.r1, self.s2, self.r2, self.s3, self.r3) = sems
        rep, self.grp = lax.axis_index("rep"), lax.axis_index("grp")
        self.z = lax.axis_index("fs")
        plane = rep % 2
        y, c = self.grp // 2, self.grp % 2
        self.me = plane * 4 + self.grp
        self.peers = []
        for q in range(1, PIECES):
            x_to = 1 - plane if q // 4 else plane
            y_to = 1 - y if q // 2 % 2 else y
            c_to = 1 - c if q % 2 else c
            where = {"grp": y_to * 2 + c_to}
            if q // 4:
                where["rep"] = rep + 1 - 2 * plane
            self.peers.append((q, x_to * 4 + y_to * 2 + c_to, where))
        self.piece = self.out.shape[2] // units

    @staticmethod
    def scratch(n_fs, units, piece, count):
        two, wide = 2 * RANK, units * piece
        rows = count * RANK // n_fs
        bufs = [
            pltpu.VMEM((PIECES, two, wide), BF),
            pltpu.VMEM((PIECES, two, wide), BF),
            pltpu.VMEM((n_fs, rows, wide), BF),
            pltpu.VMEM((n_fs, rows, wide), BF),
            pltpu.VMEM((PIECES, rows, wide), BF),
        ]
        dma = pltpu.SemaphoreType.DMA
        return bufs, [dma((PIECES,))] * 2 + [dma((n_fs,))] * 2 + [dma((PIECES,))] * 2

    def pack(self, unit, value, first=0):
        value = value.astype(BF)
        cols = slice(unit * self.piece, (unit + 1) * self.piece)
        for n in range(value.shape[1] // self.piece):
            self.out[first + n, :, cols] = value[:, n * self.piece : (n + 1) * self.piece]

    def exchange(self):
        return [
            pltpu.make_async_remote_copy(
                self.out.at[to],
                self.got.at[self.me],
                self.s1.at[q],
                self.r1.at[q],
                device_id=where,
                device_id_type=MESH,
            )
            for q, to, where in self.peers
        ]

    def along_fs(self):
        copies = []
        for d in range(1, self.n_fs):
            to = lax.rem(self.z + d, self.n_fs)
            copies.append(
                pltpu.make_async_remote_copy(
                    self.dense.at[to],
                    self.parts.at[self.z],
                    self.s2.at[d],
                    self.r2.at[d],
                    device_id={"fs": to},
                    device_id_type=MESH,
                )
            )
        return copies

    def hand(self, n, whose, q):
        return pltpu.make_async_remote_copy(
            self.sums.at[whose],
            self.sums.at[whose],
            self.s3.at[n],
            self.r3.at[n],
            device_id=self.peers[q - 1][2],
            device_id_type=MESH,
        )

    def hand_out(self):
        return [self.hand(q, self.me, q) for q, _, _ in self.peers]

    def relay(self, stage):
        far_row, far_rep, both = (self.peers[q - 1][1] for q in (2, 4, 6))
        steps = [
            [(4, self.me, 4), (2, self.me, 2), (1, self.me, 1)],
            [(6, far_rep, 2), (5, far_rep, 1), (3, far_row, 1)],
            [(7, both, 1)],
        ]
        return [self.hand(*step) for step in steps[stage]]

    def arrived(self, q):
        ref = self.sums.at[self.peers[q - 1][1]]
        pltpu.make_async_copy(ref, ref, self.r3.at[q]).wait()

    def first(self):
        for copy in self.exchange():
            copy.start()
        self.got[self.me] = self.out[self.me]

    def second(self):
        for q, whose, _ in self.peers:
            ref = self.got.at[whose]
            pltpu.make_async_copy(ref, ref, self.r1.at[q]).wait()
        for copy in self.exchange():
            copy.wait_send()
        wide = self.out.shape[2]
        hots = self.hots[...].reshape(PIECES * 2 * RANK, -1)
        dense = mm_tn(hots, self.got[...].reshape(PIECES * 2 * RANK, wide))
        self.dense[...] = dense.astype(BF).reshape(self.dense.shape)
        for copy in self.along_fs():
            copy.start()
        self.parts[self.z] = self.dense[self.z]

    def third(self):
        for d in range(1, self.n_fs):
            ref = self.parts.at[lax.rem(self.z + self.n_fs - d, self.n_fs)]
            pltpu.make_async_copy(ref, ref, self.r2.at[d]).wait()
        for copy in self.along_fs():
            copy.wait_send()
        total = self.parts[0].astype(F32)
        for n in range(1, self.n_fs):
            total = total + self.parts[n].astype(F32)
        self.sums[self.me] = total.astype(BF)
        if not self.stepwise:
            for copy in self.hand_out():
                copy.start()
            return
        for copy in self.relay(0):
            copy.start()

    def fourth(self):
        self.arrived(4)
        self.arrived(2)
        for copy in self.relay(1):
            copy.start()

    def fifth(self):
        self.arrived(6)
        for copy in self.relay(2):
            copy.start()

    def last(self, places):
        if self.stepwise:
            for q in (1, 3, 5, 7):
                self.arrived(q)
            sent = self.relay(0) + self.relay(1) + self.relay(2)
        else:
            for q, _, _ in self.peers:
                self.arrived(q)
            sent = self.hand_out()
        for copy in sent:
            copy.wait_send()
        for unit, place in enumerate(places):
            for k in range(PIECES):
                cols = slice(unit * self.piece, (unit + 1) * self.piece)
                for a in range(self.sums.shape[1] // RANK):
                    value = self.sums[k, a * RANK : (a + 1) * RANK, cols]
                    place(a, k * self.piece, value)


def back_call(
    grad_attn, mixed, low_o, lows, gain, a_ext, b_ext, hot, mid, qkv, kp, x_p, x_c, normed, grad_resid, w_all, n_fs, count
):
    rows, width = grad_attn.shape
    prompt_len, cont_len = x_p.shape[0], x_c.shape[0]
    heads = width // HDIM
    n_grp = kp.shape[0]
    n_shard, shard_rows = w_all.shape[1:3]
    per = width // BLOCK
    n_qkv = 3 * per
    hidden = mid[1].shape[1]
    adapters = count // n_fs
    groups = 4
    group_heads = heads // groups
    half = group_heads * HDIM
    two = 2 * RANK
    wide_units = hidden // width
    first_units = 2 * wide_units + 4
    last_units = 6
    piece = width // PIECES

    def kernel(*refs):
        (grad_attn, mixed, low_o, lows, gain, a_ext, b_ext, hot), refs = refs[:8], refs[8:]
        (g_a_up, g_b_up, g_a_dn, g_b_dn), refs = refs[:4], refs[4:]
        (qkv, kp, x_p, x_c, normed, grad_resid, w_all), refs = refs[:7], refs[7:]
        (out_p, out_c, t_a, t_b, t_a_up, t_b_up, t_a_dn, t_b_dn), refs = refs[:8], refs[8:]
        (grads, keep, late, x, normed_here, wbuf, gm, acc, dlow, dlow_o), refs = refs[:10], refs[10:]
        (far, far_core, far_row, hots), refs = refs[:4], refs[4:]
        bufs_one, bufs_two, refs = refs[:5], refs[5:10], refs[10:]
        sems_one, sems_two, refs = refs[:6], refs[6:12], refs[12:]
        lsem, wsem, csend, crecv, rsend, rrecv, hsend, hrecv = refs
        grp = lax.axis_index("grp")
        y, c = grp // 2, grp % 2
        own, rest = slice(0, prompt_len), slice(prompt_len, None)
        one = TableSum(n_fs, hots, first_units, bufs_one, sems_one, True)
        two_ = TableSum(n_fs, hots, last_units, bufs_two, sems_two, False)
        barrier = pltpu.get_barrier_semaphore()
        for _, _, where in one.peers:
            pl.semaphore_signal(barrier, 1, device_id=where, device_id_type=MESH)
        for d in range(1, n_fs):
            to = lax.rem(one.z + d, n_fs)
            pl.semaphore_signal(barrier, 1, device_id={"fs": to}, device_id_type=MESH)

        loads = [
            pltpu.make_async_copy(src, dst, lsem.at[n])
            for n, (src, dst) in enumerate(
                [
                    (qkv, grads),
                    (kp, keep),
                    (grad_resid, late),
                    (normed, normed_here),
                    (x_p, x.at[pl.ds(0, prompt_len)]),
                    (x_c, x.at[pl.ds(prompt_len, cont_len)]),
                ]
            )
        ]
        for copy in loads:
            copy.start()

        def load_w(i, k):
            for copy in pair_loads(w_all, 2 * i, wbuf, wsem, k):
                copy.start()

        def wait_w(i, k):
            for copy in pair_loads(w_all, 2 * i, wbuf, wsem, k):
                copy.wait()

        load_w(n_qkv, 0)
        pl.semaphore_wait(barrier, len(one.peers) + n_fs - 1)

        hots[one.me] = hot[...]
        hot_sends = [
            pltpu.make_async_remote_copy(
                hots.at[one.me],
                hots.at[one.me],
                hsend.at[q],
                hrecv.at[q],
                device_id=where,
                device_id_type=MESH,
            )
            for q, _, where in one.peers
        ]
        for copy in hot_sends:
            copy.start()
        for n in range(wide_units):
            one.pack(n, g_b_up[:, n * width : (n + 1) * width])
            one.pack(wide_units + n, g_a_dn[:, n * width : (n + 1) * width])
        one.pack(2 * wide_units, g_a_up[...])
        one.pack(2 * wide_units + 1, g_b_dn[...])
        dlow_o[...] = low_of(mm_nt(grad_attn[...], b_ext[3]), prompt_len)
        one.pack(2 * wide_units + 2, mm_tn(dlow_o[...], mixed[...]))
        one.pack(2 * wide_units + 3, mm_tn(low_o[...], grad_attn[...]))
        one.first()

        acc[...] = mm(dlow_o[...], a_ext[3])
        for n in range(per):
            wait_w(n_qkv + n, n % 2)
            if n + 1 < per:
                load_w(n_qkv + n + 1, (n + 1) % 2)
            w = wbuf[n % 2].reshape(-1, BLOCK)
            acc[...] += mm_nt(grad_attn[:, n * BLOCK : (n + 1) * BLOCK], w)
        gm[...] = acc[...].astype(BF)
        load_w(0, 0)
        load_w(1, 1)

        loads[0].wait()
        loads[1].wait()

        def head(part, n, carry):
            h = part * group_heads + n
            first = grp * prompt_len
            (q_p, q_c, k_p, k_c, v_p, v_c), (c_p, c_1, c_2) = head_chances(
                grads, keep, h, prompt_len, width, first
            )
            lanes = [
                pl.ds(pl.multiple_of(i * width + h * HDIM, HDIM), HDIM) for i in range(3)
            ]
            gm_p, gm_c = gm[own, lanes[0]], gm[rest, lanes[0]]
            d_p = mm_nt(gm_p, v_p)
            d_1, d_2 = mm_nt(gm_c, v_p), mm_nt(gm_c, v_c)
            s_p = (c_p * (d_p - jnp.sum(c_p * d_p, axis=-1, keepdims=True))).astype(BF)
            inner = jnp.sum(c_1 * d_1, axis=-1, keepdims=True) + jnp.sum(
                c_2 * d_2, axis=-1, keepdims=True
            )
            s_1 = (c_1 * (d_1 - inner)).astype(BF)
            s_2 = (c_2 * (d_2 - inner)).astype(BF)
            grads[own, lanes[0]] = (mm(s_p, k_p) * SCALE).astype(BF)
            grads[rest, lanes[0]] = ((mm(s_1, k_p) + mm(s_2, k_c)) * SCALE).astype(BF)
            grads[rest, lanes[1]] = (mm_tn(s_2, q_c) * SCALE).astype(BF)
            grads[rest, lanes[2]] = mm_tn(c_2.astype(BF), gm_c).astype(BF)
            g_k = ((mm_tn(s_p, q_p) + mm_tn(s_1, q_c)) * SCALE).astype(BF)
            g_v = (mm_tn(c_p.astype(BF), gm_p) + mm_tn(c_1.astype(BF), gm_c)).astype(BF)
            into = [pl.ds(pl.multiple_of(i * half + n * HDIM, HDIM), HDIM) for i in range(2)]
            far[part, :, :, into[0]] = g_k.reshape(n_grp, prompt_len, HDIM)
            far[part, :, :, into[1]] = g_v.reshape(n_grp, prompt_len, HDIM)
            return carry

        def to_core(part):
            return [
                pltpu.make_async_remote_copy(
                    far.at[part, row * 2 + 1 - c],
                    far_core.at[part, row],
                    csend.at[part, row],
                    crecv.at[part, row],
                    device_id={"grp": y * 2 + 1 - c},
                    device_id_type=MESH,
                )
                for row in range(2)
            ]

        def to_row(part):
            return pltpu.make_async_remote_copy(
                far.at[part, (1 - y) * 2 + c],
                far_row.at[part],
                rsend.at[part],
                rrecv.at[part],
                device_id={"grp": (1 - y) * 2 + c},
                device_id_type=MESH,
            )

        def add_core(part):
            for copy in to_core(part):
                copy.wait()
            for row in range(2):
                total = far[part, row * 2 + c].astype(F32) + far_core[part, row].astype(F32)
                far[part, row * 2 + c] = total.astype(BF)
            to_row(part).start()

        def add_row(part):
            to_row(part).wait()
            total = far[part, grp].astype(F32) + far_row[part].astype(F32)
            total = total.astype(BF)
            for i in range(2):
                cols = slice((i + 1) * width + part * half, (i + 1) * width + (part + 1) * half)
                grads[own, cols] = total[:, i * half : (i + 1) * half]

        def half_group(i, carry):
            part = i // 2

            @pl.when((lax.rem(i, 2) == 1) & (part > 0))
            def _():
                add_core(part - 1)

            first = lax.rem(i, 2) * (group_heads // 2)
            lax.fori_loop(first, first + group_heads // 2, functools.partial(head, part), 0)

            @pl.when(lax.rem(i, 2) == 1)
            def _():
                for copy in to_core(part):
                    copy.start()

            @pl.when(i == groups + 1)
            def _():
                for copy in hot_sends:
                    copy.wait_send()
                for q, whose, _ in one.peers:
                    pltpu.make_async_copy(hots.at[whose], hots.at[whose], hrecv.at[q]).wait()
                one.second()

            return carry

        lax.fori_loop(0, 2 * groups, half_group, 0)

        def tables(i):
            part = grads[:, i * width : (i + 1) * width]
            low = low_of(mm_nt(part, b_ext[i]), prompt_len)
            two_.pack(i, mm_tn(low, normed_here[...]))
            two_.pack(3 + i, mm_tn(lows[i], part))
            dlow[i] = low

        def project(n, carry):
            k = lax.rem(n, 2)
            wait_w(n, k)
            part = grads[:, pl.ds(pl.multiple_of(n * BLOCK, BLOCK), BLOCK)]
            acc[...] += mm_nt(part, wbuf[k].reshape(-1, BLOCK))

            @pl.when(n + 2 < n_qkv)
            def _():
                load_w(n + 2, k)

            return carry

        loads[3].wait()
        tables(0)
        add_core(groups - 1)
        acc[...] = mm(dlow[0], a_ext[0])
        lax.fori_loop(0, per, project, 0)
        for part in range(groups):
            add_row(part)
        tables(1)
        tables(2)
        two_.first()
        one.third()
        acc[...] += mm(dlow[1], a_ext[1]) + mm(dlow[2], a_ext[2])

        def project_more(n, carry):
            pl.when(n == 2 * per)(one.fourth)
            return project(n, carry)

        lax.fori_loop(per, n_qkv, project_more, 0)
        two_.second()
        one.fifth()
        for copy in (loads[2], loads[4], loads[5]):
            copy.wait()
        back = late[...] + norm_back(x[...].astype(F32), gain[...], acc[...])
        back = back.astype(BF)
        out_p[...] = back[own]
        out_c[...] = back[rest]

        def whole(ref, first):
            def place(a, col, value):
                ref[a, :, first + col : first + col + piece] = value

            return place

        def one_map(ref, n):
            def place(a, col, value):
                ref[a, n, :, col : col + piece] = value

            return place

        one.last(
            [whole(t_b_up, n * width) for n in range(wide_units)]
            + [whole(t_a_dn, n * width) for n in range(wide_units)]
            + [whole(t_a_up, 0), whole(t_b_dn, 0), one_map(t_a, 3), one_map(t_b, 3)]
        )
        two_.third()
        two_.last([one_map(t_a, n) for n in range(3)] + [one_map(t_b, n) for n in range(3)])

    like = jax.ShapeDtypeStruct
    bufs_one, sems_one = TableSum.scratch(n_fs, first_units, piece, count)
    bufs_two, sems_two = TableSum.scratch(n_fs, last_units, piece, count)
    dma = pltpu.SemaphoreType.DMA
    return pl.pallas_call(
        kernel,
        out_shape=[
            like(x_p.shape, BF),
            like(x_c.shape, BF),
            like((adapters, 4, RANK, width), BF),
            like((adapters, 4, RANK, width), BF),
            like((adapters, RANK, width), BF),
            like((adapters, RANK, hidden), BF),
            like((adapters, RANK, hidden), BF),
            like((adapters, RANK, width), BF),
        ],
        in_specs=[WHOLE] * 12 + [ANY] * 7,
        out_specs=[WHOLE] * 8,
        scratch_shapes=[
            pltpu.VMEM((rows, 3 * width), BF),
            pltpu.VMEM(kp.shape, BF),
            pltpu.VMEM((rows, width), F32),
            pltpu.VMEM((rows, width), BF),
            pltpu.VMEM((rows, width), BF),
            pltpu.VMEM((2, n_shard, shard_rows, BLOCK), BF),
            pltpu.VMEM((rows, width), BF),
            pltpu.VMEM((rows, width), F32),
            pltpu.VMEM((3, rows, two), BF),
            pltpu.VMEM((rows, two), BF),
            pltpu.VMEM((groups, n_grp, prompt_len, 2 * half), BF),
            pltpu.VMEM((groups, 2, prompt_len, 2 * half), BF),
            pltpu.VMEM((groups, prompt_len, 2 * half), BF),
            pltpu.VMEM((PIECES,) + hot.shape, BF),
        ]
        + bufs_one
        + bufs_two
        + sems_one
        + sems_two
        + [dma((6,)), dma((2, 2)), dma((groups, 2)), dma((groups, 2)), dma((groups,)), dma((groups,))]
        + [dma((PIECES,)), dma((PIECES,))],
        compiler_params=pltpu.CompilerParams(
            collective_id=2, has_side_effects=True, vmem_limit_bytes=ROOM
        ),
        name="back",
    )(
        grad_attn, mixed, low_o, lows, gain, a_ext, b_ext, hot, *mid,
        qkv, kp, x_p, x_c, normed, grad_resid, w_all,
    )


def make_body(sizes):
    n_rep, n_grp, n_fs = sizes
    n_shard = n_grp * n_fs

    def other_pairs(v):
        step = 2
        while step < n_rep:
            far = lax.ppermute(v, "rep", [(i, i ^ step) for i in range(n_rep)])
            v = (v.astype(F32) + far.astype(F32)).astype(BF)
            step *= 2
        return v.astype(F32)

    def body(
        prompt_input_rows,
        continuation_input,
        prompt_group_adapter,
        continuation_adapter,
        first_norm_scale,
        first_norm_bias,
        second_norm_scale,
        second_norm_bias,
        frozen_query_key_value,
        frozen_output_weight,
        frozen_up_weight,
        frozen_down_weight,
        adapter_attention_input,
        adapter_attention_output,
        adapter_up_input,
        adapter_up_output,
        adapter_down_input,
        adapter_down_output,
        prompt_cotangent,
        continuation_cotangent,
    ):
        prompt_len, width = prompt_input_rows.shape[2:]
        count = adapter_up_input.shape[0]
        hidden = frozen_up_weight.shape[1]
        shard_rows = frozen_query_key_value.shape[0]
        assert n_grp == 4 and hidden == n_shard * BLOCK
        assert frozen_down_weight.shape[0] == BLOCK and BLOCK % shard_rows == 0

        def flat(v):
            return v.reshape(v.shape[-2:])

        x_p, x_c = flat(prompt_input_rows), flat(continuation_input)
        cot_p, cot_c = flat(prompt_cotangent), flat(continuation_cotangent)
        ids = jnp.concatenate([prompt_group_adapter.reshape(1), continuation_adapter.reshape(1)])
        a_ext, b_ext, a_up, b_up, a_dn, b_dn = select_call(
            ids,
            [
                adapter_attention_input.swapaxes(2, 3),
                adapter_attention_output,
                adapter_up_input.swapaxes(1, 2),
                adapter_up_output,
                adapter_down_input.swapaxes(1, 2),
                adapter_down_output,
            ],
        )
        place = jnp.repeat(ids, RANK) * RANK + jnp.arange(2 * RANK) % RANK
        hot = (place[:, None] == jnp.arange(count * RANK)[None, :]).astype(BF)
        norms = [
            v[None, :]
            for v in (first_norm_scale, first_norm_bias, second_norm_scale, second_norm_bias)
        ]
        (
            w_all,
            qkv,
            kp,
            normed_one,
            mixed,
            lows,
            res_p,
            res_c,
            grad_resid,
            grad_attn,
            low_o,
            *mid,
        ) = forward_call(
            x_p,
            x_c,
            cot_p,
            cot_c,
            norms,
            (a_ext, b_ext, a_up, b_up, a_dn, b_dn),
            (frozen_query_key_value, frozen_output_weight, frozen_down_weight, frozen_up_weight),
            n_fs,
            n_shard,
        )
        grad_p, grad_c, t_a, t_b, t_a_up, t_b_up, t_a_dn, t_b_dn = back_call(
            grad_attn,
            mixed,
            low_o,
            lows,
            norms[0],
            a_ext,
            b_ext,
            hot,
            mid,
            qkv,
            kp,
            x_p,
            x_c,
            normed_one,
            grad_resid,
            w_all,
            n_fs,
            count,
        )
        return (
            res_p.reshape(prompt_input_rows.shape),
            res_c.reshape(continuation_input.shape),
            grad_p.reshape(prompt_input_rows.shape),
            grad_c.reshape(continuation_input.shape),
            other_pairs(t_a).swapaxes(2, 3),
            other_pairs(t_b),
            other_pairs(t_a_up).swapaxes(1, 2),
            other_pairs(t_b_up),
            other_pairs(t_a_dn).swapaxes(1, 2),
            other_pairs(t_b_dn),
        )

    return body


def solution(mesh):
    sizes = (mesh.shape["rep"], mesh.shape["grp"], mesh.shape["fs"])
    rows_in = P("rep", "fs", "grp", None)
    conts_in = P("rep", "fs", "grp", None, None)
    weight = P(("grp", "fs"), None)
    return jax.shard_map(
        make_body(sizes),
        mesh=mesh,
        in_specs=(
            rows_in,
            conts_in,
            P("rep", "fs"),
            P("rep", "fs", "grp"),
            P(),
            P(),
            P(),
            P(),
            weight,
            weight,
            weight,
            weight,
            P(),
            P(),
            P(),
            P(),
            P(),
            P(),
            rows_in,
            conts_in,
        ),
        out_specs=(
            rows_in,
            conts_in,
            rows_in,
            conts_in,
            P("fs", None, None, None),
            P("fs", None, None, None),
            P("fs", None, None),
            P("fs", None, None),
            P("fs", None, None),
            P("fs", None, None),
        ),
        check_vma=False,
    )
```

```python
import functools
import math

import jax
import jax.numpy as jnp
from jax import lax
from jax.experimental import pallas as pl
from jax.experimental.pallas import tpu as pltpu
from jax.sharding import PartitionSpec as P

HDIM = 128
RANK = 16
BLOCK = 512
PART = 256
AWAY = (40, 48)
ALONG = 40
SCALE = HDIM ** (-0.5)
NEG_FILL = -1e30
BF = jnp.bfloat16
F32 = jnp.float32
MESH = pl.DeviceIdType.MESH
ANY = pl.BlockSpec(memory_space=pl.ANY)
WHOLE = pl.BlockSpec(memory_space=pltpu.VMEM)
ROOM = 62 * 2**20


def mm(a, b):
    return jnp.dot(a, b, preferred_element_type=F32)


def mm_nt(a, b):
    return lax.dot_general(a, b, (((1,), (1,)), ((), ())), preferred_element_type=F32)


def mm_tn(a, b):
    return lax.dot_general(a, b, (((0,), (0,)), ((), ())), preferred_element_type=F32)


def norm_stats(values):
    center = values - jnp.mean(values, axis=-1, keepdims=True)
    spread = jnp.mean(center * center, axis=-1, keepdims=True)
    rstd = lax.rsqrt(spread + 1e-05)
    return center * rstd, rstd


def norm_back(values, gain, grad):
    hat, rstd = norm_stats(values)
    e = grad * gain
    return (
        e - jnp.mean(e, axis=-1, keepdims=True) - hat * jnp.mean(e * hat, axis=-1, keepdims=True)
    ) * rstd


def low_of(product, prompt_len):
    row = lax.broadcasted_iota(jnp.int32, product.shape, 0)
    col = lax.broadcasted_iota(jnp.int32, product.shape, 1)
    return jnp.where((row < prompt_len) == (col < RANK), product, 0.0).astype(BF)


class Gather:
    def __init__(self, n_fs, sources, dst, sems, lag=2):
        (self.zs, self.zr, self.ws, self.wr, self.ys, self.yr, self.xs, self.xr) = sems[:8]
        (self.cs, self.cr, self.ds, self.dr, self.loc) = sems[8:]
        self.nz, self.sources, self.dst = n_fs, sources, dst
        self.count, self.rows = dst.shape[0], dst.shape[2]
        self.lag, self.slots, self.last = lag, 2 * lag, n_fs + 2
        rep, grp = lax.axis_index("rep"), lax.axis_index("grp")
        self.z = lax.axis_index("fs")
        self.y, self.c, plane = grp // 2, grp % 2, rep % 2
        self.far_rep = rep + 1 - 2 * plane
        self.far_core = self.y * 2 + 1 - self.c
        self.far_row = (1 - self.y) * 2 + self.c
        self.own = grp * n_fs + self.z
        self.inner, self.outer, self.far = [], [], []
        for away in AWAY:
            stay = self.rows - away
            self.inner.append((pl.multiple_of(away * plane, 8), stay))
            self.outer.append((pl.multiple_of(stay * plane, 8), away))
            self.far.append((pl.multiple_of(stay * (1 - plane), 8), away))
        first, stay = self.inner[1]
        self.near = (first, stay - ALONG)
        self.along = (pl.multiple_of(first + stay - ALONG, 8), ALONG)

    @staticmethod
    def semaphores(n_fs, lag=2):
        slots, dma = 2 * lag, pltpu.SemaphoreType.DMA
        return (
            [dma((3 * slots, 2, n_fs)), dma((3 * slots, n_fs))]
            + [dma((3 * slots, n_fs))] * 2
            + [dma((slots, n_fs))] * 2
            + [dma((slots, 2 * n_fs))] * 6
            + [dma((slots,))]
        )

    def barrier(self):
        sem = pltpu.get_barrier_semaphore()

        def greet(**where):
            pl.semaphore_signal(sem, 1, device_id=where, device_id_type=MESH)

        greet(rep=self.far_rep)
        greet(grp=self.far_core)
        greet(grp=self.far_row)
        below, above = self.z > 0, self.z < self.nz - 1
        pl.when(below)(lambda: greet(fs=self.z - 1))
        pl.when(above)(lambda: greet(fs=self.z + 1))
        pl.semaphore_wait(sem, 3 + below.astype(jnp.int32) + above.astype(jnp.int32))

    def at_distance(self, d):
        if d < 0 or d >= self.nz:
            return []
        if d == 0:
            return [(None, self.z, 0)]
        return [(self.z >= d, self.z - d, 1), (self.z < self.nz - d, self.z + d, -1)]

    def crossing(self, d, ok, fs, way):
        if d < self.nz // 2:
            return [(ok, self.inner[1])]
        if d == self.nz - 1:
            return [(ok, self.near)]
        end = fs == (0 if way > 0 else self.nz - 1)
        inside = jnp.logical_not(end)
        return [(self.both(ok, inside), self.inner[1]), (self.both(ok, end), self.near)]

    @staticmethod
    def both(left, right):
        return right if left is None else jnp.logical_and(left, right)

    def shard(self, other, fs, core):
        row = 1 - self.y if other else self.y
        return (row * 2 + core) * self.nz + fs

    def send(self, j, shard, span, sems, src=None, **where):
        rows = pl.ds(*span)
        return pltpu.make_async_remote_copy(
            self.dst.at[j, shard, rows] if src is None else src(*span),
            self.dst.at[j, shard, rows],
            *sems,
            device_id=where,
            device_id_type=MESH,
        )

    def own_blocks(self, j):
        start = 0
        for count, ref in self.sources:
            ok = (j >= start) & (j < start + count) if len(self.sources) > 1 else None
            yield ok, functools.partial(ref, j - start)
            start += count

    def keeps(self, j, t):
        sem = self.loc.at[lax.rem(t, self.slots)]
        for ok, src in self.own_blocks(j):
            yield ok, pltpu.make_async_copy(src(0, self.rows), self.dst.at[j, self.own], sem)

    def sends(self, a, j, t):
        todo, nz = [], self.nz
        k, kz = lax.rem(t, self.slots), lax.rem(t, 3 * self.slots)

        def column(ok, fs, way, src):
            shard = self.shard(0, fs, self.c)
            if way >= 0:
                sems = (self.zs.at[kz, 0, fs], self.zr.at[kz, fs])
                up = self.send(j, shard, self.inner[0], sems, src, fs=self.z + 1)
                todo.append((self.both(ok, self.z < nz - 1), up))
            if way <= 0:
                sems = (self.zs.at[kz, 1, fs], self.zr.at[kz, fs])
                down = self.send(j, shard, self.inner[0], sems, src, fs=self.z - 1)
                todo.append((self.both(ok, self.z > 0), down))
            sems = (self.ys.at[k, fs], self.yr.at[k, fs])
            for ok_row, span in self.crossing(a, ok, fs, way):
                todo.append((ok_row, self.send(j, shard, span, sems, src, grp=self.far_row)))
            if way:
                sems = (self.xs.at[k, fs], self.xr.at[k, fs])
                todo.append((ok, self.send(j, shard, self.outer[0], sems, rep=self.far_rep)))
            sems = (self.cs.at[k, fs], self.cr.at[k, fs])
            span = self.inner[0] if way else (0, self.rows)
            todo.append((ok, self.send(j, shard, span, sems, src, grp=self.far_core)))

        if a == 0:
            for ok, src in self.own_blocks(j):
                column(ok, self.z, 0, src)
        else:
            for ok, fs, way in self.at_distance(a):
                column(ok, fs, way, None)
        for ok, fs, way in self.at_distance(a - 1):
            shard = self.shard(1, fs, self.c)
            sems = (self.xs.at[k, nz + fs], self.xr.at[k, nz + fs])
            todo.append((ok, self.send(j, shard, self.outer[1], sems, rep=self.far_rep)))
            sems = (self.cs.at[k, nz + fs], self.cr.at[k, nz + fs])
            todo.append((ok, self.send(j, shard, self.inner[1], sems, grp=self.far_core)))
            if nz // 2 <= a < nz:
                to = self.z + way
                ok = (fs == (0 if way > 0 else nz - 1)) & (to >= 0) & (to < nz)
                sems = (self.ws.at[kz, fs], self.wr.at[kz, fs])
                todo.append((ok, self.send(j, shard, self.along, sems, fs=to)))
        for other in (0, 1):
            for ok, fs, way in self.at_distance(a - 1 - other):
                if way or other:
                    i = other * nz + fs
                    sems = (self.ds.at[k, i], self.dr.at[k, i])
                    shard = self.shard(other, fs, self.c)
                    core = self.send(j, shard, self.far[other], sems, grp=self.far_core)
                    todo.append((ok, core))
        return todo

    def arrivals(self, a, j, t):
        todo, nz = [], self.nz
        k, kz = lax.rem(t, self.slots), lax.rem(t, 3 * self.slots)

        def expect(ok, shard, span, sem):
            ref = self.dst.at[j, shard, pl.ds(*span)]
            todo.append((ok, pltpu.make_async_copy(ref, ref, sem)))

        for ok, fs, way in self.at_distance(a):
            if way:
                expect(ok, self.shard(0, fs, self.c), self.inner[0], self.zr.at[kz, fs])
        for ok, fs, way in self.at_distance(a - 1):
            shard = self.shard(1, fs, self.c)
            for ok_row, span in self.crossing(a - 1, ok, fs, way):
                expect(ok_row, shard, span, self.yr.at[k, fs])
            if a - 1 >= nz // 2:
                end = self.both(ok, fs == (0 if way > 0 else nz - 1))
                expect(end, shard, self.along, self.wr.at[kz, fs])
        for other in (0, 1):
            inner, far = self.inner[other], self.far[other]
            for ok, fs, way in self.at_distance(a - 1 - other):
                i = other * nz + fs
                if way or other:
                    expect(ok, self.shard(other, fs, self.c), far, self.xr.at[k, i])
                span = inner if way or other else (0, self.rows)
                expect(ok, self.shard(other, fs, 1 - self.c), span, self.cr.at[k, i])
            for ok, fs, way in self.at_distance(a - 2 - other):
                if way or other:
                    i = other * nz + fs
                    expect(ok, self.shard(other, fs, 1 - self.c), far, self.dr.at[k, i])
        return todo

    def run(self, early=None, compute=None):
        lag = self.lag

        def act(ok, fn):
            if ok is None:
                fn()
            else:
                pl.when(ok)(fn)

        def finish(a, j, t):
            for ok, copy in self.sends(a - 1, j, t):
                act(ok, copy.wait_send)
            for ok, copy in self.arrivals(a, j, t):
                act(ok, copy.wait)
            if a == 1:
                for ok, copy in self.keeps(j, t):
                    act(ok, copy.wait)

        def begin(a, j, t):
            for ok, copy in self.sends(a, j, t):
                act(ok, copy.start)
            if a == 0:
                for ok, copy in self.keeps(j, t):
                    act(ok, copy.start)

        def tick(t, carry):
            for a in range(self.last, 0, -1):
                j = t - lag * a
                pl.when((j >= 0) & (j < self.count))(functools.partial(finish, a, j, t - lag))
            for a in range(self.last - 1, -1, -1):
                j = t - lag * a
                pl.when((j >= 0) & (j < self.count))(functools.partial(begin, a, j, t))
            if early is not None:
                early(t)
            if compute is not None:
                j = t - lag * self.last
                pl.when(j >= 0)(functools.partial(compute, j))
            return carry

        lax.fori_loop(0, self.count + lag * self.last + (compute is not None), tick, 0)


def head_columns(ref, rows, part, h, width):
    first = pl.multiple_of(part * width + h * HDIM, HDIM)
    return ref[rows, pl.ds(first, HDIM)]


def seen(shape, first):
    row = lax.broadcasted_iota(jnp.int32, shape, 0)
    return lax.broadcasted_iota(jnp.int32, shape, 1) <= first + row


def head_chances(qkv, kp, h, prompt_len, width, first):
    own, cont = slice(0, prompt_len), slice(prompt_len, None)
    q_p = head_columns(qkv, own, 0, h, width)
    q_c = head_columns(qkv, cont, 0, h, width)
    k_c = head_columns(qkv, cont, 1, h, width)
    v_c = head_columns(qkv, cont, 2, h, width)
    lanes = pl.ds(pl.multiple_of(h * HDIM, HDIM), HDIM)
    k_p = kp[:, :, lanes].reshape(-1, HDIM)
    lanes = pl.ds(pl.multiple_of(width + h * HDIM, HDIM), HDIM)
    v_p = kp[:, :, lanes].reshape(-1, HDIM)
    s_p = mm_nt(q_p, k_p) * SCALE
    s_p = jnp.where(seen(s_p.shape, first), s_p, NEG_FILL)
    e_p = jnp.exp(s_p - jnp.max(s_p, axis=-1, keepdims=True))
    c_p = e_p * (1.0 / jnp.sum(e_p, axis=-1, keepdims=True))
    s_1 = mm_nt(q_c, k_p) * SCALE
    s_2 = mm_nt(q_c, k_c) * SCALE
    s_2 = jnp.where(seen(s_2.shape, 0), s_2, NEG_FILL)
    peak = jnp.maximum(
        jnp.max(s_1, axis=-1, keepdims=True), jnp.max(s_2, axis=-1, keepdims=True)
    )
    e_1, e_2 = jnp.exp(s_1 - peak), jnp.exp(s_2 - peak)
    mass = jnp.sum(e_1, axis=-1, keepdims=True) + jnp.sum(e_2, axis=-1, keepdims=True)
    inv = 1.0 / mass
    return (q_p, q_c, k_p, k_c, v_p, v_c), (c_p, e_1 * inv, e_2 * inv)


def select_call(ids, tables):
    def kernel(ids, *refs):
        for src, dst in zip(refs[: len(tables)], refs[len(tables) :]):
            dst[...] = src[0]

    def spec_in(t):
        return pl.BlockSpec((1,) + t.shape[1:], lambda i, ids: (ids[i],) + (0,) * (t.ndim - 1))

    def spec_out(t):
        lead = t.ndim - 3
        return pl.BlockSpec(t.shape[1:], lambda i, ids: (0,) * lead + (i, 0))

    return pl.pallas_call(
        kernel,
        grid_spec=pltpu.PrefetchScalarGridSpec(
            num_scalar_prefetch=1,
            grid=(2,),
            in_specs=[spec_in(t) for t in tables],
            out_specs=[spec_out(t) for t in tables],
        ),
        out_shape=[
            jax.ShapeDtypeStruct(t.shape[1:-2] + (2 * RANK, t.shape[-1]), BF) for t in tables
        ],
        name="select",
    )(ids, *tables)


def columns_of(ref):
    return lambda j, first, size: ref.at[
        pl.ds(first, size), pl.ds(pl.multiple_of(j * PART, PART), PART)
    ]


def tiles_of(ref, shard_rows, parts):
    def tile(j, first, size):
        row = pl.multiple_of(lax.rem(j, parts) * shard_rows + first, 8)
        return ref.at[pl.ds(row, size), pl.ds(pl.multiple_of(j // parts * PART, PART), PART)]

    return tile


def pair_loads(blocks, first, wbuf, wsem, k):
    return [
        pltpu.make_async_copy(
            blocks.at[first + i], wbuf.at[k, :, :, pl.ds(i * PART, PART)], wsem.at[k, i]
        )
        for i in range(2)
    ]


PIECES = 8


def pack(out, unit, piece, value):
    value = value.astype(BF)
    for n in range(PIECES):
        out[n, :, unit * piece : (unit + 1) * piece] = value[:, n * piece : (n + 1) * piece]


def forward_call(x_p, x_c, cot_p, cot_c, norms, tables, weights, n_fs, n_shard):
    prompt_len, width = x_p.shape
    rows = prompt_len + x_c.shape[0]
    shard_rows, hidden = weights[3].shape
    parts = weights[2].shape[0] // shard_rows
    n_qkv, n_out, n_up = 3 * width // PART, width // PART, hidden // PART
    n_dn = n_out * parts
    before_up = n_qkv + n_out + n_dn
    count = before_up + n_up
    n_grp = n_shard // n_fs
    heads = width // HDIM
    per = width // BLOCK
    piece = width // PIECES
    lag = 2
    t_share = n_qkv + lag * (n_fs + 2) + 1
    t_onward = t_share + 10
    t_head = t_onward + 1
    t_out = t_head + heads
    t_norm = t_out + per

    def kernel(x_p, x_c, gain_one, bias_one, gain_two, bias_two, *refs):
        (a_ext, b_ext, a_up, b_up, a_dn, b_dn), refs = refs[:6], refs[6:]
        (cot_p, cot_c), src, refs = refs[:2], refs[2:6], refs[6:]
        (dst, qkv_out, kp_out, normed_out, mixed_out), refs = refs[:5], refs[5:]
        (lows, res_p, res_c, resid_back, grad_attn, low_o), refs = refs[:6], refs[6:]
        packed, refs = refs[0], refs[1:]
        (qkv, kp, normed_one, normed, mixed, cot, resid, out_acc), refs = refs[:8], refs[8:]
        (low_up, dlow_dn, low_dn, dlow_up, wbuf, dbuf), refs = refs[:6], refs[6:]
        (wsem, dsem, ksend, krecv, lsem), sems = refs[:5], refs[5:]
        own, rest = slice(0, prompt_len), slice(prompt_len, None)
        sources = [
            (n_qkv, columns_of(src[0])),
            (n_out, columns_of(src[1])),
            (n_dn, tiles_of(src[2], shard_rows, parts)),
            (n_up, columns_of(src[3])),
        ]
        engine = Gather(n_fs, sources, dst, sems, lag)
        engine.barrier()
        grp = lax.axis_index("grp")
        loads = [
            pltpu.make_async_copy(cot_p, cot.at[pl.ds(0, prompt_len)], lsem.at[0]),
            pltpu.make_async_copy(cot_c, cot.at[pl.ds(prompt_len, rows - prompt_len)], lsem.at[1]),
        ]
        stores = [
            pltpu.make_async_copy(qkv, qkv_out, lsem.at[2]),
            pltpu.make_async_copy(kp, kp_out, lsem.at[3]),
            pltpu.make_async_copy(normed_one, normed_out, lsem.at[4]),
            pltpu.make_async_copy(mixed, mixed_out, lsem.at[5]),
        ]

        def pass_on(n, whose, to):
            return pltpu.make_async_remote_copy(
                kp.at[whose],
                kp.at[whose],
                ksend.at[n],
                krecv.at[n],
                device_id={"grp": to},
                device_id_type=MESH,
            )

        def landed(n, whose):
            return pltpu.make_async_copy(kp.at[whose], kp.at[whose], krecv.at[n])

        to_row = pass_on(0, grp, engine.far_row)
        to_core = pass_on(1, grp, engine.far_core)
        onward = pass_on(2, engine.far_row, engine.far_core)
        diagonal = (1 - engine.y) * 2 + 1 - engine.c

        def early(t):
            @pl.when(t == 0)
            def _():
                for copy in loads:
                    copy.start()
                for x, part in ((x_p, own), (x_c, rest)):
                    hat, _ = norm_stats(x[...].astype(F32))
                    normed_one[part] = (hat * gain_one[...] + bias_one[...]).astype(BF)
                for n in range(3):
                    lows[n] = low_of(mm_nt(normed_one[...], a_ext[n]), prompt_len)
                for copy in loads:
                    copy.wait()
                dlow_dn[...] = low_of(mm_nt(cot[...], b_dn[...]), prompt_len)

            @pl.when(t == t_share)
            def _():
                kp[grp] = qkv[:prompt_len, width:]
                to_row.start()
                to_core.start()
                stores[0].start()
                stores[2].start()

            @pl.when(t == t_onward)
            def _():
                landed(0, engine.far_row).wait()
                onward.start()

            @pl.when(t == t_head)
            def _():
                landed(1, engine.far_core).wait()
                landed(2, diagonal).wait()
                to_row.wait_send()
                to_core.wait_send()
                onward.wait_send()
                stores[1].start()

            @pl.when((t >= t_head) & (t < t_out))
            def _():
                h = t - t_head
                (_, _, _, _, v_p, v_c), (c_p, c_1, c_2) = head_chances(
                    qkv, kp, h, prompt_len, width, grp * prompt_len
                )
                lanes = pl.ds(pl.multiple_of(h * HDIM, HDIM), HDIM)
                mixed[own, lanes] = mm(c_p.astype(BF), v_p).astype(BF)
                mixed[rest, lanes] = (mm(c_1.astype(BF), v_p) + mm(c_2.astype(BF), v_c)).astype(BF)

            def load_out(b):
                return pair_loads(dst, n_qkv + 2 * b, wbuf, wsem, lax.rem(b, 2))

            @pl.when(t == t_out - 1)
            def _():
                for copy in load_out(0):
                    copy.start()

            @pl.when((t >= t_out) & (t < t_norm))
            def _():
                b = t - t_out

                @pl.when(b == 0)
                def _():
                    stores[3].start()
                    low_o[...] = low_of(mm_nt(mixed[...], a_ext[3]), prompt_len)

                for copy in load_out(b):
                    copy.wait()

                @pl.when(b + 1 < per)
                def _():
                    for copy in load_out(b + 1):
                        copy.start()

                cols = pl.ds(pl.multiple_of(b * BLOCK, BLOCK), BLOCK)
                w = wbuf[lax.rem(b, 2)].reshape(-1, BLOCK)
                branch = mm(mixed[...], w) + mm(low_o[...], b_ext[3, :, cols])
                resid[own, cols] = x_p[:, cols].astype(F32) + branch[own]
                resid[rest, cols] = x_c[:, cols].astype(F32) + branch[rest]

            @pl.when(t == t_norm)
            def _():
                hat, _ = norm_stats(resid[...])
                normed[...] = (hat * gain_two[...] + bias_two[...]).astype(BF)
                low_up[...] = low_of(mm_nt(normed[...], a_up[...]), prompt_len)
                out_acc[...] = resid[...]
                resid_back[...] = jnp.zeros_like(resid_back)
                low_dn[...] = jnp.zeros_like(low_dn)
                dlow_up[...] = jnp.zeros_like(dlow_up)

        def load(j):
            k, i = lax.rem(j // 2, 2), lax.rem(j, 2)
            into = wbuf.at[k, :, :, pl.ds(pl.multiple_of(i * PART, PART), PART)]
            return pltpu.make_async_copy(dst.at[j], into, wsem.at[k, i])

        def load_down(n):
            k = lax.rem(n, 2)
            return [
                pltpu.make_async_copy(
                    dst.at[pl.ds(n_qkv + n_out + b * parts, parts), n],
                    dbuf.at[k, :, :, pl.ds(b * PART, PART)],
                    dsem.at[k, b],
                )
                for b in range(n_out)
            ]

        def compute(j):
            n = j - before_up

            @pl.when((j < n_qkv) | ((n >= 0) & (n < n_up)))
            def _():
                load(j).start()

            @pl.when((n >= 0) & (n < n_up) & (lax.rem(j, 2) == 0))
            def _():
                for copy in load_down(n // 2):
                    copy.start()

            @pl.when((j > 0) & (j <= n_qkv) & (lax.rem(j, 2) == 0))
            def _():
                i = j // 2 - 1
                for first in (j - 2, j - 1):
                    load(first).wait()
                w = wbuf[lax.rem(i, 2)].reshape(-1, BLOCK)
                m = i // per
                inside = pl.ds(pl.multiple_of(lax.rem(i, per) * BLOCK, BLOCK), BLOCK)
                cols = pl.ds(pl.multiple_of(i * BLOCK, BLOCK), BLOCK)
                extra = mm(lows[m], b_ext[m, :, inside])
                qkv[:, cols] = (mm(normed_one[...], w) + extra).astype(BF)

            @pl.when((n > 0) & (lax.rem(j, 2) == 0))
            def _():
                i = n // 2 - 1
                for first in (j - 2, j - 1):
                    load(first).wait()
                for copy in load_down(i):
                    copy.wait()
                cols = pl.ds(pl.multiple_of(i * BLOCK, BLOCK), BLOCK)
                w_up = wbuf[lax.rem(j // 2 - 1, 2)].reshape(-1, BLOCK)
                w_dn = dbuf[lax.rem(i, 2)].reshape(BLOCK, width)
                a_d, b_u = a_dn[:, cols], b_up[:, cols]
                pre = mm(normed[...], w_up) + mm(low_up[...], b_u)
                cdf = 0.5 * (1.0 + lax.erf(pre * math.sqrt(0.5)))
                act = (pre * cdf).astype(BF)
                slope = cdf + pre * jnp.exp(-0.5 * pre * pre) * (1.0 / math.sqrt(2.0 * math.pi))
                grad_act = mm_nt(cot[...], w_dn) + mm(dlow_dn[...], a_d)
                grad_pre = (grad_act * slope).astype(BF)
                out_acc[...] += mm(act, w_dn)
                resid_back[...] += mm_nt(grad_pre, w_up)
                low_dn[...] += mm_nt(act, a_d)
                dlow_up[...] += mm_nt(grad_pre, b_u)
                wide = hidden // width
                for base, grad in (
                    (0, mm_tn(low_up[...], grad_pre).astype(BF)),
                    (wide, mm_tn(dlow_dn[...], act).astype(BF)),
                ):
                    unit = pl.ds(pl.multiple_of((base + i // per) * piece, piece), piece)
                    for m in range(BLOCK // piece):
                        where = lax.rem(i, per) * (BLOCK // piece) + m
                        packed[where, :, unit] = grad[:, m * piece : (m + 1) * piece]

        engine.run(early, compute)
        dlow = low_of(dlow_up[...], prompt_len)
        pack(packed, 2 * (hidden // width), piece, mm_tn(dlow, normed[...]))
        grad = resid_back[...] + mm(dlow, a_up[...])
        grad = cot[...].astype(F32) + norm_back(resid[...], gain_two[...], grad)
        resid_back[...] = grad
        grad_attn[...] = grad.astype(BF)
        low = low_of(low_dn[...], prompt_len)
        result = (out_acc[...] + mm(low, b_dn[...])).astype(BF)
        res_p[...] = result[own]
        res_c[...] = result[rest]
        pack(packed, 2 * (hidden // width) + 1, piece, mm_tn(low, cot[...]))
        for copy in stores:
            copy.wait()

    like = jax.ShapeDtypeStruct
    two = 2 * RANK
    dma = pltpu.SemaphoreType.DMA
    share = (n_grp, prompt_len, 2 * width)
    return pl.pallas_call(
        kernel,
        out_shape=[
            like((count, n_shard, shard_rows, PART), BF),
            like((rows, 3 * width), BF),
            like(share, BF),
            like((rows, width), BF),
            like((rows, width), BF),
            like((3, rows, two), BF),
            like(x_p.shape, BF),
            like(x_c.shape, BF),
            like((rows, width), F32),
            like((rows, width), BF),
            like((rows, two), BF),
            like((PIECES, two, (2 * (hidden // width) + 2) * piece), BF),
        ],
        in_specs=[WHOLE] * 12 + [ANY] * 6,
        out_specs=[ANY] * 5 + [WHOLE] * 7,
        scratch_shapes=[
            pltpu.VMEM((rows, 3 * width), BF),
            pltpu.VMEM(share, BF),
            pltpu.VMEM((rows, width), BF),
            pltpu.VMEM((rows, width), BF),
            pltpu.VMEM((rows, width), BF),
            pltpu.VMEM((rows, width), BF),
            pltpu.VMEM((rows, width), F32),
            pltpu.VMEM((rows, width), F32),
            pltpu.VMEM((rows, two), BF),
            pltpu.VMEM((rows, two), BF),
            pltpu.VMEM((rows, two), F32),
            pltpu.VMEM((rows, two), F32),
            pltpu.VMEM((2, n_shard, shard_rows, BLOCK), BF),
            pltpu.VMEM((2, parts, shard_rows, width), BF),
            dma((2, 2)),
            dma((2, n_out)),
            dma((3,)),
            dma((3,)),
            dma((6,)),
        ]
        + Gather.semaphores(n_fs, lag),
        compiler_params=pltpu.CompilerParams(
            collective_id=0, has_side_effects=True, vmem_limit_bytes=ROOM
        ),
        name="forward",
    )(x_p, x_c, *norms, *tables, cot_p, cot_c, *weights)


class TableSum:
    def __init__(self, n_fs, hots, units, bufs, sems, stepwise):
        self.n_fs, self.hots, self.units, self.stepwise = n_fs, hots, units, stepwise
        self.out, self.got, self.dense, self.parts, self.sums = bufs
        (self.s1, self.r1, self.s2, self.r2, self.s3, self.r3) = sems
        rep, self.grp = lax.axis_index("rep"), lax.axis_index("grp")
        self.z = lax.axis_index("fs")
        plane = rep % 2
        y, c = self.grp // 2, self.grp % 2
        self.me = plane * 4 + self.grp
        self.peers = []
        for q in range(1, PIECES):
            x_to = 1 - plane if q // 4 else plane
            y_to = 1 - y if q // 2 % 2 else y
            c_to = 1 - c if q % 2 else c
            where = {"grp": y_to * 2 + c_to}
            if q // 4:
                where["rep"] = rep + 1 - 2 * plane
            self.peers.append((q, x_to * 4 + y_to * 2 + c_to, where))
        self.piece = self.out.shape[2] // units

    @staticmethod
    def scratch(n_fs, units, piece, count):
        two, wide = 2 * RANK, units * piece
        rows = count * RANK // n_fs
        bufs = [
            pltpu.VMEM((PIECES, two, wide), BF),
            pltpu.VMEM((PIECES, two, wide), BF),
            pltpu.VMEM((n_fs, rows, wide), BF),
            pltpu.VMEM((n_fs, rows, wide), BF),
            pltpu.VMEM((PIECES, rows, wide), BF),
        ]
        dma = pltpu.SemaphoreType.DMA
        return bufs, [dma((PIECES,))] * 2 + [dma((n_fs,))] * 2 + [dma((PIECES,))] * 2

    def pack(self, unit, value):
        pack(self.out, unit, self.piece, value)

    def exchange(self):
        return [
            pltpu.make_async_remote_copy(
                self.out.at[to],
                self.got.at[self.me],
                self.s1.at[q],
                self.r1.at[q],
                device_id=where,
                device_id_type=MESH,
            )
            for q, to, where in self.peers
        ]

    def along_fs(self):
        copies = []
        for d in range(1, self.n_fs):
            to = lax.rem(self.z + d, self.n_fs)
            copies.append(
                pltpu.make_async_remote_copy(
                    self.dense.at[to],
                    self.parts.at[self.z],
                    self.s2.at[d],
                    self.r2.at[d],
                    device_id={"fs": to},
                    device_id_type=MESH,
                )
            )
        return copies

    def hand(self, n, whose, q):
        return pltpu.make_async_remote_copy(
            self.sums.at[whose],
            self.sums.at[whose],
            self.s3.at[n],
            self.r3.at[n],
            device_id=self.peers[q - 1][2],
            device_id_type=MESH,
        )

    def hand_out(self):
        return [self.hand(q, self.me, q) for q, _, _ in self.peers]

    def relay(self, stage):
        far_row, far_rep, both = (self.peers[q - 1][1] for q in (2, 4, 6))
        steps = [
            [(4, self.me, 4), (2, self.me, 2), (1, self.me, 1)],
            [(6, far_rep, 2), (5, far_rep, 1), (3, far_row, 1)],
            [(7, both, 1)],
        ]
        return [self.hand(*step) for step in steps[stage]]

    def arrived(self, q):
        ref = self.sums.at[self.peers[q - 1][1]]
        pltpu.make_async_copy(ref, ref, self.r3.at[q]).wait()

    def first(self):
        for copy in self.exchange():
            copy.start()
        self.got[self.me] = self.out[self.me]

    def second(self):
        for q, whose, _ in self.peers:
            ref = self.got.at[whose]
            pltpu.make_async_copy(ref, ref, self.r1.at[q]).wait()
        for copy in self.exchange():
            copy.wait_send()
        wide = self.out.shape[2]
        hots = self.hots[...].reshape(PIECES * 2 * RANK, -1)
        dense = mm_tn(hots, self.got[...].reshape(PIECES * 2 * RANK, wide))
        self.dense[...] = dense.astype(BF).reshape(self.dense.shape)
        for copy in self.along_fs():
            copy.start()
        self.parts[self.z] = self.dense[self.z]

    def third(self):
        for d in range(1, self.n_fs):
            ref = self.parts.at[lax.rem(self.z + self.n_fs - d, self.n_fs)]
            pltpu.make_async_copy(ref, ref, self.r2.at[d]).wait()
        for copy in self.along_fs():
            copy.wait_send()
        total = self.parts[0].astype(F32)
        for n in range(1, self.n_fs):
            total = total + self.parts[n].astype(F32)
        self.sums[self.me] = total.astype(BF)
        if not self.stepwise:
            for copy in self.hand_out():
                copy.start()
            return
        for copy in self.relay(0):
            copy.start()

    def fourth(self):
        self.arrived(4)
        self.arrived(2)
        for copy in self.relay(1):
            copy.start()

    def fifth(self):
        self.arrived(6)
        for copy in self.relay(2):
            copy.start()

    def last(self, places):
        if self.stepwise:
            for q in (1, 3, 5, 7):
                self.arrived(q)
            sent = self.relay(0) + self.relay(1) + self.relay(2)
        else:
            for q, _, _ in self.peers:
                self.arrived(q)
            sent = self.hand_out()
        for copy in sent:
            copy.wait_send()
        for unit, place in enumerate(places):
            for k in range(PIECES):
                cols = slice(unit * self.piece, (unit + 1) * self.piece)
                for a in range(self.sums.shape[1] // RANK):
                    value = self.sums[k, a * RANK : (a + 1) * RANK, cols]
                    place(a, k * self.piece, value)


def back_call(
    grad_attn, mixed, low_o, lows, gain, a_ext, b_ext, hot, packed, qkv, kp, x_p, x_c, normed, grad_resid, w_all, n_fs, count
):
    rows, width = grad_attn.shape
    prompt_len, cont_len = x_p.shape[0], x_c.shape[0]
    heads = width // HDIM
    n_grp = kp.shape[0]
    n_shard, shard_rows = w_all.shape[1:3]
    per = width // BLOCK
    n_qkv = 3 * per
    piece = width // PIECES
    adapters = count // n_fs
    groups = 4
    group_heads = heads // groups
    half = group_heads * HDIM
    two = 2 * RANK
    first_units = packed.shape[2] // piece
    wide_units = first_units // 2 - 1
    hidden = wide_units * width
    last_units = 4

    def kernel(*refs):
        (grad_attn, mixed, low_o, lows, gain, a_ext, b_ext, hot), refs = refs[:8], refs[8:]
        packed, refs = refs[0], refs[1:]
        (qkv, kp, x_p, x_c, normed, grad_resid, w_all), refs = refs[:7], refs[7:]
        (out_p, out_c, t_a, t_b, t_a_up, t_b_up, t_a_dn, t_b_dn), refs = refs[:8], refs[8:]
        (grads, keep, late, x, normed_here, wbuf, gm, acc, dlow, dlow_o), refs = refs[:10], refs[10:]
        (far, far_core, far_row, hots), refs = refs[:4], refs[4:]
        bufs_one, bufs_mid, bufs_two, refs = (packed, *refs[:4]), refs[4:9], refs[9:14], refs[14:]
        sems_one, sems_mid, sems_two, refs = refs[:6], refs[6:12], refs[12:18], refs[18:]
        lsem, wsem, csend, crecv, rsend, rrecv, hsend, hrecv = refs
        grp = lax.axis_index("grp")
        y, c = grp // 2, grp % 2
        own, rest = slice(0, prompt_len), slice(prompt_len, None)
        one = TableSum(n_fs, hots, first_units, bufs_one, sems_one, True)
        mid = TableSum(n_fs, hots, last_units, bufs_mid, sems_mid, True)
        two_ = TableSum(n_fs, hots, last_units, bufs_two, sems_two, False)
        barrier = pltpu.get_barrier_semaphore()
        for _, _, where in one.peers:
            pl.semaphore_signal(barrier, 1, device_id=where, device_id_type=MESH)
        for d in range(1, n_fs):
            to = lax.rem(one.z + d, n_fs)
            pl.semaphore_signal(barrier, 1, device_id={"fs": to}, device_id_type=MESH)

        loads = [
            pltpu.make_async_copy(src, dst, lsem.at[n])
            for n, (src, dst) in enumerate(
                [
                    (qkv, grads),
                    (kp, keep),
                    (grad_resid, late),
                    (normed, normed_here),
                    (x_p, x.at[pl.ds(0, prompt_len)]),
                    (x_c, x.at[pl.ds(prompt_len, cont_len)]),
                ]
            )
        ]
        for copy in loads:
            copy.start()

        def load_w(i, k):
            for copy in pair_loads(w_all, 2 * i, wbuf, wsem, k):
                copy.start()

        def wait_w(i, k):
            for copy in pair_loads(w_all, 2 * i, wbuf, wsem, k):
                copy.wait()

        load_w(n_qkv, 0)
        pl.semaphore_wait(barrier, len(one.peers) + n_fs - 1)

        hots[one.me] = hot[...]
        hot_sends = [
            pltpu.make_async_remote_copy(
                hots.at[one.me],
                hots.at[one.me],
                hsend.at[q],
                hrecv.at[q],
                device_id=where,
                device_id_type=MESH,
            )
            for q, _, where in one.peers
        ]
        for copy in hot_sends:
            copy.start()
        one.first()
        dlow_o[...] = low_of(mm_nt(grad_attn[...], b_ext[3]), prompt_len)
        mid.pack(0, mm_tn(dlow_o[...], mixed[...]))
        mid.pack(1, mm_tn(low_o[...], grad_attn[...]))

        acc[...] = mm(dlow_o[...], a_ext[3])
        for n in range(per):
            wait_w(n_qkv + n, n % 2)
            if n + 1 < per:
                load_w(n_qkv + n + 1, (n + 1) % 2)
            w = wbuf[n % 2].reshape(-1, BLOCK)
            acc[...] += mm_nt(grad_attn[:, n * BLOCK : (n + 1) * BLOCK], w)
        gm[...] = acc[...].astype(BF)
        load_w(0, 0)
        load_w(1, 1)

        loads[0].wait()
        loads[1].wait()

        def head(part, n, carry):
            h = part * group_heads + n
            first = grp * prompt_len
            (q_p, q_c, k_p, k_c, v_p, v_c), (c_p, c_1, c_2) = head_chances(
                grads, keep, h, prompt_len, width, first
            )
            lanes = [
                pl.ds(pl.multiple_of(i * width + h * HDIM, HDIM), HDIM) for i in range(3)
            ]
            gm_p, gm_c = gm[own, lanes[0]], gm[rest, lanes[0]]
            d_p = mm_nt(gm_p, v_p)
            d_1, d_2 = mm_nt(gm_c, v_p), mm_nt(gm_c, v_c)
            s_p = (c_p * (d_p - jnp.sum(c_p * d_p, axis=-1, keepdims=True))).astype(BF)
            inner = jnp.sum(c_1 * d_1, axis=-1, keepdims=True) + jnp.sum(
                c_2 * d_2, axis=-1, keepdims=True
            )
            s_1 = (c_1 * (d_1 - inner)).astype(BF)
            s_2 = (c_2 * (d_2 - inner)).astype(BF)
            grads[own, lanes[0]] = (mm(s_p, k_p) * SCALE).astype(BF)
            grads[rest, lanes[0]] = ((mm(s_1, k_p) + mm(s_2, k_c)) * SCALE).astype(BF)
            grads[rest, lanes[1]] = (mm_tn(s_2, q_c) * SCALE).astype(BF)
            grads[rest, lanes[2]] = mm_tn(c_2.astype(BF), gm_c).astype(BF)
            g_k = ((mm_tn(s_p, q_p) + mm_tn(s_1, q_c)) * SCALE).astype(BF)
            g_v = (mm_tn(c_p.astype(BF), gm_p) + mm_tn(c_1.astype(BF), gm_c)).astype(BF)
            into = [pl.ds(pl.multiple_of(i * half + n * HDIM, HDIM), HDIM) for i in range(2)]
            far[part, :, :, into[0]] = g_k.reshape(n_grp, prompt_len, HDIM)
            far[part, :, :, into[1]] = g_v.reshape(n_grp, prompt_len, HDIM)
            return carry

        def to_core(part):
            return [
                pltpu.make_async_remote_copy(
                    far.at[part, row * 2 + 1 - c],
                    far_core.at[part, row],
                    csend.at[part, row],
                    crecv.at[part, row],
                    device_id={"grp": y * 2 + 1 - c},
                    device_id_type=MESH,
                )
                for row in range(2)
            ]

        def to_row(part):
            return pltpu.make_async_remote_copy(
                far.at[part, (1 - y) * 2 + c],
                far_row.at[part],
                rsend.at[part],
                rrecv.at[part],
                device_id={"grp": (1 - y) * 2 + c},
                device_id_type=MESH,
            )

        def add_core(part):
            for copy in to_core(part):
                copy.wait()
            for row in range(2):
                total = far[part, row * 2 + c].astype(F32) + far_core[part, row].astype(F32)
                far[part, row * 2 + c] = total.astype(BF)
            to_row(part).start()

        def add_row(part):
            to_row(part).wait()
            total = far[part, grp].astype(F32) + far_row[part].astype(F32)
            total = total.astype(BF)
            for i in range(2):
                cols = slice((i + 1) * width + part * half, (i + 1) * width + (part + 1) * half)
                grads[own, cols] = total[:, i * half : (i + 1) * half]

        def half_group(i, carry):
            part = i // 2

            @pl.when((lax.rem(i, 2) == 1) & (part > 0))
            def _():
                add_core(part - 1)

            first = lax.rem(i, 2) * (group_heads // 2)
            lax.fori_loop(first, first + group_heads // 2, functools.partial(head, part), 0)

            @pl.when(lax.rem(i, 2) == 1)
            def _():
                for copy in to_core(part):
                    copy.start()

            @pl.when(i == 1)
            def _():
                for copy in hot_sends:
                    copy.wait_send()
                for q, whose, _ in one.peers:
                    pltpu.make_async_copy(hots.at[whose], hots.at[whose], hrecv.at[q]).wait()
                one.second()

            return carry

        lax.fori_loop(0, 2 * groups, half_group, 0)

        def tables(i, into, first):
            part = grads[:, i * width : (i + 1) * width]
            low = low_of(mm_nt(part, b_ext[i]), prompt_len)
            into.pack(first, mm_tn(low, normed_here[...]))
            into.pack(first + 1, mm_tn(lows[i], part))
            dlow[i] = low

        def project(n, carry):
            k = lax.rem(n, 2)
            wait_w(n, k)
            part = grads[:, pl.ds(pl.multiple_of(n * BLOCK, BLOCK), BLOCK)]
            acc[...] += mm_nt(part, wbuf[k].reshape(-1, BLOCK))

            @pl.when(n + 2 < n_qkv)
            def _():
                load_w(n + 2, k)

            return carry

        loads[3].wait()
        add_core(groups - 1)
        tables(0, mid, 2)
        mid.first()
        acc[...] = mm(dlow[0], a_ext[0])
        lax.fori_loop(0, per, project, 0)
        for part in range(groups):
            add_row(part)
        tables(1, two_, 0)
        tables(2, two_, 2)
        two_.first()
        mid.second()
        one.third()
        acc[...] += mm(dlow[1], a_ext[1]) + mm(dlow[2], a_ext[2])

        def project_more(n, carry):
            pl.when(n == 2 * per + 1)(two_.second)
            return project(n, carry)

        lax.fori_loop(per, n_qkv, project_more, 0)
        mid.third()
        one.fourth()
        for copy in (loads[2], loads[4], loads[5]):
            copy.wait()
        back = late[...] + norm_back(x[...].astype(F32), gain[...], acc[...])
        back = back.astype(BF)
        out_p[...] = back[own]
        out_c[...] = back[rest]

        def whole(ref, first):
            def place(a, col, value):
                ref[a, :, first + col : first + col + piece] = value

            return place

        def one_map(ref, n):
            def place(a, col, value):
                ref[a, n, :, col : col + piece] = value

            return place

        two_.third()
        one.fifth()
        mid.fourth()
        mid.fifth()
        one.last(
            [whole(t_b_up, n * width) for n in range(wide_units)]
            + [whole(t_a_dn, n * width) for n in range(wide_units)]
            + [whole(t_a_up, 0), whole(t_b_dn, 0)]
        )
        mid.last([one_map(t_a, 3), one_map(t_b, 3), one_map(t_a, 0), one_map(t_b, 0)])
        two_.last([one_map(t_a, 1), one_map(t_b, 1), one_map(t_a, 2), one_map(t_b, 2)])

    like = jax.ShapeDtypeStruct
    bufs_one, sems_one = TableSum.scratch(n_fs, first_units, piece, count)
    bufs_mid, sems_mid = TableSum.scratch(n_fs, last_units, piece, count)
    bufs_two, sems_two = TableSum.scratch(n_fs, last_units, piece, count)
    dma = pltpu.SemaphoreType.DMA
    return pl.pallas_call(
        kernel,
        out_shape=[
            like(x_p.shape, BF),
            like(x_c.shape, BF),
            like((adapters, 4, RANK, width), BF),
            like((adapters, 4, RANK, width), BF),
            like((adapters, RANK, width), BF),
            like((adapters, RANK, hidden), BF),
            like((adapters, RANK, hidden), BF),
            like((adapters, RANK, width), BF),
        ],
        in_specs=[WHOLE] * 9 + [ANY] * 7,
        out_specs=[WHOLE] * 8,
        scratch_shapes=[
            pltpu.VMEM((rows, 3 * width), BF),
            pltpu.VMEM(kp.shape, BF),
            pltpu.VMEM((rows, width), F32),
            pltpu.VMEM((rows, width), BF),
            pltpu.VMEM((rows, width), BF),
            pltpu.VMEM((2, n_shard, shard_rows, BLOCK), BF),
            pltpu.VMEM((rows, width), BF),
            pltpu.VMEM((rows, width), F32),
            pltpu.VMEM((3, rows, two), BF),
            pltpu.VMEM((rows, two), BF),
            pltpu.VMEM((groups, n_grp, prompt_len, 2 * half), BF),
            pltpu.VMEM((groups, 2, prompt_len, 2 * half), BF),
            pltpu.VMEM((groups, prompt_len, 2 * half), BF),
            pltpu.VMEM((PIECES,) + hot.shape, BF),
        ]
        + bufs_one[1:]
        + bufs_mid
        + bufs_two
        + sems_one
        + sems_mid
        + sems_two
        + [dma((6,)), dma((2, 2)), dma((groups, 2)), dma((groups, 2)), dma((groups,)), dma((groups,))]
        + [dma((PIECES,)), dma((PIECES,))],
        compiler_params=pltpu.CompilerParams(
            collective_id=2, has_side_effects=True, vmem_limit_bytes=ROOM
        ),
        name="back",
    )(
        grad_attn, mixed, low_o, lows, gain, a_ext, b_ext, hot, packed,
        qkv, kp, x_p, x_c, normed, grad_resid, w_all,
    )


def make_body(sizes):
    n_rep, n_grp, n_fs = sizes
    n_shard = n_grp * n_fs

    def other_pairs(v):
        step = 2
        while step < n_rep:
            far = lax.ppermute(v, "rep", [(i, i ^ step) for i in range(n_rep)])
            v = (v.astype(F32) + far.astype(F32)).astype(BF)
            step *= 2
        return v.astype(F32)

    def body(
        prompt_input_rows,
        continuation_input,
        prompt_group_adapter,
        continuation_adapter,
        first_norm_scale,
        first_norm_bias,
        second_norm_scale,
        second_norm_bias,
        frozen_query_key_value,
        frozen_output_weight,
        frozen_up_weight,
        frozen_down_weight,
        adapter_attention_input,
        adapter_attention_output,
        adapter_up_input,
        adapter_up_output,
        adapter_down_input,
        adapter_down_output,
        prompt_cotangent,
        continuation_cotangent,
    ):
        prompt_len, width = prompt_input_rows.shape[2:]
        count = adapter_up_input.shape[0]
        hidden = frozen_up_weight.shape[1]
        shard_rows = frozen_query_key_value.shape[0]
        assert n_grp == 4 and hidden == n_shard * BLOCK
        assert frozen_down_weight.shape[0] == BLOCK and BLOCK % shard_rows == 0

        def flat(v):
            return v.reshape(v.shape[-2:])

        x_p, x_c = flat(prompt_input_rows), flat(continuation_input)
        cot_p, cot_c = flat(prompt_cotangent), flat(continuation_cotangent)
        ids = jnp.concatenate([prompt_group_adapter.reshape(1), continuation_adapter.reshape(1)])
        a_ext, b_ext, a_up, b_up, a_dn, b_dn = select_call(
            ids,
            [
                adapter_attention_input.swapaxes(2, 3),
                adapter_attention_output,
                adapter_up_input.swapaxes(1, 2),
                adapter_up_output,
                adapter_down_input.swapaxes(1, 2),
                adapter_down_output,
            ],
        )
        place = jnp.repeat(ids, RANK) * RANK + jnp.arange(2 * RANK) % RANK
        hot = (place[:, None] == jnp.arange(count * RANK)[None, :]).astype(BF)
        norms = [
            v[None, :]
            for v in (first_norm_scale, first_norm_bias, second_norm_scale, second_norm_bias)
        ]
        (
            w_all,
            qkv,
            kp,
            normed_one,
            mixed,
            lows,
            res_p,
            res_c,
            grad_resid,
            grad_attn,
            low_o,
            packed,
        ) = forward_call(
            x_p,
            x_c,
            cot_p,
            cot_c,
            norms,
            (a_ext, b_ext, a_up, b_up, a_dn, b_dn),
            (frozen_query_key_value, frozen_output_weight, frozen_down_weight, frozen_up_weight),
            n_fs,
            n_shard,
        )
        grad_p, grad_c, t_a, t_b, t_a_up, t_b_up, t_a_dn, t_b_dn = back_call(
            grad_attn,
            mixed,
            low_o,
            lows,
            norms[0],
            a_ext,
            b_ext,
            hot,
            packed,
            qkv,
            kp,
            x_p,
            x_c,
            normed_one,
            grad_resid,
            w_all,
            n_fs,
            count,
        )
        return (
            res_p.reshape(prompt_input_rows.shape),
            res_c.reshape(continuation_input.shape),
            grad_p.reshape(prompt_input_rows.shape),
            grad_c.reshape(continuation_input.shape),
            other_pairs(t_a).swapaxes(2, 3),
            other_pairs(t_b),
            other_pairs(t_a_up).swapaxes(1, 2),
            other_pairs(t_b_up),
            other_pairs(t_a_dn).swapaxes(1, 2),
            other_pairs(t_b_dn),
        )

    return body


def solution(mesh):
    sizes = (mesh.shape["rep"], mesh.shape["grp"], mesh.shape["fs"])
    rows_in = P("rep", "fs", "grp", None)
    conts_in = P("rep", "fs", "grp", None, None)
    weight = P(("grp", "fs"), None)
    return jax.shard_map(
        make_body(sizes),
        mesh=mesh,
        in_specs=(
            rows_in,
            conts_in,
            P("rep", "fs"),
            P("rep", "fs", "grp"),
            P(),
            P(),
            P(),
            P(),
            weight,
            weight,
            weight,
            weight,
            P(),
            P(),
            P(),
            P(),
            P(),
            P(),
            rows_in,
            conts_in,
        ),
        out_specs=(
            rows_in,
            conts_in,
            rows_in,
            conts_in,
            P("fs", None, None, None),
            P("fs", None, None, None),
            P("fs", None, None),
            P("fs", None, None),
            P("fs", None, None),
            P("fs", None, None),
        ),
        check_vma=False,
    )
```

```python
import functools
import math

import jax
import jax.numpy as jnp
from jax import lax
from jax.experimental import pallas as pl
from jax.experimental.pallas import tpu as pltpu
from jax.sharding import PartitionSpec as P

HDIM = 128
RANK = 16
BLOCK = 512
PART = 256
AWAY = (40, 48)
ALONG = 40
SCALE = HDIM ** (-0.5)
NEG_FILL = -1e30
BF = jnp.bfloat16
F32 = jnp.float32
MESH = pl.DeviceIdType.MESH
ANY = pl.BlockSpec(memory_space=pl.ANY)
WHOLE = pl.BlockSpec(memory_space=pltpu.VMEM)
ROOM = 62 * 2**20


def mm(a, b):
    return jnp.dot(a, b, preferred_element_type=F32)


def mm_nt(a, b):
    return lax.dot_general(a, b, (((1,), (1,)), ((), ())), preferred_element_type=F32)


def mm_tn(a, b):
    return lax.dot_general(a, b, (((0,), (0,)), ((), ())), preferred_element_type=F32)


def norm_stats(values):
    center = values - jnp.mean(values, axis=-1, keepdims=True)
    spread = jnp.mean(center * center, axis=-1, keepdims=True)
    rstd = lax.rsqrt(spread + 1e-05)
    return center * rstd, rstd


def norm_back(values, gain, grad):
    hat, rstd = norm_stats(values)
    e = grad * gain
    return (
        e - jnp.mean(e, axis=-1, keepdims=True) - hat * jnp.mean(e * hat, axis=-1, keepdims=True)
    ) * rstd


def low_of(product, prompt_len):
    row = lax.broadcasted_iota(jnp.int32, product.shape, 0)
    col = lax.broadcasted_iota(jnp.int32, product.shape, 1)
    return jnp.where((row < prompt_len) == (col < RANK), product, 0.0).astype(BF)


class Gather:
    def __init__(self, n_fs, sources, dst, sems, lag=2):
        (self.zs, self.zr, self.ws, self.wr, self.ys, self.yr, self.xs, self.xr) = sems[:8]
        (self.cs, self.cr, self.ds, self.dr, self.loc) = sems[8:]
        self.nz, self.sources, self.dst = n_fs, sources, dst
        self.count, self.rows = dst.shape[0], dst.shape[2]
        self.lag, self.slots, self.last = lag, 2 * lag, n_fs + 2
        rep, grp = lax.axis_index("rep"), lax.axis_index("grp")
        self.z = lax.axis_index("fs")
        self.y, self.c, plane = grp // 2, grp % 2, rep % 2
        self.far_rep = rep + 1 - 2 * plane
        self.far_core = self.y * 2 + 1 - self.c
        self.far_row = (1 - self.y) * 2 + self.c
        self.own = grp * n_fs + self.z
        self.inner, self.outer, self.far = [], [], []
        for away in AWAY:
            stay = self.rows - away
            self.inner.append((pl.multiple_of(away * plane, 8), stay))
            self.outer.append((pl.multiple_of(stay * plane, 8), away))
            self.far.append((pl.multiple_of(stay * (1 - plane), 8), away))
        first, stay = self.inner[1]
        self.near = (first, stay - ALONG)
        self.along = (pl.multiple_of(first + stay - ALONG, 8), ALONG)

    @staticmethod
    def semaphores(n_fs, lag=2):
        slots, dma = 2 * lag, pltpu.SemaphoreType.DMA
        return (
            [dma((3 * slots, 2, n_fs)), dma((3 * slots, n_fs))]
            + [dma((3 * slots, n_fs))] * 2
            + [dma((slots, n_fs))] * 2
            + [dma((slots, 2 * n_fs))] * 6
            + [dma((slots,))]
        )

    def barrier(self):
        sem = pltpu.get_barrier_semaphore()

        def greet(**where):
            pl.semaphore_signal(sem, 1, device_id=where, device_id_type=MESH)

        greet(rep=self.far_rep)
        greet(grp=self.far_core)
        greet(grp=self.far_row)
        below, above = self.z > 0, self.z < self.nz - 1
        pl.when(below)(lambda: greet(fs=self.z - 1))
        pl.when(above)(lambda: greet(fs=self.z + 1))
        pl.semaphore_wait(sem, 3 + below.astype(jnp.int32) + above.astype(jnp.int32))

    def at_distance(self, d):
        if d < 0 or d >= self.nz:
            return []
        if d == 0:
            return [(None, self.z, 0)]
        return [(self.z >= d, self.z - d, 1), (self.z < self.nz - d, self.z + d, -1)]

    def crossing(self, d, ok, fs, way):
        if d < self.nz // 2:
            return [(ok, self.inner[1])]
        if d == self.nz - 1:
            return [(ok, self.near)]
        end = fs == (0 if way > 0 else self.nz - 1)
        inside = jnp.logical_not(end)
        return [(self.both(ok, inside), self.inner[1]), (self.both(ok, end), self.near)]

    @staticmethod
    def both(left, right):
        return right if left is None else jnp.logical_and(left, right)

    def shard(self, other, fs, core):
        row = 1 - self.y if other else self.y
        return (row * 2 + core) * self.nz + fs

    def send(self, j, shard, span, sems, src=None, **where):
        rows = pl.ds(*span)
        return pltpu.make_async_remote_copy(
            self.dst.at[j, shard, rows] if src is None else src(*span),
            self.dst.at[j, shard, rows],
            *sems,
            device_id=where,
            device_id_type=MESH,
        )

    def own_blocks(self, j):
        start = 0
        for count, ref in self.sources:
            ok = (j >= start) & (j < start + count) if len(self.sources) > 1 else None
            yield ok, functools.partial(ref, j - start)
            start += count

    def keeps(self, j, t):
        sem = self.loc.at[lax.rem(t, self.slots)]
        for ok, src in self.own_blocks(j):
            yield ok, pltpu.make_async_copy(src(0, self.rows), self.dst.at[j, self.own], sem)

    def sends(self, a, j, t):
        todo, nz = [], self.nz
        k, kz = lax.rem(t, self.slots), lax.rem(t, 3 * self.slots)

        def column(ok, fs, way, src):
            shard = self.shard(0, fs, self.c)
            if way >= 0:
                sems = (self.zs.at[kz, 0, fs], self.zr.at[kz, fs])
                up = self.send(j, shard, self.inner[0], sems, src, fs=self.z + 1)
                todo.append((self.both(ok, self.z < nz - 1), up))
            if way <= 0:
                sems = (self.zs.at[kz, 1, fs], self.zr.at[kz, fs])
                down = self.send(j, shard, self.inner[0], sems, src, fs=self.z - 1)
                todo.append((self.both(ok, self.z > 0), down))
            sems = (self.ys.at[k, fs], self.yr.at[k, fs])
            for ok_row, span in self.crossing(a, ok, fs, way):
                todo.append((ok_row, self.send(j, shard, span, sems, src, grp=self.far_row)))
            if way:
                sems = (self.xs.at[k, fs], self.xr.at[k, fs])
                todo.append((ok, self.send(j, shard, self.outer[0], sems, rep=self.far_rep)))
            sems = (self.cs.at[k, fs], self.cr.at[k, fs])
            span = self.inner[0] if way else (0, self.rows)
            todo.append((ok, self.send(j, shard, span, sems, src, grp=self.far_core)))

        if a == 0:
            for ok, src in self.own_blocks(j):
                column(ok, self.z, 0, src)
        else:
            for ok, fs, way in self.at_distance(a):
                column(ok, fs, way, None)
        for ok, fs, way in self.at_distance(a - 1):
            shard = self.shard(1, fs, self.c)
            sems = (self.xs.at[k, nz + fs], self.xr.at[k, nz + fs])
            todo.append((ok, self.send(j, shard, self.outer[1], sems, rep=self.far_rep)))
            sems = (self.cs.at[k, nz + fs], self.cr.at[k, nz + fs])
            todo.append((ok, self.send(j, shard, self.inner[1], sems, grp=self.far_core)))
            if nz // 2 <= a < nz:
                to = self.z + way
                ok = (fs == (0 if way > 0 else nz - 1)) & (to >= 0) & (to < nz)
                sems = (self.ws.at[kz, fs], self.wr.at[kz, fs])
                todo.append((ok, self.send(j, shard, self.along, sems, fs=to)))
        for other in (0, 1):
            for ok, fs, way in self.at_distance(a - 1 - other):
                if way or other:
                    i = other * nz + fs
                    sems = (self.ds.at[k, i], self.dr.at[k, i])
                    shard = self.shard(other, fs, self.c)
                    core = self.send(j, shard, self.far[other], sems, grp=self.far_core)
                    todo.append((ok, core))
        return todo

    def arrivals(self, a, j, t):
        todo, nz = [], self.nz
        k, kz = lax.rem(t, self.slots), lax.rem(t, 3 * self.slots)

        def expect(ok, shard, span, sem):
            ref = self.dst.at[j, shard, pl.ds(*span)]
            todo.append((ok, pltpu.make_async_copy(ref, ref, sem)))

        for ok, fs, way in self.at_distance(a):
            if way:
                expect(ok, self.shard(0, fs, self.c), self.inner[0], self.zr.at[kz, fs])
        for ok, fs, way in self.at_distance(a - 1):
            shard = self.shard(1, fs, self.c)
            for ok_row, span in self.crossing(a - 1, ok, fs, way):
                expect(ok_row, shard, span, self.yr.at[k, fs])
            if a - 1 >= nz // 2:
                end = self.both(ok, fs == (0 if way > 0 else nz - 1))
                expect(end, shard, self.along, self.wr.at[kz, fs])
        for other in (0, 1):
            inner, far = self.inner[other], self.far[other]
            for ok, fs, way in self.at_distance(a - 1 - other):
                i = other * nz + fs
                if way or other:
                    expect(ok, self.shard(other, fs, self.c), far, self.xr.at[k, i])
                span = inner if way or other else (0, self.rows)
                expect(ok, self.shard(other, fs, 1 - self.c), span, self.cr.at[k, i])
            for ok, fs, way in self.at_distance(a - 2 - other):
                if way or other:
                    i = other * nz + fs
                    expect(ok, self.shard(other, fs, 1 - self.c), far, self.dr.at[k, i])
        return todo

    def run(self, early=None, compute=None):
        lag = self.lag

        def act(ok, fn):
            if ok is None:
                fn()
            else:
                pl.when(ok)(fn)

        def finish(a, j, t):
            for ok, copy in self.sends(a - 1, j, t):
                act(ok, copy.wait_send)
            for ok, copy in self.arrivals(a, j, t):
                act(ok, copy.wait)
            if a == 1:
                for ok, copy in self.keeps(j, t):
                    act(ok, copy.wait)

        def begin(a, j, t):
            for ok, copy in self.sends(a, j, t):
                act(ok, copy.start)
            if a == 0:
                for ok, copy in self.keeps(j, t):
                    act(ok, copy.start)

        def tick(t, carry):
            for a in range(self.last, 0, -1):
                j = t - lag * a
                pl.when((j >= 0) & (j < self.count))(functools.partial(finish, a, j, t - lag))
            for a in range(self.last - 1, -1, -1):
                j = t - lag * a
                pl.when((j >= 0) & (j < self.count))(functools.partial(begin, a, j, t))
            if early is not None:
                early(t)
            if compute is not None:
                j = t - lag * self.last
                pl.when(j >= 0)(functools.partial(compute, j))
            return carry

        lax.fori_loop(0, self.count + lag * self.last + (compute is not None), tick, 0)


def head_columns(ref, rows, part, h, width):
    first = pl.multiple_of(part * width + h * HDIM, HDIM)
    return ref[rows, pl.ds(first, HDIM)]


def seen(shape, first):
    row = lax.broadcasted_iota(jnp.int32, shape, 0)
    return lax.broadcasted_iota(jnp.int32, shape, 1) <= first + row


def head_chances(qkv, kp, h, prompt_len, width, first):
    own, cont = slice(0, prompt_len), slice(prompt_len, None)
    q_p = head_columns(qkv, own, 0, h, width)
    q_c = head_columns(qkv, cont, 0, h, width)
    k_c = head_columns(qkv, cont, 1, h, width)
    v_c = head_columns(qkv, cont, 2, h, width)
    lanes = pl.ds(pl.multiple_of(h * HDIM, HDIM), HDIM)
    k_p = kp[:, :, lanes].reshape(-1, HDIM)
    lanes = pl.ds(pl.multiple_of(width + h * HDIM, HDIM), HDIM)
    v_p = kp[:, :, lanes].reshape(-1, HDIM)
    s_p = mm_nt(q_p, k_p) * SCALE
    s_p = jnp.where(seen(s_p.shape, first), s_p, NEG_FILL)
    e_p = jnp.exp(s_p - jnp.max(s_p, axis=-1, keepdims=True))
    c_p = e_p * (1.0 / jnp.sum(e_p, axis=-1, keepdims=True))
    s_1 = mm_nt(q_c, k_p) * SCALE
    s_2 = mm_nt(q_c, k_c) * SCALE
    s_2 = jnp.where(seen(s_2.shape, 0), s_2, NEG_FILL)
    peak = jnp.maximum(
        jnp.max(s_1, axis=-1, keepdims=True), jnp.max(s_2, axis=-1, keepdims=True)
    )
    e_1, e_2 = jnp.exp(s_1 - peak), jnp.exp(s_2 - peak)
    mass = jnp.sum(e_1, axis=-1, keepdims=True) + jnp.sum(e_2, axis=-1, keepdims=True)
    inv = 1.0 / mass
    return (q_p, q_c, k_p, k_c, v_p, v_c), (c_p, e_1 * inv, e_2 * inv)


def select_call(ids, tables):
    def kernel(ids, *refs):
        for src, dst in zip(refs[: len(tables)], refs[len(tables) :]):
            dst[...] = src[0]

    def spec_in(t):
        return pl.BlockSpec((1,) + t.shape[1:], lambda i, ids: (ids[i],) + (0,) * (t.ndim - 1))

    def spec_out(t):
        lead = t.ndim - 3
        return pl.BlockSpec(t.shape[1:], lambda i, ids: (0,) * lead + (i, 0))

    return pl.pallas_call(
        kernel,
        grid_spec=pltpu.PrefetchScalarGridSpec(
            num_scalar_prefetch=1,
            grid=(2,),
            in_specs=[spec_in(t) for t in tables],
            out_specs=[spec_out(t) for t in tables],
        ),
        out_shape=[
            jax.ShapeDtypeStruct(t.shape[1:-2] + (2 * RANK, t.shape[-1]), BF) for t in tables
        ],
        name="select",
    )(ids, *tables)


def columns_of(ref):
    return lambda j, first, size: ref.at[
        pl.ds(first, size), pl.ds(pl.multiple_of(j * PART, PART), PART)
    ]


def tiles_of(ref, shard_rows, parts):
    def tile(j, first, size):
        row = pl.multiple_of(lax.rem(j, parts) * shard_rows + first, 8)
        return ref.at[pl.ds(row, size), pl.ds(pl.multiple_of(j // parts * PART, PART), PART)]

    return tile


def pair_loads(blocks, first, wbuf, wsem, k):
    return [
        pltpu.make_async_copy(
            blocks.at[first + i], wbuf.at[k, :, :, pl.ds(i * PART, PART)], wsem.at[k, i]
        )
        for i in range(2)
    ]


PIECES = 8


def pack(out, unit, piece, value):
    value = value.astype(BF)
    for n in range(PIECES):
        out[n, :, unit * piece : (unit + 1) * piece] = value[:, n * piece : (n + 1) * piece]


def forward_call(x_p, x_c, cot_p, cot_c, norms, tables, weights, n_fs, n_shard):
    prompt_len, width = x_p.shape
    rows = prompt_len + x_c.shape[0]
    shard_rows, hidden = weights[3].shape
    parts = weights[2].shape[0] // shard_rows
    n_qkv, n_out, n_up = 3 * width // PART, width // PART, hidden // PART
    n_dn = n_out * parts
    before_up = n_qkv + n_out + n_dn
    count = before_up + n_up
    n_grp = n_shard // n_fs
    heads = width // HDIM
    per = width // BLOCK
    piece = width // PIECES
    lag = 2
    t_onward, t_low = 6, 12
    t_head = n_qkv + lag * (n_fs + 2) + 1
    t_out = t_head + heads
    t_norm = t_out + per

    def kernel(x_p, x_c, gain_one, bias_one, gain_two, bias_two, *refs):
        (a_ext, b_ext, a_up, b_up, a_dn, b_dn), refs = refs[:6], refs[6:]
        (cot_p, cot_c), src, refs = refs[:2], refs[2:6], refs[6:]
        (dst, qkv_out, kp_out, normed_out, mixed_out), refs = refs[:5], refs[5:]
        (lows, res_p, res_c, resid_back, grad_attn, low_o), refs = refs[:6], refs[6:]
        packed, refs = refs[0], refs[1:]
        (qkv, kp, group, low_group, normed_one, normed, mixed, cot, resid, out_acc), refs = refs[:10], refs[10:]
        (low_up, dlow_dn, low_dn, dlow_up, wbuf, dbuf), refs = refs[:6], refs[6:]
        (wsem, dsem, ksend, krecv, lsem), sems = refs[:5], refs[5:]
        own, rest = slice(0, prompt_len), slice(prompt_len, None)
        sources = [
            (n_qkv, columns_of(src[0])),
            (n_out, columns_of(src[1])),
            (n_dn, tiles_of(src[2], shard_rows, parts)),
            (n_up, columns_of(src[3])),
        ]
        engine = Gather(n_fs, sources, dst, sems, lag)
        engine.barrier()
        grp = lax.axis_index("grp")
        loads = [
            pltpu.make_async_copy(cot_p, cot.at[pl.ds(0, prompt_len)], lsem.at[0]),
            pltpu.make_async_copy(cot_c, cot.at[pl.ds(prompt_len, rows - prompt_len)], lsem.at[1]),
        ]
        stores = [
            pltpu.make_async_copy(qkv, qkv_out, lsem.at[2]),
            pltpu.make_async_copy(kp, kp_out, lsem.at[3]),
            pltpu.make_async_copy(normed_one, normed_out, lsem.at[4]),
            pltpu.make_async_copy(mixed, mixed_out, lsem.at[5]),
        ]

        def pass_on(n, whose, to):
            return pltpu.make_async_remote_copy(
                group.at[whose],
                group.at[whose],
                ksend.at[n],
                krecv.at[n],
                device_id={"grp": to},
                device_id_type=MESH,
            )

        def landed(n, whose):
            return pltpu.make_async_copy(group.at[whose], group.at[whose], krecv.at[n])

        to_row = pass_on(0, grp, engine.far_row)
        to_core = pass_on(1, grp, engine.far_core)
        onward = pass_on(2, engine.far_row, engine.far_core)
        diagonal = (1 - engine.y) * 2 + 1 - engine.c

        def early(t):
            @pl.when(t == 0)
            def _():
                for copy in loads:
                    copy.start()
                for x, part in ((x_p, own), (x_c, rest)):
                    hat, _ = norm_stats(x[...].astype(F32))
                    normed_one[part] = (hat * gain_one[...] + bias_one[...]).astype(BF)
                    if part == own:
                        group[grp] = normed_one[part]
                        to_row.start()
                        to_core.start()
                for n in range(3):
                    lows[n] = low_of(mm_nt(normed_one[...], a_ext[n]), prompt_len)
                for copy in loads:
                    copy.wait()
                dlow_dn[...] = low_of(mm_nt(cot[...], b_dn[...]), prompt_len)

            @pl.when(t == t_onward)
            def _():
                landed(0, engine.far_row).wait()
                onward.start()

            @pl.when(t == t_low)
            def _():
                landed(1, engine.far_core).wait()
                landed(2, diagonal).wait()
                to_row.wait_send()
                to_core.wait_send()
                onward.wait_send()
                for n in range(2):
                    low = mm_nt(group[...].reshape(-1, width), a_ext[1 + n, :RANK])
                    low_group[n] = low.astype(BF)

            @pl.when(t == t_head)
            def _():
                for n in range(3):
                    stores[n].start()

            @pl.when((t >= t_head) & (t < t_out))
            def _():
                h = t - t_head
                (_, _, _, _, v_p, v_c), (c_p, c_1, c_2) = head_chances(
                    qkv, kp, h, prompt_len, width, grp * prompt_len
                )
                lanes = pl.ds(pl.multiple_of(h * HDIM, HDIM), HDIM)
                mixed[own, lanes] = mm(c_p.astype(BF), v_p).astype(BF)
                mixed[rest, lanes] = (mm(c_1.astype(BF), v_p) + mm(c_2.astype(BF), v_c)).astype(BF)

            def load_out(b):
                return pair_loads(dst, n_qkv + 2 * b, wbuf, wsem, lax.rem(b, 2))

            @pl.when(t == t_out - 1)
            def _():
                for copy in load_out(0):
                    copy.start()

            @pl.when((t >= t_out) & (t < t_norm))
            def _():
                b = t - t_out

                @pl.when(b == 0)
                def _():
                    stores[3].start()
                    low_o[...] = low_of(mm_nt(mixed[...], a_ext[3]), prompt_len)

                for copy in load_out(b):
                    copy.wait()

                @pl.when(b + 1 < per)
                def _():
                    for copy in load_out(b + 1):
                        copy.start()

                cols = pl.ds(pl.multiple_of(b * BLOCK, BLOCK), BLOCK)
                w = wbuf[lax.rem(b, 2)].reshape(-1, BLOCK)
                branch = mm(mixed[...], w) + mm(low_o[...], b_ext[3, :, cols])
                resid[own, cols] = x_p[:, cols].astype(F32) + branch[own]
                resid[rest, cols] = x_c[:, cols].astype(F32) + branch[rest]

            @pl.when(t == t_norm)
            def _():
                hat, _ = norm_stats(resid[...])
                normed[...] = (hat * gain_two[...] + bias_two[...]).astype(BF)
                low_up[...] = low_of(mm_nt(normed[...], a_up[...]), prompt_len)
                out_acc[...] = resid[...]
                resid_back[...] = jnp.zeros_like(resid_back)
                low_dn[...] = jnp.zeros_like(low_dn)
                dlow_up[...] = jnp.zeros_like(dlow_up)

        def load(j):
            k, i = lax.rem(j // 2, 2), lax.rem(j, 2)
            into = wbuf.at[k, :, :, pl.ds(pl.multiple_of(i * PART, PART), PART)]
            return pltpu.make_async_copy(dst.at[j], into, wsem.at[k, i])

        def load_down(n):
            k = lax.rem(n, 2)
            return [
                pltpu.make_async_copy(
                    dst.at[pl.ds(n_qkv + n_out + b * parts, parts), n],
                    dbuf.at[k, :, :, pl.ds(b * PART, PART)],
                    dsem.at[k, b],
                )
                for b in range(n_out)
            ]

        def compute(j):
            n = j - before_up

            @pl.when((j < n_qkv) | ((n >= 0) & (n < n_up)))
            def _():
                load(j).start()

            @pl.when((n >= 0) & (n < n_up) & (lax.rem(j, 2) == 0))
            def _():
                for copy in load_down(n // 2):
                    copy.start()

            @pl.when((j > 0) & (j <= n_qkv) & (lax.rem(j, 2) == 0))
            def _():
                i = j // 2 - 1
                for first in (j - 2, j - 1):
                    load(first).wait()
                w = wbuf[lax.rem(i, 2)].reshape(-1, BLOCK)
                m = i // per
                inside = pl.ds(pl.multiple_of(lax.rem(i, per) * BLOCK, BLOCK), BLOCK)
                cols = pl.ds(pl.multiple_of(i * BLOCK, BLOCK), BLOCK)

                @pl.when(m == 0)
                def _():
                    extra = mm(lows[0], b_ext[0, :, inside])
                    qkv[:, cols] = (mm(normed_one[...], w) + extra).astype(BF)

                @pl.when(m > 0)
                def _():
                    extra = mm(lows[m, rest], b_ext[m, :, inside])
                    qkv[rest, cols] = (mm(normed_one[rest], w) + extra).astype(BF)
                    extra = mm(low_group[m - 1], b_ext[m, :RANK, inside])
                    shared = (mm(group[...].reshape(-1, width), w) + extra).astype(BF)
                    there = pl.ds(pl.multiple_of((i - per) * BLOCK, BLOCK), BLOCK)
                    kp[:, :, there] = shared.reshape(n_grp, prompt_len, BLOCK)

            @pl.when((n > 0) & (lax.rem(j, 2) == 0))
            def _():
                i = n // 2 - 1
                for first in (j - 2, j - 1):
                    load(first).wait()
                for copy in load_down(i):
                    copy.wait()
                cols = pl.ds(pl.multiple_of(i * BLOCK, BLOCK), BLOCK)
                w_up = wbuf[lax.rem(j // 2 - 1, 2)].reshape(-1, BLOCK)
                w_dn = dbuf[lax.rem(i, 2)].reshape(BLOCK, width)
                a_d, b_u = a_dn[:, cols], b_up[:, cols]
                pre = mm(normed[...], w_up) + mm(low_up[...], b_u)
                cdf = 0.5 * (1.0 + lax.erf(pre * math.sqrt(0.5)))
                act = (pre * cdf).astype(BF)
                slope = cdf + pre * jnp.exp(-0.5 * pre * pre) * (1.0 / math.sqrt(2.0 * math.pi))
                grad_act = mm_nt(cot[...], w_dn) + mm(dlow_dn[...], a_d)
                grad_pre = (grad_act * slope).astype(BF)
                out_acc[...] += mm(act, w_dn)
                resid_back[...] += mm_nt(grad_pre, w_up)
                low_dn[...] += mm_nt(act, a_d)
                dlow_up[...] += mm_nt(grad_pre, b_u)
                wide = hidden // width
                for base, grad in (
                    (0, mm_tn(low_up[...], grad_pre).astype(BF)),
                    (wide, mm_tn(dlow_dn[...], act).astype(BF)),
                ):
                    unit = pl.ds(pl.multiple_of((base + i // per) * piece, piece), piece)
                    for m in range(BLOCK // piece):
                        where = lax.rem(i, per) * (BLOCK // piece) + m
                        packed[where, :, unit] = grad[:, m * piece : (m + 1) * piece]

        engine.run(early, compute)
        dlow = low_of(dlow_up[...], prompt_len)
        pack(packed, 2 * (hidden // width), piece, mm_tn(dlow, normed[...]))
        grad = resid_back[...] + mm(dlow, a_up[...])
        grad = cot[...].astype(F32) + norm_back(resid[...], gain_two[...], grad)
        resid_back[...] = grad
        grad_attn[...] = grad.astype(BF)
        low = low_of(low_dn[...], prompt_len)
        result = (out_acc[...] + mm(low, b_dn[...])).astype(BF)
        res_p[...] = result[own]
        res_c[...] = result[rest]
        pack(packed, 2 * (hidden // width) + 1, piece, mm_tn(low, cot[...]))
        for copy in stores:
            copy.wait()

    like = jax.ShapeDtypeStruct
    two = 2 * RANK
    dma = pltpu.SemaphoreType.DMA
    share = (n_grp, prompt_len, 2 * width)
    return pl.pallas_call(
        kernel,
        out_shape=[
            like((count, n_shard, shard_rows, PART), BF),
            like((rows, 3 * width), BF),
            like(share, BF),
            like((rows, width), BF),
            like((rows, width), BF),
            like((3, rows, two), BF),
            like(x_p.shape, BF),
            like(x_c.shape, BF),
            like((rows, width), F32),
            like((rows, width), BF),
            like((rows, two), BF),
            like((PIECES, two, (2 * (hidden // width) + 2) * piece), BF),
        ],
        in_specs=[WHOLE] * 12 + [ANY] * 6,
        out_specs=[ANY] * 5 + [WHOLE] * 7,
        scratch_shapes=[
            pltpu.VMEM((rows, 3 * width), BF),
            pltpu.VMEM(share, BF),
            pltpu.VMEM((n_grp, prompt_len, width), BF),
            pltpu.VMEM((2, n_grp * prompt_len, RANK), BF),
            pltpu.VMEM((rows, width), BF),
            pltpu.VMEM((rows, width), BF),
            pltpu.VMEM((rows, width), BF),
            pltpu.VMEM((rows, width), BF),
            pltpu.VMEM((rows, width), F32),
            pltpu.VMEM((rows, width), F32),
            pltpu.VMEM((rows, two), BF),
            pltpu.VMEM((rows, two), BF),
            pltpu.VMEM((rows, two), F32),
            pltpu.VMEM((rows, two), F32),
            pltpu.VMEM((2, n_shard, shard_rows, BLOCK), BF),
            pltpu.VMEM((2, parts, shard_rows, width), BF),
            dma((2, 2)),
            dma((2, n_out)),
            dma((3,)),
            dma((3,)),
            dma((6,)),
        ]
        + Gather.semaphores(n_fs, lag),
        compiler_params=pltpu.CompilerParams(
            collective_id=0, has_side_effects=True, vmem_limit_bytes=ROOM
        ),
        name="forward",
    )(x_p, x_c, *norms, *tables, cot_p, cot_c, *weights)


class TableSum:
    def __init__(self, n_fs, hots, units, bufs, sems, stepwise):
        self.n_fs, self.hots, self.units, self.stepwise = n_fs, hots, units, stepwise
        self.out, self.got, self.dense, self.parts, self.sums = bufs
        (self.s1, self.r1, self.s2, self.r2, self.s3, self.r3) = sems
        rep, self.grp = lax.axis_index("rep"), lax.axis_index("grp")
        self.z = lax.axis_index("fs")
        plane = rep % 2
        y, c = self.grp // 2, self.grp % 2
        self.me = plane * 4 + self.grp
        self.peers = []
        for q in range(1, PIECES):
            x_to = 1 - plane if q // 4 else plane
            y_to = 1 - y if q // 2 % 2 else y
            c_to = 1 - c if q % 2 else c
            where = {"grp": y_to * 2 + c_to}
            if q // 4:
                where["rep"] = rep + 1 - 2 * plane
            self.peers.append((q, x_to * 4 + y_to * 2 + c_to, where))
        self.piece = self.out.shape[2] // units

    @staticmethod
    def scratch(n_fs, units, piece, count):
        two, wide = 2 * RANK, units * piece
        rows = count * RANK // n_fs
        bufs = [
            pltpu.VMEM((PIECES, two, wide), BF),
            pltpu.VMEM((PIECES, two, wide), BF),
            pltpu.VMEM((n_fs, rows, wide), BF),
            pltpu.VMEM((n_fs, rows, wide), BF),
            pltpu.VMEM((PIECES, rows, wide), BF),
        ]
        dma = pltpu.SemaphoreType.DMA
        return bufs, [dma((PIECES,))] * 2 + [dma((n_fs,))] * 2 + [dma((PIECES,))] * 2

    def pack(self, unit, value):
        pack(self.out, unit, self.piece, value)

    def exchange(self):
        return [
            pltpu.make_async_remote_copy(
                self.out.at[to],
                self.got.at[self.me],
                self.s1.at[q],
                self.r1.at[q],
                device_id=where,
                device_id_type=MESH,
            )
            for q, to, where in self.peers
        ]

    def along_fs(self):
        copies = []
        for d in range(1, self.n_fs):
            to = lax.rem(self.z + d, self.n_fs)
            copies.append(
                pltpu.make_async_remote_copy(
                    self.dense.at[to],
                    self.parts.at[self.z],
                    self.s2.at[d],
                    self.r2.at[d],
                    device_id={"fs": to},
                    device_id_type=MESH,
                )
            )
        return copies

    def hand(self, n, whose, q):
        return pltpu.make_async_remote_copy(
            self.sums.at[whose],
            self.sums.at[whose],
            self.s3.at[n],
            self.r3.at[n],
            device_id=self.peers[q - 1][2],
            device_id_type=MESH,
        )

    def hand_out(self):
        return [self.hand(q, self.me, q) for q, _, _ in self.peers]

    def relay(self, stage):
        far_row, far_rep, both = (self.peers[q - 1][1] for q in (2, 4, 6))
        steps = [
            [(4, self.me, 4), (2, self.me, 2), (1, self.me, 1)],
            [(6, far_rep, 2), (5, far_rep, 1), (3, far_row, 1)],
            [(7, both, 1)],
        ]
        return [self.hand(*step) for step in steps[stage]]

    def arrived(self, q):
        ref = self.sums.at[self.peers[q - 1][1]]
        pltpu.make_async_copy(ref, ref, self.r3.at[q]).wait()

    def first(self):
        for copy in self.exchange():
            copy.start()
        self.got[self.me] = self.out[self.me]

    def second(self):
        for q, whose, _ in self.peers:
            ref = self.got.at[whose]
            pltpu.make_async_copy(ref, ref, self.r1.at[q]).wait()
        for copy in self.exchange():
            copy.wait_send()
        wide = self.out.shape[2]
        hots = self.hots[...].reshape(PIECES * 2 * RANK, -1)
        dense = mm_tn(hots, self.got[...].reshape(PIECES * 2 * RANK, wide))
        self.dense[...] = dense.astype(BF).reshape(self.dense.shape)
        for copy in self.along_fs():
            copy.start()
        self.parts[self.z] = self.dense[self.z]

    def third(self):
        for d in range(1, self.n_fs):
            ref = self.parts.at[lax.rem(self.z + self.n_fs - d, self.n_fs)]
            pltpu.make_async_copy(ref, ref, self.r2.at[d]).wait()
        for copy in self.along_fs():
            copy.wait_send()
        total = self.parts[0].astype(F32)
        for n in range(1, self.n_fs):
            total = total + self.parts[n].astype(F32)
        self.sums[self.me] = total.astype(BF)
        if not self.stepwise:
            for copy in self.hand_out():
                copy.start()
            return
        for copy in self.relay(0):
            copy.start()

    def fourth(self):
        self.arrived(4)
        self.arrived(2)
        for copy in self.relay(1):
            copy.start()

    def fifth(self):
        self.arrived(6)
        for copy in self.relay(2):
            copy.start()

    def last(self, places):
        if self.stepwise:
            for q in (1, 3, 5, 7):
                self.arrived(q)
            sent = self.relay(0) + self.relay(1) + self.relay(2)
        else:
            for q, _, _ in self.peers:
                self.arrived(q)
            sent = self.hand_out()
        for copy in sent:
            copy.wait_send()
        for unit, place in enumerate(places):
            for k in range(PIECES):
                cols = slice(unit * self.piece, (unit + 1) * self.piece)
                for a in range(self.sums.shape[1] // RANK):
                    value = self.sums[k, a * RANK : (a + 1) * RANK, cols]
                    place(a, k * self.piece, value)


def back_call(
    grad_attn, mixed, low_o, lows, gain, a_ext, b_ext, hot, packed, qkv, kp, x_p, x_c, normed, grad_resid, w_all, n_fs, count
):
    rows, width = grad_attn.shape
    prompt_len, cont_len = x_p.shape[0], x_c.shape[0]
    heads = width // HDIM
    n_grp = kp.shape[0]
    n_shard, shard_rows = w_all.shape[1:3]
    per = width // BLOCK
    n_qkv = 3 * per
    piece = width // PIECES
    adapters = count // n_fs
    groups = 4
    group_heads = heads // groups
    half = group_heads * HDIM
    two = 2 * RANK
    first_units = packed.shape[2] // piece
    wide_units = first_units // 2 - 1
    hidden = wide_units * width
    last_units = 4

    def kernel(*refs):
        (grad_attn, mixed, low_o, lows, gain, a_ext, b_ext, hot), refs = refs[:8], refs[8:]
        packed, refs = refs[0], refs[1:]
        (qkv, kp, x_p, x_c, normed, grad_resid, w_all), refs = refs[:7], refs[7:]
        (out_p, out_c, t_a, t_b, t_a_up, t_b_up, t_a_dn, t_b_dn), refs = refs[:8], refs[8:]
        (grads, keep, late, x, normed_here, wbuf, gm, acc, dlow, dlow_o), refs = refs[:10], refs[10:]
        (far, far_core, far_row, hots), refs = refs[:4], refs[4:]
        bufs_one, bufs_mid, bufs_two, refs = (packed, *refs[:4]), refs[4:9], refs[9:14], refs[14:]
        sems_one, sems_mid, sems_two, refs = refs[:6], refs[6:12], refs[12:18], refs[18:]
        lsem, wsem, csend, crecv, rsend, rrecv, hsend, hrecv = refs
        grp = lax.axis_index("grp")
        y, c = grp // 2, grp % 2
        own, rest = slice(0, prompt_len), slice(prompt_len, None)
        one = TableSum(n_fs, hots, first_units, bufs_one, sems_one, True)
        mid = TableSum(n_fs, hots, last_units, bufs_mid, sems_mid, True)
        two_ = TableSum(n_fs, hots, last_units, bufs_two, sems_two, False)
        barrier = pltpu.get_barrier_semaphore()
        for _, _, where in one.peers:
            pl.semaphore_signal(barrier, 1, device_id=where, device_id_type=MESH)
        for d in range(1, n_fs):
            to = lax.rem(one.z + d, n_fs)
            pl.semaphore_signal(barrier, 1, device_id={"fs": to}, device_id_type=MESH)

        loads = [
            pltpu.make_async_copy(src, dst, lsem.at[n])
            for n, (src, dst) in enumerate(
                [
                    (qkv, grads),
                    (kp, keep),
                    (grad_resid, late),
                    (normed, normed_here),
                    (x_p, x.at[pl.ds(0, prompt_len)]),
                    (x_c, x.at[pl.ds(prompt_len, cont_len)]),
                ]
            )
        ]
        for copy in loads:
            copy.start()

        def load_w(i, k):
            for copy in pair_loads(w_all, 2 * i, wbuf, wsem, k):
                copy.start()

        def wait_w(i, k):
            for copy in pair_loads(w_all, 2 * i, wbuf, wsem, k):
                copy.wait()

        load_w(n_qkv, 0)
        pl.semaphore_wait(barrier, len(one.peers) + n_fs - 1)

        hots[one.me] = hot[...]
        hot_sends = [
            pltpu.make_async_remote_copy(
                hots.at[one.me],
                hots.at[one.me],
                hsend.at[q],
                hrecv.at[q],
                device_id=where,
                device_id_type=MESH,
            )
            for q, _, where in one.peers
        ]
        for copy in hot_sends:
            copy.start()
        one.first()
        dlow_o[...] = low_of(mm_nt(grad_attn[...], b_ext[3]), prompt_len)
        mid.pack(0, mm_tn(dlow_o[...], mixed[...]))
        mid.pack(1, mm_tn(low_o[...], grad_attn[...]))

        acc[...] = mm(dlow_o[...], a_ext[3])
        for n in range(per):
            wait_w(n_qkv + n, n % 2)
            if n + 1 < per:
                load_w(n_qkv + n + 1, (n + 1) % 2)
            w = wbuf[n % 2].reshape(-1, BLOCK)
            acc[...] += mm_nt(grad_attn[:, n * BLOCK : (n + 1) * BLOCK], w)
        gm[...] = acc[...].astype(BF)
        load_w(0, 0)
        load_w(1, 1)

        loads[0].wait()
        loads[1].wait()

        def head(part, n, carry):
            h = part * group_heads + n
            first = grp * prompt_len
            (q_p, q_c, k_p, k_c, v_p, v_c), (c_p, c_1, c_2) = head_chances(
                grads, keep, h, prompt_len, width, first
            )
            lanes = [
                pl.ds(pl.multiple_of(i * width + h * HDIM, HDIM), HDIM) for i in range(3)
            ]
            gm_p, gm_c = gm[own, lanes[0]], gm[rest, lanes[0]]
            d_p = mm_nt(gm_p, v_p)
            d_1, d_2 = mm_nt(gm_c, v_p), mm_nt(gm_c, v_c)
            s_p = (c_p * (d_p - jnp.sum(c_p * d_p, axis=-1, keepdims=True))).astype(BF)
            inner = jnp.sum(c_1 * d_1, axis=-1, keepdims=True) + jnp.sum(
                c_2 * d_2, axis=-1, keepdims=True
            )
            s_1 = (c_1 * (d_1 - inner)).astype(BF)
            s_2 = (c_2 * (d_2 - inner)).astype(BF)
            grads[own, lanes[0]] = (mm(s_p, k_p) * SCALE).astype(BF)
            grads[rest, lanes[0]] = ((mm(s_1, k_p) + mm(s_2, k_c)) * SCALE).astype(BF)
            grads[rest, lanes[1]] = (mm_tn(s_2, q_c) * SCALE).astype(BF)
            grads[rest, lanes[2]] = mm_tn(c_2.astype(BF), gm_c).astype(BF)
            g_k = ((mm_tn(s_p, q_p) + mm_tn(s_1, q_c)) * SCALE).astype(BF)
            g_v = (mm_tn(c_p.astype(BF), gm_p) + mm_tn(c_1.astype(BF), gm_c)).astype(BF)
            into = [pl.ds(pl.multiple_of(i * half + n * HDIM, HDIM), HDIM) for i in range(2)]
            far[part, :, :, into[0]] = g_k.reshape(n_grp, prompt_len, HDIM)
            far[part, :, :, into[1]] = g_v.reshape(n_grp, prompt_len, HDIM)
            return carry

        def to_core(part):
            return [
                pltpu.make_async_remote_copy(
                    far.at[part, row * 2 + 1 - c],
                    far_core.at[part, row],
                    csend.at[part, row],
                    crecv.at[part, row],
                    device_id={"grp": y * 2 + 1 - c},
                    device_id_type=MESH,
                )
                for row in range(2)
            ]

        def to_row(part):
            return pltpu.make_async_remote_copy(
                far.at[part, (1 - y) * 2 + c],
                far_row.at[part],
                rsend.at[part],
                rrecv.at[part],
                device_id={"grp": (1 - y) * 2 + c},
                device_id_type=MESH,
            )

        def add_core(part):
            for copy in to_core(part):
                copy.wait()
            for row in range(2):
                total = far[part, row * 2 + c].astype(F32) + far_core[part, row].astype(F32)
                far[part, row * 2 + c] = total.astype(BF)
            to_row(part).start()

        def add_row(part):
            to_row(part).wait()
            total = far[part, grp].astype(F32) + far_row[part].astype(F32)
            total = total.astype(BF)
            for i in range(2):
                cols = slice((i + 1) * width + part * half, (i + 1) * width + (part + 1) * half)
                grads[own, cols] = total[:, i * half : (i + 1) * half]

        def half_group(i, carry):
            part = i // 2

            @pl.when((lax.rem(i, 2) == 1) & (part > 0))
            def _():
                add_core(part - 1)

            first = lax.rem(i, 2) * (group_heads // 2)
            lax.fori_loop(first, first + group_heads // 2, functools.partial(head, part), 0)

            @pl.when(lax.rem(i, 2) == 1)
            def _():
                for copy in to_core(part):
                    copy.start()

            @pl.when(i == 1)
            def _():
                for copy in hot_sends:
                    copy.wait_send()
                for q, whose, _ in one.peers:
                    pltpu.make_async_copy(hots.at[whose], hots.at[whose], hrecv.at[q]).wait()
                one.second()

            return carry

        lax.fori_loop(0, 2 * groups, half_group, 0)

        def tables(i, into, first):
            part = grads[:, i * width : (i + 1) * width]
            low = low_of(mm_nt(part, b_ext[i]), prompt_len)
            into.pack(first, mm_tn(low, normed_here[...]))
            into.pack(first + 1, mm_tn(lows[i], part))
            dlow[i] = low

        def project(n, carry):
            k = lax.rem(n, 2)
            wait_w(n, k)
            part = grads[:, pl.ds(pl.multiple_of(n * BLOCK, BLOCK), BLOCK)]
            acc[...] += mm_nt(part, wbuf[k].reshape(-1, BLOCK))

            @pl.when(n + 2 < n_qkv)
            def _():
                load_w(n + 2, k)

            return carry

        loads[3].wait()
        add_core(groups - 1)
        tables(0, mid, 2)
        mid.first()
        acc[...] = mm(dlow[0], a_ext[0])
        lax.fori_loop(0, per, project, 0)
        for part in range(groups):
            add_row(part)
        tables(1, two_, 0)
        tables(2, two_, 2)
        two_.first()
        mid.second()
        one.third()
        acc[...] += mm(dlow[1], a_ext[1]) + mm(dlow[2], a_ext[2])

        def project_more(n, carry):
            pl.when(n == 2 * per + 1)(two_.second)
            return project(n, carry)

        lax.fori_loop(per, n_qkv, project_more, 0)
        mid.third()
        one.fourth()
        for copy in (loads[2], loads[4], loads[5]):
            copy.wait()
        back = late[...] + norm_back(x[...].astype(F32), gain[...], acc[...])
        back = back.astype(BF)
        out_p[...] = back[own]
        out_c[...] = back[rest]

        def whole(ref, first):
            def place(a, col, value):
                ref[a, :, first + col : first + col + piece] = value

            return place

        def one_map(ref, n):
            def place(a, col, value):
                ref[a, n, :, col : col + piece] = value

            return place

        two_.third()
        one.fifth()
        mid.fourth()
        mid.fifth()
        one.last(
            [whole(t_b_up, n * width) for n in range(wide_units)]
            + [whole(t_a_dn, n * width) for n in range(wide_units)]
            + [whole(t_a_up, 0), whole(t_b_dn, 0)]
        )
        mid.last([one_map(t_a, 3), one_map(t_b, 3), one_map(t_a, 0), one_map(t_b, 0)])
        two_.last([one_map(t_a, 1), one_map(t_b, 1), one_map(t_a, 2), one_map(t_b, 2)])

    like = jax.ShapeDtypeStruct
    bufs_one, sems_one = TableSum.scratch(n_fs, first_units, piece, count)
    bufs_mid, sems_mid = TableSum.scratch(n_fs, last_units, piece, count)
    bufs_two, sems_two = TableSum.scratch(n_fs, last_units, piece, count)
    dma = pltpu.SemaphoreType.DMA
    return pl.pallas_call(
        kernel,
        out_shape=[
            like(x_p.shape, BF),
            like(x_c.shape, BF),
            like((adapters, 4, RANK, width), BF),
            like((adapters, 4, RANK, width), BF),
            like((adapters, RANK, width), BF),
            like((adapters, RANK, hidden), BF),
            like((adapters, RANK, hidden), BF),
            like((adapters, RANK, width), BF),
        ],
        in_specs=[WHOLE] * 9 + [ANY] * 7,
        out_specs=[WHOLE] * 8,
        scratch_shapes=[
            pltpu.VMEM((rows, 3 * width), BF),
            pltpu.VMEM(kp.shape, BF),
            pltpu.VMEM((rows, width), F32),
            pltpu.VMEM((rows, width), BF),
            pltpu.VMEM((rows, width), BF),
            pltpu.VMEM((2, n_shard, shard_rows, BLOCK), BF),
            pltpu.VMEM((rows, width), BF),
            pltpu.VMEM((rows, width), F32),
            pltpu.VMEM((3, rows, two), BF),
            pltpu.VMEM((rows, two), BF),
            pltpu.VMEM((groups, n_grp, prompt_len, 2 * half), BF),
            pltpu.VMEM((groups, 2, prompt_len, 2 * half), BF),
            pltpu.VMEM((groups, prompt_len, 2 * half), BF),
            pltpu.VMEM((PIECES,) + hot.shape, BF),
        ]
        + bufs_one[1:]
        + bufs_mid
        + bufs_two
        + sems_one
        + sems_mid
        + sems_two
        + [dma((6,)), dma((2, 2)), dma((groups, 2)), dma((groups, 2)), dma((groups,)), dma((groups,))]
        + [dma((PIECES,)), dma((PIECES,))],
        compiler_params=pltpu.CompilerParams(
            collective_id=2, has_side_effects=True, vmem_limit_bytes=ROOM
        ),
        name="back",
    )(
        grad_attn, mixed, low_o, lows, gain, a_ext, b_ext, hot, packed,
        qkv, kp, x_p, x_c, normed, grad_resid, w_all,
    )


def finish_call(rows, tables):
    steps = (2, 4)

    def kernel(*refs):
        for src, dst in zip(refs[: len(refs) // 2], refs[len(refs) // 2 :]):
            dst[...] = src[...].astype(dst.dtype)

    def row_spec(v):
        return pl.BlockSpec((v.shape[0] // 8, v.shape[1]), lambda a, n: (a * 4 + n, 0))

    def table_spec(v):
        if v.ndim == 4:
            return pl.BlockSpec((1, 1) + v.shape[2:], lambda a, n: (a, n, 0, 0))
        return pl.BlockSpec((1, v.shape[1], v.shape[2] // 4), lambda a, n: (a, 0, n))

    specs = [row_spec(v) for v in rows] + [table_spec(v) for v in tables]
    return pl.pallas_call(
        kernel,
        grid=steps,
        in_specs=specs,
        out_specs=specs,
        out_shape=[jax.ShapeDtypeStruct(v.shape, BF) for v in rows]
        + [jax.ShapeDtypeStruct(v.shape, F32) for v in tables],
        name="finish",
    )(*rows, *tables)


def make_body(sizes):
    n_rep, n_grp, n_fs = sizes
    n_shard = n_grp * n_fs

    def other_pairs(v):
        step = 2
        while step < n_rep:
            far = lax.ppermute(v, "rep", [(i, i ^ step) for i in range(n_rep)])
            v = (v.astype(F32) + far.astype(F32)).astype(BF)
            step *= 2
        return v

    def body(
        prompt_input_rows,
        continuation_input,
        prompt_group_adapter,
        continuation_adapter,
        first_norm_scale,
        first_norm_bias,
        second_norm_scale,
        second_norm_bias,
        frozen_query_key_value,
        frozen_output_weight,
        frozen_up_weight,
        frozen_down_weight,
        adapter_attention_input,
        adapter_attention_output,
        adapter_up_input,
        adapter_up_output,
        adapter_down_input,
        adapter_down_output,
        prompt_cotangent,
        continuation_cotangent,
    ):
        prompt_len, width = prompt_input_rows.shape[2:]
        count = adapter_up_input.shape[0]
        hidden = frozen_up_weight.shape[1]
        shard_rows = frozen_query_key_value.shape[0]
        assert n_grp == 4 and hidden == n_shard * BLOCK and count // n_fs == 2
        assert frozen_down_weight.shape[0] == BLOCK and BLOCK % shard_rows == 0

        def flat(v):
            return v.reshape(v.shape[-2:])

        x_p, x_c = flat(prompt_input_rows), flat(continuation_input)
        cot_p, cot_c = flat(prompt_cotangent), flat(continuation_cotangent)
        ids = jnp.concatenate([prompt_group_adapter.reshape(1), continuation_adapter.reshape(1)])
        a_ext, b_ext, a_up, b_up, a_dn, b_dn = select_call(
            ids,
            [
                adapter_attention_input.swapaxes(2, 3),
                adapter_attention_output,
                adapter_up_input.swapaxes(1, 2),
                adapter_up_output,
                adapter_down_input.swapaxes(1, 2),
                adapter_down_output,
            ],
        )
        place = jnp.repeat(ids, RANK) * RANK + jnp.arange(2 * RANK) % RANK
        hot = (place[:, None] == jnp.arange(count * RANK)[None, :]).astype(BF)
        norms = [
            v[None, :]
            for v in (first_norm_scale, first_norm_bias, second_norm_scale, second_norm_bias)
        ]
        (
            w_all,
            qkv,
            kp,
            normed_one,
            mixed,
            lows,
            res_p,
            res_c,
            grad_resid,
            grad_attn,
            low_o,
            packed,
        ) = forward_call(
            x_p,
            x_c,
            cot_p,
            cot_c,
            norms,
            (a_ext, b_ext, a_up, b_up, a_dn, b_dn),
            (frozen_query_key_value, frozen_output_weight, frozen_down_weight, frozen_up_weight),
            n_fs,
            n_shard,
        )
        grad_p, grad_c, t_a, t_b, t_a_up, t_b_up, t_a_dn, t_b_dn = back_call(
            grad_attn,
            mixed,
            low_o,
            lows,
            norms[0],
            a_ext,
            b_ext,
            hot,
            packed,
            qkv,
            kp,
            x_p,
            x_c,
            normed_one,
            grad_resid,
            w_all,
            n_fs,
            count,
        )
        tables = [other_pairs(t) for t in (t_a, t_b, t_a_up, t_b_up, t_a_dn, t_b_dn)]
        res_p, res_c, grad_p, grad_c, t_a, t_b, t_a_up, t_b_up, t_a_dn, t_b_dn = finish_call(
            [res_p, res_c, grad_p, grad_c], tables
        )
        return (
            res_p.reshape(prompt_input_rows.shape),
            res_c.reshape(continuation_input.shape),
            grad_p.reshape(prompt_input_rows.shape),
            grad_c.reshape(continuation_input.shape),
            t_a.swapaxes(2, 3),
            t_b,
            t_a_up.swapaxes(1, 2),
            t_b_up,
            t_a_dn.swapaxes(1, 2),
            t_b_dn,
        )

    return body


def solution(mesh):
    sizes = (mesh.shape["rep"], mesh.shape["grp"], mesh.shape["fs"])
    rows_in = P("rep", "fs", "grp", None)
    conts_in = P("rep", "fs", "grp", None, None)
    weight = P(("grp", "fs"), None)
    return jax.shard_map(
        make_body(sizes),
        mesh=mesh,
        in_specs=(
            rows_in,
            conts_in,
            P("rep", "fs"),
            P("rep", "fs", "grp"),
            P(),
            P(),
            P(),
            P(),
            weight,
            weight,
            weight,
            weight,
            P(),
            P(),
            P(),
            P(),
            P(),
            P(),
            rows_in,
            conts_in,
        ),
        out_specs=(
            rows_in,
            conts_in,
            rows_in,
            conts_in,
            P("fs", None, None, None),
            P("fs", None, None, None),
            P("fs", None, None),
            P("fs", None, None),
            P("fs", None, None),
            P("fs", None, None),
        ),
        check_vma=False,
    )
```

```python
import functools
import math

import jax
import jax.numpy as jnp
from jax import lax
from jax.experimental import pallas as pl
from jax.experimental.pallas import tpu as pltpu
from jax.sharding import PartitionSpec as P

HDIM = 128
RANK = 16
BLOCK = 512
PART = 256
AWAY = (32, 48)
ALONG = 16
SCALE = HDIM ** (-0.5)
NEG_FILL = -1e30
BF = jnp.bfloat16
F32 = jnp.float32
MESH = pl.DeviceIdType.MESH
ANY = pl.BlockSpec(memory_space=pl.ANY)
WHOLE = pl.BlockSpec(memory_space=pltpu.VMEM)
ROOM = 62 * 2**20


def mm(a, b):
    return jnp.dot(a, b, preferred_element_type=F32)


def mm_nt(a, b):
    return lax.dot_general(a, b, (((1,), (1,)), ((), ())), preferred_element_type=F32)


def mm_tn(a, b):
    return lax.dot_general(a, b, (((0,), (0,)), ((), ())), preferred_element_type=F32)


def norm_stats(values):
    center = values - jnp.mean(values, axis=-1, keepdims=True)
    spread = jnp.mean(center * center, axis=-1, keepdims=True)
    rstd = lax.rsqrt(spread + 1e-05)
    return center * rstd, rstd


def norm_back(values, gain, grad):
    hat, rstd = norm_stats(values)
    e = grad * gain
    return (
        e - jnp.mean(e, axis=-1, keepdims=True) - hat * jnp.mean(e * hat, axis=-1, keepdims=True)
    ) * rstd


def low_of(product, prompt_len):
    row = lax.broadcasted_iota(jnp.int32, product.shape, 0)
    col = lax.broadcasted_iota(jnp.int32, product.shape, 1)
    return jnp.where((row < prompt_len) == (col < RANK), product, 0.0).astype(BF)


class Gather:
    def __init__(self, n_fs, sources, dst, sems, lag=2):
        (self.zs, self.zr, self.ws, self.wr, self.ys, self.yr, self.xs, self.xr) = sems[:8]
        (self.cs, self.cr, self.ds, self.dr, self.loc) = sems[8:]
        self.nz, self.sources, self.dst = n_fs, sources, dst
        self.count, self.rows = dst.shape[0], dst.shape[2]
        self.lag, self.slots, self.last = lag, 2 * lag, n_fs + 2
        rep, grp = lax.axis_index("rep"), lax.axis_index("grp")
        self.z = lax.axis_index("fs")
        self.y, self.c, plane = grp // 2, grp % 2, rep % 2
        self.far_rep = rep + 1 - 2 * plane
        self.far_core = self.y * 2 + 1 - self.c
        self.far_row = (1 - self.y) * 2 + self.c
        self.own = grp * n_fs + self.z
        self.inner, self.outer, self.far = [], [], []
        for away in AWAY:
            stay = self.rows - away
            self.inner.append((pl.multiple_of(away * plane, 8), stay))
            self.outer.append((pl.multiple_of(stay * plane, 8), away))
            self.far.append((pl.multiple_of(stay * (1 - plane), 8), away))
        first, stay = self.inner[1]
        self.near = (first, stay - ALONG)
        self.along = (pl.multiple_of(first + stay - ALONG, 8), ALONG)

    @staticmethod
    def semaphores(n_fs, lag=2):
        slots, dma = 2 * lag, pltpu.SemaphoreType.DMA
        return (
            [dma((3 * slots, 2, n_fs)), dma((3 * slots, n_fs))]
            + [dma((3 * slots, n_fs))] * 2
            + [dma((slots, n_fs))] * 2
            + [dma((slots, 2 * n_fs))] * 6
            + [dma((slots,))]
        )

    def barrier(self):
        sem = pltpu.get_barrier_semaphore()

        def greet(**where):
            pl.semaphore_signal(sem, 1, device_id=where, device_id_type=MESH)

        greet(rep=self.far_rep)
        greet(grp=self.far_core)
        greet(grp=self.far_row)
        below, above = self.z > 0, self.z < self.nz - 1
        pl.when(below)(lambda: greet(fs=self.z - 1))
        pl.when(above)(lambda: greet(fs=self.z + 1))
        pl.semaphore_wait(sem, 3 + below.astype(jnp.int32) + above.astype(jnp.int32))

    def at_distance(self, d):
        if d < 0 or d >= self.nz:
            return []
        if d == 0:
            return [(None, self.z, 0)]
        return [(self.z >= d, self.z - d, 1), (self.z < self.nz - d, self.z + d, -1)]

    def crossing(self, d, ok, fs, way):
        if d < self.nz // 2:
            return [(ok, self.inner[1])]
        if d == self.nz - 1:
            return [(ok, self.near)]
        end = fs == (0 if way > 0 else self.nz - 1)
        inside = jnp.logical_not(end)
        return [(self.both(ok, inside), self.inner[1]), (self.both(ok, end), self.near)]

    @staticmethod
    def both(left, right):
        return right if left is None else jnp.logical_and(left, right)

    def shard(self, other, fs, core):
        row = 1 - self.y if other else self.y
        return (row * 2 + core) * self.nz + fs

    def send(self, j, shard, span, sems, src=None, **where):
        rows = pl.ds(*span)
        return pltpu.make_async_remote_copy(
            self.dst.at[j, shard, rows] if src is None else src(*span),
            self.dst.at[j, shard, rows],
            *sems,
            device_id=where,
            device_id_type=MESH,
        )

    def own_blocks(self, j):
        start = 0
        for count, ref in self.sources:
            ok = (j >= start) & (j < start + count) if len(self.sources) > 1 else None
            yield ok, functools.partial(ref, j - start)
            start += count

    def keeps(self, j, t):
        sem = self.loc.at[lax.rem(t, self.slots)]
        for ok, src in self.own_blocks(j):
            yield ok, pltpu.make_async_copy(src(0, self.rows), self.dst.at[j, self.own], sem)

    def sends(self, a, j, t):
        todo, nz = [], self.nz
        k, kz = lax.rem(t, self.slots), lax.rem(t, 3 * self.slots)

        def column(ok, fs, way, src):
            shard = self.shard(0, fs, self.c)
            if way >= 0:
                sems = (self.zs.at[kz, 0, fs], self.zr.at[kz, fs])
                up = self.send(j, shard, self.inner[0], sems, src, fs=self.z + 1)
                todo.append((self.both(ok, self.z < nz - 1), up))
            if way <= 0:
                sems = (self.zs.at[kz, 1, fs], self.zr.at[kz, fs])
                down = self.send(j, shard, self.inner[0], sems, src, fs=self.z - 1)
                todo.append((self.both(ok, self.z > 0), down))
            sems = (self.ys.at[k, fs], self.yr.at[k, fs])
            for ok_row, span in self.crossing(a, ok, fs, way):
                todo.append((ok_row, self.send(j, shard, span, sems, src, grp=self.far_row)))
            if way:
                sems = (self.xs.at[k, fs], self.xr.at[k, fs])
                todo.append((ok, self.send(j, shard, self.outer[0], sems, rep=self.far_rep)))
            sems = (self.cs.at[k, fs], self.cr.at[k, fs])
            span = self.inner[0] if way else (0, self.rows)
            todo.append((ok, self.send(j, shard, span, sems, src, grp=self.far_core)))

        if a == 0:
            for ok, src in self.own_blocks(j):
                column(ok, self.z, 0, src)
        else:
            for ok, fs, way in self.at_distance(a):
                column(ok, fs, way, None)
        for ok, fs, way in self.at_distance(a - 1):
            shard = self.shard(1, fs, self.c)
            sems = (self.xs.at[k, nz + fs], self.xr.at[k, nz + fs])
            todo.append((ok, self.send(j, shard, self.outer[1], sems, rep=self.far_rep)))
            sems = (self.cs.at[k, nz + fs], self.cr.at[k, nz + fs])
            todo.append((ok, self.send(j, shard, self.inner[1], sems, grp=self.far_core)))
            if nz // 2 <= a < nz:
                to = self.z + way
                ok = (fs == (0 if way > 0 else nz - 1)) & (to >= 0) & (to < nz)
                sems = (self.ws.at[kz, fs], self.wr.at[kz, fs])
                todo.append((ok, self.send(j, shard, self.along, sems, fs=to)))
        for other in (0, 1):
            for ok, fs, way in self.at_distance(a - 1 - other):
                if way or other:
                    i = other * nz + fs
                    sems = (self.ds.at[k, i], self.dr.at[k, i])
                    shard = self.shard(other, fs, self.c)
                    core = self.send(j, shard, self.far[other], sems, grp=self.far_core)
                    todo.append((ok, core))
        return todo

    def arrivals(self, a, j, t):
        todo, nz = [], self.nz
        k, kz = lax.rem(t, self.slots), lax.rem(t, 3 * self.slots)

        def expect(ok, shard, span, sem):
            ref = self.dst.at[j, shard, pl.ds(*span)]
            todo.append((ok, pltpu.make_async_copy(ref, ref, sem)))

        for ok, fs, way in self.at_distance(a):
            if way:
                expect(ok, self.shard(0, fs, self.c), self.inner[0], self.zr.at[kz, fs])
        for ok, fs, way in self.at_distance(a - 1):
            shard = self.shard(1, fs, self.c)
            for ok_row, span in self.crossing(a - 1, ok, fs, way):
                expect(ok_row, shard, span, self.yr.at[k, fs])
            if a - 1 >= nz // 2:
                end = self.both(ok, fs == (0 if way > 0 else nz - 1))
                expect(end, shard, self.along, self.wr.at[kz, fs])
        for other in (0, 1):
            inner, far = self.inner[other], self.far[other]
            for ok, fs, way in self.at_distance(a - 1 - other):
                i = other * nz + fs
                if way or other:
                    expect(ok, self.shard(other, fs, self.c), far, self.xr.at[k, i])
                span = inner if way or other else (0, self.rows)
                expect(ok, self.shard(other, fs, 1 - self.c), span, self.cr.at[k, i])
            for ok, fs, way in self.at_distance(a - 2 - other):
                if way or other:
                    i = other * nz + fs
                    expect(ok, self.shard(other, fs, 1 - self.c), far, self.dr.at[k, i])
        return todo

    def run(self, early=None, compute=None):
        lag = self.lag

        def act(ok, fn):
            if ok is None:
                fn()
            else:
                pl.when(ok)(fn)

        def finish(a, j, t):
            for ok, copy in self.sends(a - 1, j, t):
                act(ok, copy.wait_send)
            for ok, copy in self.arrivals(a, j, t):
                act(ok, copy.wait)
            if a == 1:
                for ok, copy in self.keeps(j, t):
                    act(ok, copy.wait)

        def begin(a, j, t):
            for ok, copy in self.sends(a, j, t):
                act(ok, copy.start)
            if a == 0:
                for ok, copy in self.keeps(j, t):
                    act(ok, copy.start)

        def tick(t, carry):
            for a in range(self.last, 0, -1):
                j = t - lag * a
                pl.when((j >= 0) & (j < self.count))(functools.partial(finish, a, j, t - lag))
            for a in range(self.last - 1, -1, -1):
                j = t - lag * a
                pl.when((j >= 0) & (j < self.count))(functools.partial(begin, a, j, t))
            if early is not None:
                early(t)
            if compute is not None:
                j = t - lag * self.last
                pl.when(j >= 0)(functools.partial(compute, j))
            return carry

        lax.fori_loop(0, self.count + lag * self.last + (compute is not None), tick, 0)


def head_columns(ref, rows, part, h, width):
    first = pl.multiple_of(part * width + h * HDIM, HDIM)
    return ref[rows, pl.ds(first, HDIM)]


def seen(shape, first):
    row = lax.broadcasted_iota(jnp.int32, shape, 0)
    return lax.broadcasted_iota(jnp.int32, shape, 1) <= first + row


def head_chances(qkv, kp, h, prompt_len, width, first):
    own, cont = slice(0, prompt_len), slice(prompt_len, None)
    q_p = head_columns(qkv, own, 0, h, width)
    q_c = head_columns(qkv, cont, 0, h, width)
    k_c = head_columns(qkv, cont, 1, h, width)
    v_c = head_columns(qkv, cont, 2, h, width)
    lanes = pl.ds(pl.multiple_of(h * HDIM, HDIM), HDIM)
    k_p = kp[:, :, lanes].reshape(-1, HDIM)
    lanes = pl.ds(pl.multiple_of(width + h * HDIM, HDIM), HDIM)
    v_p = kp[:, :, lanes].reshape(-1, HDIM)
    s_p = mm_nt(q_p, k_p) * SCALE
    s_p = jnp.where(seen(s_p.shape, first), s_p, NEG_FILL)
    e_p = jnp.exp(s_p - jnp.max(s_p, axis=-1, keepdims=True))
    c_p = e_p * (1.0 / jnp.sum(e_p, axis=-1, keepdims=True))
    s_1 = mm_nt(q_c, k_p) * SCALE
    s_2 = mm_nt(q_c, k_c) * SCALE
    s_2 = jnp.where(seen(s_2.shape, 0), s_2, NEG_FILL)
    peak = jnp.maximum(
        jnp.max(s_1, axis=-1, keepdims=True), jnp.max(s_2, axis=-1, keepdims=True)
    )
    e_1, e_2 = jnp.exp(s_1 - peak), jnp.exp(s_2 - peak)
    mass = jnp.sum(e_1, axis=-1, keepdims=True) + jnp.sum(e_2, axis=-1, keepdims=True)
    inv = 1.0 / mass
    return (q_p, q_c, k_p, k_c, v_p, v_c), (c_p, e_1 * inv, e_2 * inv)


def select_call(ids, tables):
    def kernel(ids, *refs):
        for src, dst in zip(refs[: len(tables)], refs[len(tables) :]):
            dst[...] = src[0]

    def spec_in(t):
        return pl.BlockSpec((1,) + t.shape[1:], lambda i, ids: (ids[i],) + (0,) * (t.ndim - 1))

    def spec_out(t):
        lead = t.ndim - 3
        return pl.BlockSpec(t.shape[1:], lambda i, ids: (0,) * lead + (i, 0))

    return pl.pallas_call(
        kernel,
        grid_spec=pltpu.PrefetchScalarGridSpec(
            num_scalar_prefetch=1,
            grid=(2,),
            in_specs=[spec_in(t) for t in tables],
            out_specs=[spec_out(t) for t in tables],
        ),
        out_shape=[
            jax.ShapeDtypeStruct(t.shape[1:-2] + (2 * RANK, t.shape[-1]), BF) for t in tables
        ],
        name="select",
    )(ids, *tables)


def columns_of(ref):
    return lambda j, first, size: ref.at[
        pl.ds(first, size), pl.ds(pl.multiple_of(j * PART, PART), PART)
    ]


def tiles_of(ref, shard_rows, parts):
    def tile(j, first, size):
        row = pl.multiple_of(lax.rem(j, parts) * shard_rows + first, 8)
        return ref.at[pl.ds(row, size), pl.ds(pl.multiple_of(j // parts * PART, PART), PART)]

    return tile


def pair_loads(blocks, first, wbuf, wsem, k):
    return [
        pltpu.make_async_copy(
            blocks.at[first + i], wbuf.at[k, :, :, pl.ds(i * PART, PART)], wsem.at[k, i]
        )
        for i in range(2)
    ]


PIECES = 8


def pack(out, unit, piece, value):
    value = value.astype(BF)
    for n in range(PIECES):
        out[n, :, unit * piece : (unit + 1) * piece] = value[:, n * piece : (n + 1) * piece]


def forward_call(x_p, x_c, cot_p, cot_c, norms, tables, weights, n_fs, n_shard):
    prompt_len, width = x_p.shape
    rows = prompt_len + x_c.shape[0]
    shard_rows, hidden = weights[3].shape
    parts = weights[2].shape[0] // shard_rows
    n_qkv, n_out, n_up = 3 * width // PART, width // PART, hidden // PART
    n_dn = n_out * parts
    before_up = n_qkv + n_out + n_dn
    count = before_up + n_up
    n_grp = n_shard // n_fs
    heads = width // HDIM
    per = width // BLOCK
    piece = width // PIECES
    lag = 2
    t_onward, t_low = 6, 12
    t_head = n_qkv + lag * (n_fs + 2) + 1
    t_out = t_head + heads
    t_norm = t_out + per

    def kernel(x_p, x_c, gain_one, bias_one, gain_two, bias_two, *refs):
        (a_ext, b_ext, a_up, b_up, a_dn, b_dn), refs = refs[:6], refs[6:]
        (cot_p, cot_c), src, refs = refs[:2], refs[2:6], refs[6:]
        (dst, qkv_out, kp_out, normed_out, mixed_out), refs = refs[:5], refs[5:]
        (lows, res_p, res_c, resid_back, grad_attn, low_o), refs = refs[:6], refs[6:]
        packed, refs = refs[0], refs[1:]
        (qkv, kp, group, low_group, normed_one, normed, mixed, cot, resid, out_acc), refs = refs[:10], refs[10:]
        (low_up, dlow_dn, low_dn, dlow_up, wbuf, dbuf), refs = refs[:6], refs[6:]
        (wsem, dsem, ksend, krecv, lsem), sems = refs[:5], refs[5:]
        own, rest = slice(0, prompt_len), slice(prompt_len, None)
        sources = [
            (n_qkv, columns_of(src[0])),
            (n_out, columns_of(src[1])),
            (n_dn, tiles_of(src[2], shard_rows, parts)),
            (n_up, columns_of(src[3])),
        ]
        engine = Gather(n_fs, sources, dst, sems, lag)
        engine.barrier()
        grp = lax.axis_index("grp")
        loads = [
            pltpu.make_async_copy(cot_p, cot.at[pl.ds(0, prompt_len)], lsem.at[0]),
            pltpu.make_async_copy(cot_c, cot.at[pl.ds(prompt_len, rows - prompt_len)], lsem.at[1]),
        ]
        stores = [
            pltpu.make_async_copy(qkv, qkv_out, lsem.at[2]),
            pltpu.make_async_copy(kp, kp_out, lsem.at[3]),
            pltpu.make_async_copy(normed_one, normed_out, lsem.at[4]),
            pltpu.make_async_copy(mixed, mixed_out, lsem.at[5]),
        ]

        def pass_on(n, whose, to):
            return pltpu.make_async_remote_copy(
                group.at[whose],
                group.at[whose],
                ksend.at[n],
                krecv.at[n],
                device_id={"grp": to},
                device_id_type=MESH,
            )

        def landed(n, whose):
            return pltpu.make_async_copy(group.at[whose], group.at[whose], krecv.at[n])

        to_row = pass_on(0, grp, engine.far_row)
        to_core = pass_on(1, grp, engine.far_core)
        onward = pass_on(2, engine.far_row, engine.far_core)
        diagonal = (1 - engine.y) * 2 + 1 - engine.c

        def early(t):
            @pl.when(t == 0)
            def _():
                for copy in loads:
                    copy.start()
                for x, part in ((x_p, own), (x_c, rest)):
                    hat, _ = norm_stats(x[...].astype(F32))
                    normed_one[part] = (hat * gain_one[...] + bias_one[...]).astype(BF)
                    if part == own:
                        group[grp] = normed_one[part]
                        to_row.start()
                        to_core.start()
                for n in range(3):
                    lows[n] = low_of(mm_nt(normed_one[...], a_ext[n]), prompt_len)
                for copy in loads:
                    copy.wait()
                dlow_dn[...] = low_of(mm_nt(cot[...], b_dn[...]), prompt_len)

            @pl.when(t == t_onward)
            def _():
                landed(0, engine.far_row).wait()
                onward.start()

            @pl.when(t == t_low)
            def _():
                landed(1, engine.far_core).wait()
                landed(2, diagonal).wait()
                to_row.wait_send()
                to_core.wait_send()
                onward.wait_send()
                for n in range(2):
                    low = mm_nt(group[...].reshape(-1, width), a_ext[1 + n, :RANK])
                    low_group[n] = low.astype(BF)

            @pl.when(t == t_head)
            def _():
                for n in range(3):
                    stores[n].start()

            @pl.when((t >= t_head) & (t < t_out))
            def _():
                h = t - t_head
                (_, _, _, _, v_p, v_c), (c_p, c_1, c_2) = head_chances(
                    qkv, kp, h, prompt_len, width, grp * prompt_len
                )
                lanes = pl.ds(pl.multiple_of(h * HDIM, HDIM), HDIM)
                mixed[own, lanes] = mm(c_p.astype(BF), v_p).astype(BF)
                mixed[rest, lanes] = (mm(c_1.astype(BF), v_p) + mm(c_2.astype(BF), v_c)).astype(BF)

            def load_out(b):
                return pair_loads(dst, n_qkv + 2 * b, wbuf, wsem, lax.rem(b, 2))

            @pl.when(t == t_out - 1)
            def _():
                for copy in load_out(0):
                    copy.start()

            @pl.when((t >= t_out) & (t < t_norm))
            def _():
                b = t - t_out

                @pl.when(b == 0)
                def _():
                    stores[3].start()
                    low_o[...] = low_of(mm_nt(mixed[...], a_ext[3]), prompt_len)

                for copy in load_out(b):
                    copy.wait()

                @pl.when(b + 1 < per)
                def _():
                    for copy in load_out(b + 1):
                        copy.start()

                cols = pl.ds(pl.multiple_of(b * BLOCK, BLOCK), BLOCK)
                w = wbuf[lax.rem(b, 2)].reshape(-1, BLOCK)
                branch = mm(mixed[...], w) + mm(low_o[...], b_ext[3, :, cols])
                resid[own, cols] = x_p[:, cols].astype(F32) + branch[own]
                resid[rest, cols] = x_c[:, cols].astype(F32) + branch[rest]

            @pl.when(t == t_norm)
            def _():
                hat, _ = norm_stats(resid[...])
                normed[...] = (hat * gain_two[...] + bias_two[...]).astype(BF)
                low_up[...] = low_of(mm_nt(normed[...], a_up[...]), prompt_len)
                out_acc[...] = resid[...]
                resid_back[...] = jnp.zeros_like(resid_back)
                low_dn[...] = jnp.zeros_like(low_dn)
                dlow_up[...] = jnp.zeros_like(dlow_up)

        def load(j):
            k, i = lax.rem(j // 2, 2), lax.rem(j, 2)
            into = wbuf.at[k, :, :, pl.ds(pl.multiple_of(i * PART, PART), PART)]
            return pltpu.make_async_copy(dst.at[j], into, wsem.at[k, i])

        def load_down(n):
            k = lax.rem(n, 2)
            return [
                pltpu.make_async_copy(
                    dst.at[pl.ds(n_qkv + n_out + b * parts, parts), n],
                    dbuf.at[k, :, :, pl.ds(b * PART, PART)],
                    dsem.at[k, b],
                )
                for b in range(n_out)
            ]

        def compute(j):
            n = j - before_up

            @pl.when((j < n_qkv) | ((n >= 0) & (n < n_up)))
            def _():
                load(j).start()

            @pl.when((n >= 0) & (n < n_up) & (lax.rem(j, 2) == 0))
            def _():
                for copy in load_down(n // 2):
                    copy.start()

            @pl.when((j > 0) & (j <= n_qkv) & (lax.rem(j, 2) == 0))
            def _():
                i = j // 2 - 1
                for first in (j - 2, j - 1):
                    load(first).wait()
                w = wbuf[lax.rem(i, 2)].reshape(-1, BLOCK)
                m = i // per
                inside = pl.ds(pl.multiple_of(lax.rem(i, per) * BLOCK, BLOCK), BLOCK)
                cols = pl.ds(pl.multiple_of(i * BLOCK, BLOCK), BLOCK)

                @pl.when(m == 0)
                def _():
                    extra = mm(lows[0], b_ext[0, :, inside])
                    qkv[:, cols] = (mm(normed_one[...], w) + extra).astype(BF)

                @pl.when(m > 0)
                def _():
                    extra = mm(lows[m, rest], b_ext[m, :, inside])
                    qkv[rest, cols] = (mm(normed_one[rest], w) + extra).astype(BF)
                    extra = mm(low_group[m - 1], b_ext[m, :RANK, inside])
                    shared = (mm(group[...].reshape(-1, width), w) + extra).astype(BF)
                    there = pl.ds(pl.multiple_of((i - per) * BLOCK, BLOCK), BLOCK)
                    kp[:, :, there] = shared.reshape(n_grp, prompt_len, BLOCK)

            @pl.when((n > 0) & (lax.rem(j, 2) == 0))
            def _():
                i = n // 2 - 1
                for first in (j - 2, j - 1):
                    load(first).wait()
                for copy in load_down(i):
                    copy.wait()
                cols = pl.ds(pl.multiple_of(i * BLOCK, BLOCK), BLOCK)
                w_up = wbuf[lax.rem(j // 2 - 1, 2)].reshape(-1, BLOCK)
                w_dn = dbuf[lax.rem(i, 2)].reshape(BLOCK, width)
                a_d, b_u = a_dn[:, cols], b_up[:, cols]
                pre = mm(normed[...], w_up) + mm(low_up[...], b_u)
                cdf = 0.5 * (1.0 + lax.erf(pre * math.sqrt(0.5)))
                act = (pre * cdf).astype(BF)
                slope = cdf + pre * jnp.exp(-0.5 * pre * pre) * (1.0 / math.sqrt(2.0 * math.pi))
                grad_act = mm_nt(cot[...], w_dn) + mm(dlow_dn[...], a_d)
                grad_pre = (grad_act * slope).astype(BF)
                out_acc[...] += mm(act, w_dn)
                resid_back[...] += mm_nt(grad_pre, w_up)
                low_dn[...] += mm_nt(act, a_d)
                dlow_up[...] += mm_nt(grad_pre, b_u)
                wide = hidden // width
                for base, grad in (
                    (0, mm_tn(low_up[...], grad_pre).astype(BF)),
                    (wide, mm_tn(dlow_dn[...], act).astype(BF)),
                ):
                    unit = pl.ds(pl.multiple_of((base + i // per) * piece, piece), piece)
                    for m in range(BLOCK // piece):
                        where = lax.rem(i, per) * (BLOCK // piece) + m
                        packed[where, :, unit] = grad[:, m * piece : (m + 1) * piece]

        engine.run(early, compute)
        dlow = low_of(dlow_up[...], prompt_len)
        pack(packed, 2 * (hidden // width), piece, mm_tn(dlow, normed[...]))
        grad = resid_back[...] + mm(dlow, a_up[...])
        grad = cot[...].astype(F32) + norm_back(resid[...], gain_two[...], grad)
        resid_back[...] = grad
        grad_attn[...] = grad.astype(BF)
        low = low_of(low_dn[...], prompt_len)
        result = (out_acc[...] + mm(low, b_dn[...])).astype(BF)
        res_p[...] = result[own]
        res_c[...] = result[rest]
        pack(packed, 2 * (hidden // width) + 1, piece, mm_tn(low, cot[...]))
        for copy in stores:
            copy.wait()

    like = jax.ShapeDtypeStruct
    two = 2 * RANK
    dma = pltpu.SemaphoreType.DMA
    share = (n_grp, prompt_len, 2 * width)
    return pl.pallas_call(
        kernel,
        out_shape=[
            like((count, n_shard, shard_rows, PART), BF),
            like((rows, 3 * width), BF),
            like(share, BF),
            like((rows, width), BF),
            like((rows, width), BF),
            like((3, rows, two), BF),
            like(x_p.shape, BF),
            like(x_c.shape, BF),
            like((rows, width), F32),
            like((rows, width), BF),
            like((rows, two), BF),
            like((PIECES, two, (2 * (hidden // width) + 2) * piece), BF),
        ],
        in_specs=[WHOLE] * 12 + [ANY] * 6,
        out_specs=[ANY] * 5 + [WHOLE] * 7,
        scratch_shapes=[
            pltpu.VMEM((rows, 3 * width), BF),
            pltpu.VMEM(share, BF),
            pltpu.VMEM((n_grp, prompt_len, width), BF),
            pltpu.VMEM((2, n_grp * prompt_len, RANK), BF),
            pltpu.VMEM((rows, width), BF),
            pltpu.VMEM((rows, width), BF),
            pltpu.VMEM((rows, width), BF),
            pltpu.VMEM((rows, width), BF),
            pltpu.VMEM((rows, width), F32),
            pltpu.VMEM((rows, width), F32),
            pltpu.VMEM((rows, two), BF),
            pltpu.VMEM((rows, two), BF),
            pltpu.VMEM((rows, two), F32),
            pltpu.VMEM((rows, two), F32),
            pltpu.VMEM((2, n_shard, shard_rows, BLOCK), BF),
            pltpu.VMEM((2, parts, shard_rows, width), BF),
            dma((2, 2)),
            dma((2, n_out)),
            dma((3,)),
            dma((3,)),
            dma((6,)),
        ]
        + Gather.semaphores(n_fs, lag),
        compiler_params=pltpu.CompilerParams(
            collective_id=0, has_side_effects=True, vmem_limit_bytes=ROOM
        ),
        name="forward",
    )(x_p, x_c, *norms, *tables, cot_p, cot_c, *weights)


class TableSum:
    def __init__(self, n_fs, hots, units, bufs, sems, stepwise):
        self.n_fs, self.hots, self.units, self.stepwise = n_fs, hots, units, stepwise
        self.out, self.got, self.dense, self.parts, self.sums = bufs
        (self.s1, self.r1, self.s2, self.r2, self.s3, self.r3) = sems
        rep, self.grp = lax.axis_index("rep"), lax.axis_index("grp")
        self.z = lax.axis_index("fs")
        plane = rep % 2
        y, c = self.grp // 2, self.grp % 2
        self.me = plane * 4 + self.grp
        self.peers = []
        for q in range(1, PIECES):
            x_to = 1 - plane if q // 4 else plane
            y_to = 1 - y if q // 2 % 2 else y
            c_to = 1 - c if q % 2 else c
            where = {"grp": y_to * 2 + c_to}
            if q // 4:
                where["rep"] = rep + 1 - 2 * plane
            self.peers.append((q, x_to * 4 + y_to * 2 + c_to, where))
        self.piece = self.out.shape[2] // units

    @staticmethod
    def scratch(n_fs, units, piece, count):
        two, wide = 2 * RANK, units * piece
        rows = count * RANK // n_fs
        bufs = [
            pltpu.VMEM((PIECES, two, wide), BF),
            pltpu.VMEM((PIECES, two, wide), BF),
            pltpu.VMEM((n_fs, rows, wide), BF),
            pltpu.VMEM((n_fs, rows, wide), BF),
            pltpu.VMEM((PIECES, rows, wide), BF),
        ]
        dma = pltpu.SemaphoreType.DMA
        return bufs, [dma((PIECES,))] * 2 + [dma((n_fs,))] * 2 + [dma((PIECES,))] * 2

    def pack(self, unit, value):
        pack(self.out, unit, self.piece, value)

    def exchange(self):
        return [
            pltpu.make_async_remote_copy(
                self.out.at[to],
                self.got.at[self.me],
                self.s1.at[q],
                self.r1.at[q],
                device_id=where,
                device_id_type=MESH,
            )
            for q, to, where in self.peers
        ]

    def along_fs(self):
        copies = []
        for d in range(1, self.n_fs):
            to = lax.rem(self.z + d, self.n_fs)
            copies.append(
                pltpu.make_async_remote_copy(
                    self.dense.at[to],
                    self.parts.at[self.z],
                    self.s2.at[d],
                    self.r2.at[d],
                    device_id={"fs": to},
                    device_id_type=MESH,
                )
            )
        return copies

    def hand(self, n, whose, q):
        return pltpu.make_async_remote_copy(
            self.sums.at[whose],
            self.sums.at[whose],
            self.s3.at[n],
            self.r3.at[n],
            device_id=self.peers[q - 1][2],
            device_id_type=MESH,
        )

    def hand_out(self):
        return [self.hand(q, self.me, q) for q, _, _ in self.peers]

    def relay(self, stage):
        far_row, far_rep, both = (self.peers[q - 1][1] for q in (2, 4, 6))
        steps = [
            [(4, self.me, 4), (2, self.me, 2), (1, self.me, 1)],
            [(6, far_rep, 2), (5, far_rep, 1), (3, far_row, 1)],
            [(7, both, 1)],
        ]
        return [self.hand(*step) for step in steps[stage]]

    def arrived(self, q):
        ref = self.sums.at[self.peers[q - 1][1]]
        pltpu.make_async_copy(ref, ref, self.r3.at[q]).wait()

    def first(self):
        for copy in self.exchange():
            copy.start()
        self.got[self.me] = self.out[self.me]

    def second(self):
        for q, whose, _ in self.peers:
            ref = self.got.at[whose]
            pltpu.make_async_copy(ref, ref, self.r1.at[q]).wait()
        for copy in self.exchange():
            copy.wait_send()
        wide = self.out.shape[2]
        hots = self.hots[...].reshape(PIECES * 2 * RANK, -1)
        dense = mm_tn(hots, self.got[...].reshape(PIECES * 2 * RANK, wide))
        self.dense[...] = dense.astype(BF).reshape(self.dense.shape)
        for copy in self.along_fs():
            copy.start()
        self.parts[self.z] = self.dense[self.z]

    def third(self):
        for d in range(1, self.n_fs):
            ref = self.parts.at[lax.rem(self.z + self.n_fs - d, self.n_fs)]
            pltpu.make_async_copy(ref, ref, self.r2.at[d]).wait()
        for copy in self.along_fs():
            copy.wait_send()
        total = self.parts[0].astype(F32)
        for n in range(1, self.n_fs):
            total = total + self.parts[n].astype(F32)
        self.sums[self.me] = total.astype(BF)
        if not self.stepwise:
            for copy in self.hand_out():
                copy.start()
            return
        for copy in self.relay(0):
            copy.start()

    def fourth(self):
        self.arrived(4)
        self.arrived(2)
        for copy in self.relay(1):
            copy.start()

    def fifth(self):
        self.arrived(6)
        for copy in self.relay(2):
            copy.start()

    def last(self, places):
        if self.stepwise:
            for q in (1, 3, 5, 7):
                self.arrived(q)
            sent = self.relay(0) + self.relay(1) + self.relay(2)
        else:
            for q, _, _ in self.peers:
                self.arrived(q)
            sent = self.hand_out()
        for copy in sent:
            copy.wait_send()
        for unit, place in enumerate(places):
            for k in range(PIECES):
                cols = slice(unit * self.piece, (unit + 1) * self.piece)
                for a in range(self.sums.shape[1] // RANK):
                    value = self.sums[k, a * RANK : (a + 1) * RANK, cols]
                    place(a, k * self.piece, value)


def back_call(
    grad_attn, mixed, low_o, lows, gain, a_ext, b_ext, hot, packed, qkv, kp, x_p, x_c, normed, grad_resid, w_all, n_fs, count
):
    rows, width = grad_attn.shape
    prompt_len, cont_len = x_p.shape[0], x_c.shape[0]
    heads = width // HDIM
    n_grp = kp.shape[0]
    n_shard, shard_rows = w_all.shape[1:3]
    per = width // BLOCK
    n_qkv = 3 * per
    piece = width // PIECES
    adapters = count // n_fs
    groups = 4
    group_heads = heads // groups
    half = group_heads * HDIM
    two = 2 * RANK
    first_units = packed.shape[2] // piece
    wide_units = first_units // 2 - 1
    hidden = wide_units * width
    last_units = 4

    def kernel(*refs):
        (grad_attn, mixed, low_o, lows, gain, a_ext, b_ext, hot), refs = refs[:8], refs[8:]
        packed, refs = refs[0], refs[1:]
        (qkv, kp, x_p, x_c, normed, grad_resid, w_all), refs = refs[:7], refs[7:]
        (out_p, out_c, t_a, t_b, t_a_up, t_b_up, t_a_dn, t_b_dn), refs = refs[:8], refs[8:]
        (grads, keep, late, x, normed_here, wbuf, gm, acc, dlow, dlow_o), refs = refs[:10], refs[10:]
        (far, far_core, far_row, hots), refs = refs[:4], refs[4:]
        bufs_one, bufs_mid, bufs_two, refs = (packed, *refs[:4]), refs[4:9], refs[9:14], refs[14:]
        sems_one, sems_mid, sems_two, refs = refs[:6], refs[6:12], refs[12:18], refs[18:]
        lsem, wsem, csend, crecv, rsend, rrecv, hsend, hrecv = refs
        grp = lax.axis_index("grp")
        y, c = grp // 2, grp % 2
        own, rest = slice(0, prompt_len), slice(prompt_len, None)
        one = TableSum(n_fs, hots, first_units, bufs_one, sems_one, True)
        mid = TableSum(n_fs, hots, last_units, bufs_mid, sems_mid, True)
        two_ = TableSum(n_fs, hots, last_units, bufs_two, sems_two, False)
        barrier = pltpu.get_barrier_semaphore()
        for _, _, where in one.peers:
            pl.semaphore_signal(barrier, 1, device_id=where, device_id_type=MESH)
        for d in range(1, n_fs):
            to = lax.rem(one.z + d, n_fs)
            pl.semaphore_signal(barrier, 1, device_id={"fs": to}, device_id_type=MESH)

        loads = [
            pltpu.make_async_copy(src, dst, lsem.at[n])
            for n, (src, dst) in enumerate(
                [
                    (qkv, grads),
                    (kp, keep),
                    (grad_resid, late),
                    (normed, normed_here),
                    (x_p, x.at[pl.ds(0, prompt_len)]),
                    (x_c, x.at[pl.ds(prompt_len, cont_len)]),
                ]
            )
        ]
        for copy in loads:
            copy.start()

        def load_w(i, k):
            for copy in pair_loads(w_all, 2 * i, wbuf, wsem, k):
                copy.start()

        def wait_w(i, k):
            for copy in pair_loads(w_all, 2 * i, wbuf, wsem, k):
                copy.wait()

        load_w(n_qkv, 0)
        pl.semaphore_wait(barrier, len(one.peers) + n_fs - 1)

        hots[one.me] = hot[...]
        hot_sends = [
            pltpu.make_async_remote_copy(
                hots.at[one.me],
                hots.at[one.me],
                hsend.at[q],
                hrecv.at[q],
                device_id=where,
                device_id_type=MESH,
            )
            for q, _, where in one.peers
        ]
        for copy in hot_sends:
            copy.start()
        one.first()
        dlow_o[...] = low_of(mm_nt(grad_attn[...], b_ext[3]), prompt_len)
        mid.pack(0, mm_tn(dlow_o[...], mixed[...]))
        mid.pack(1, mm_tn(low_o[...], grad_attn[...]))

        acc[...] = mm(dlow_o[...], a_ext[3])
        for n in range(per):
            wait_w(n_qkv + n, n % 2)
            if n + 1 < per:
                load_w(n_qkv + n + 1, (n + 1) % 2)
            w = wbuf[n % 2].reshape(-1, BLOCK)
            acc[...] += mm_nt(grad_attn[:, n * BLOCK : (n + 1) * BLOCK], w)
        gm[...] = acc[...].astype(BF)
        load_w(0, 0)
        load_w(1, 1)

        loads[0].wait()
        loads[1].wait()

        def head(part, n, carry):
            h = part * group_heads + n
            first = grp * prompt_len
            (q_p, q_c, k_p, k_c, v_p, v_c), (c_p, c_1, c_2) = head_chances(
                grads, keep, h, prompt_len, width, first
            )
            lanes = [
                pl.ds(pl.multiple_of(i * width + h * HDIM, HDIM), HDIM) for i in range(3)
            ]
            gm_p, gm_c = gm[own, lanes[0]], gm[rest, lanes[0]]
            d_p = mm_nt(gm_p, v_p)
            d_1, d_2 = mm_nt(gm_c, v_p), mm_nt(gm_c, v_c)
            s_p = (c_p * (d_p - jnp.sum(c_p * d_p, axis=-1, keepdims=True))).astype(BF)
            inner = jnp.sum(c_1 * d_1, axis=-1, keepdims=True) + jnp.sum(
                c_2 * d_2, axis=-1, keepdims=True
            )
            s_1 = (c_1 * (d_1 - inner)).astype(BF)
            s_2 = (c_2 * (d_2 - inner)).astype(BF)
            grads[own, lanes[0]] = (mm(s_p, k_p) * SCALE).astype(BF)
            grads[rest, lanes[0]] = ((mm(s_1, k_p) + mm(s_2, k_c)) * SCALE).astype(BF)
            grads[rest, lanes[1]] = (mm_tn(s_2, q_c) * SCALE).astype(BF)
            grads[rest, lanes[2]] = mm_tn(c_2.astype(BF), gm_c).astype(BF)
            g_k = ((mm_tn(s_p, q_p) + mm_tn(s_1, q_c)) * SCALE).astype(BF)
            g_v = (mm_tn(c_p.astype(BF), gm_p) + mm_tn(c_1.astype(BF), gm_c)).astype(BF)
            into = [pl.ds(pl.multiple_of(i * half + n * HDIM, HDIM), HDIM) for i in range(2)]
            far[part, :, :, into[0]] = g_k.reshape(n_grp, prompt_len, HDIM)
            far[part, :, :, into[1]] = g_v.reshape(n_grp, prompt_len, HDIM)
            return carry

        def to_core(part):
            return [
                pltpu.make_async_remote_copy(
                    far.at[part, row * 2 + 1 - c],
                    far_core.at[part, row],
                    csend.at[part, row],
                    crecv.at[part, row],
                    device_id={"grp": y * 2 + 1 - c},
                    device_id_type=MESH,
                )
                for row in range(2)
            ]

        def to_row(part):
            return pltpu.make_async_remote_copy(
                far.at[part, (1 - y) * 2 + c],
                far_row.at[part],
                rsend.at[part],
                rrecv.at[part],
                device_id={"grp": (1 - y) * 2 + c},
                device_id_type=MESH,
            )

        def add_core(part):
            for copy in to_core(part):
                copy.wait()
            for row in range(2):
                total = far[part, row * 2 + c].astype(F32) + far_core[part, row].astype(F32)
                far[part, row * 2 + c] = total.astype(BF)
            to_row(part).start()

        def add_row(part):
            to_row(part).wait()
            total = far[part, grp].astype(F32) + far_row[part].astype(F32)
            total = total.astype(BF)
            for i in range(2):
                cols = slice((i + 1) * width + part * half, (i + 1) * width + (part + 1) * half)
                grads[own, cols] = total[:, i * half : (i + 1) * half]

        def half_group(i, carry):
            part = i // 2

            @pl.when((lax.rem(i, 2) == 1) & (part > 0))
            def _():
                add_core(part - 1)

            first = lax.rem(i, 2) * (group_heads // 2)
            lax.fori_loop(first, first + group_heads // 2, functools.partial(head, part), 0)

            @pl.when(lax.rem(i, 2) == 1)
            def _():
                for copy in to_core(part):
                    copy.start()

            @pl.when(i == 1)
            def _():
                for copy in hot_sends:
                    copy.wait_send()
                for q, whose, _ in one.peers:
                    pltpu.make_async_copy(hots.at[whose], hots.at[whose], hrecv.at[q]).wait()
                one.second()

            return carry

        lax.fori_loop(0, 2 * groups, half_group, 0)

        def tables(i, into, first):
            part = grads[:, i * width : (i + 1) * width]
            low = low_of(mm_nt(part, b_ext[i]), prompt_len)
            into.pack(first, mm_tn(low, normed_here[...]))
            into.pack(first + 1, mm_tn(lows[i], part))
            dlow[i] = low

        def project(n, carry):
            k = lax.rem(n, 2)
            wait_w(n, k)
            part = grads[:, pl.ds(pl.multiple_of(n * BLOCK, BLOCK), BLOCK)]
            acc[...] += mm_nt(part, wbuf[k].reshape(-1, BLOCK))

            @pl.when(n + 2 < n_qkv)
            def _():
                load_w(n + 2, k)

            return carry

        loads[3].wait()
        add_core(groups - 1)
        tables(0, mid, 2)
        mid.first()
        acc[...] = mm(dlow[0], a_ext[0])
        lax.fori_loop(0, per, project, 0)
        for part in range(groups):
            add_row(part)
        tables(1, two_, 0)
        tables(2, two_, 2)
        two_.first()
        mid.second()
        one.third()
        acc[...] += mm(dlow[1], a_ext[1]) + mm(dlow[2], a_ext[2])

        def project_more(n, carry):
            pl.when(n == 2 * per + 1)(two_.second)
            return project(n, carry)

        lax.fori_loop(per, n_qkv, project_more, 0)
        mid.third()
        one.fourth()
        for copy in (loads[2], loads[4], loads[5]):
            copy.wait()
        back = late[...] + norm_back(x[...].astype(F32), gain[...], acc[...])
        back = back.astype(BF)
        out_p[...] = back[own]
        out_c[...] = back[rest]

        def whole(ref, first):
            def place(a, col, value):
                ref[a, :, first + col : first + col + piece] = value

            return place

        def one_map(ref, n):
            def place(a, col, value):
                ref[a, n, :, col : col + piece] = value

            return place

        two_.third()
        one.fifth()
        mid.fourth()
        mid.fifth()
        one.last(
            [whole(t_b_up, n * width) for n in range(wide_units)]
            + [whole(t_a_dn, n * width) for n in range(wide_units)]
            + [whole(t_a_up, 0), whole(t_b_dn, 0)]
        )
        mid.last([one_map(t_a, 3), one_map(t_b, 3), one_map(t_a, 0), one_map(t_b, 0)])
        two_.last([one_map(t_a, 1), one_map(t_b, 1), one_map(t_a, 2), one_map(t_b, 2)])

    like = jax.ShapeDtypeStruct
    bufs_one, sems_one = TableSum.scratch(n_fs, first_units, piece, count)
    bufs_mid, sems_mid = TableSum.scratch(n_fs, last_units, piece, count)
    bufs_two, sems_two = TableSum.scratch(n_fs, last_units, piece, count)
    dma = pltpu.SemaphoreType.DMA
    return pl.pallas_call(
        kernel,
        out_shape=[
            like(x_p.shape, BF),
            like(x_c.shape, BF),
            like((adapters, 4, RANK, width), BF),
            like((adapters, 4, RANK, width), BF),
            like((adapters, RANK, width), BF),
            like((adapters, RANK, hidden), BF),
            like((adapters, RANK, hidden), BF),
            like((adapters, RANK, width), BF),
        ],
        in_specs=[WHOLE] * 9 + [ANY] * 7,
        out_specs=[WHOLE] * 8,
        scratch_shapes=[
            pltpu.VMEM((rows, 3 * width), BF),
            pltpu.VMEM(kp.shape, BF),
            pltpu.VMEM((rows, width), F32),
            pltpu.VMEM((rows, width), BF),
            pltpu.VMEM((rows, width), BF),
            pltpu.VMEM((2, n_shard, shard_rows, BLOCK), BF),
            pltpu.VMEM((rows, width), BF),
            pltpu.VMEM((rows, width), F32),
            pltpu.VMEM((3, rows, two), BF),
            pltpu.VMEM((rows, two), BF),
            pltpu.VMEM((groups, n_grp, prompt_len, 2 * half), BF),
            pltpu.VMEM((groups, 2, prompt_len, 2 * half), BF),
            pltpu.VMEM((groups, prompt_len, 2 * half), BF),
            pltpu.VMEM((PIECES,) + hot.shape, BF),
        ]
        + bufs_one[1:]
        + bufs_mid
        + bufs_two
        + sems_one
        + sems_mid
        + sems_two
        + [dma((6,)), dma((2, 2)), dma((groups, 2)), dma((groups, 2)), dma((groups,)), dma((groups,))]
        + [dma((PIECES,)), dma((PIECES,))],
        compiler_params=pltpu.CompilerParams(
            collective_id=2, has_side_effects=True, vmem_limit_bytes=ROOM
        ),
        name="back",
    )(
        grad_attn, mixed, low_o, lows, gain, a_ext, b_ext, hot, packed,
        qkv, kp, x_p, x_c, normed, grad_resid, w_all,
    )


def finish_call(rows, tables):
    steps = (2, 4)

    def kernel(*refs):
        for src, dst in zip(refs[: len(refs) // 2], refs[len(refs) // 2 :]):
            dst[...] = src[...].astype(dst.dtype)

    def row_spec(v):
        return pl.BlockSpec((v.shape[0] // 8, v.shape[1]), lambda a, n: (a * 4 + n, 0))

    def table_spec(v):
        if v.ndim == 4:
            return pl.BlockSpec((1, 1) + v.shape[2:], lambda a, n: (a, n, 0, 0))
        return pl.BlockSpec((1, v.shape[1], v.shape[2] // 4), lambda a, n: (a, 0, n))

    specs = [row_spec(v) for v in rows] + [table_spec(v) for v in tables]
    return pl.pallas_call(
        kernel,
        grid=steps,
        in_specs=specs,
        out_specs=specs,
        out_shape=[jax.ShapeDtypeStruct(v.shape, BF) for v in rows]
        + [jax.ShapeDtypeStruct(v.shape, F32) for v in tables],
        name="finish",
    )(*rows, *tables)


def make_body(sizes):
    n_rep, n_grp, n_fs = sizes
    n_shard = n_grp * n_fs

    def other_pairs(v):
        step = 2
        while step < n_rep:
            far = lax.ppermute(v, "rep", [(i, i ^ step) for i in range(n_rep)])
            v = (v.astype(F32) + far.astype(F32)).astype(BF)
            step *= 2
        return v

    def body(
        prompt_input_rows,
        continuation_input,
        prompt_group_adapter,
        continuation_adapter,
        first_norm_scale,
        first_norm_bias,
        second_norm_scale,
        second_norm_bias,
        frozen_query_key_value,
        frozen_output_weight,
        frozen_up_weight,
        frozen_down_weight,
        adapter_attention_input,
        adapter_attention_output,
        adapter_up_input,
        adapter_up_output,
        adapter_down_input,
        adapter_down_output,
        prompt_cotangent,
        continuation_cotangent,
    ):
        prompt_len, width = prompt_input_rows.shape[2:]
        count = adapter_up_input.shape[0]
        hidden = frozen_up_weight.shape[1]
        shard_rows = frozen_query_key_value.shape[0]
        assert n_grp == 4 and hidden == n_shard * BLOCK and count // n_fs == 2
        assert frozen_down_weight.shape[0] == BLOCK and BLOCK % shard_rows == 0

        def flat(v):
            return v.reshape(v.shape[-2:])

        x_p, x_c = flat(prompt_input_rows), flat(continuation_input)
        cot_p, cot_c = flat(prompt_cotangent), flat(continuation_cotangent)
        ids = jnp.concatenate([prompt_group_adapter.reshape(1), continuation_adapter.reshape(1)])
        a_ext, b_ext, a_up, b_up, a_dn, b_dn = select_call(
            ids,
            [
                adapter_attention_input.swapaxes(2, 3),
                adapter_attention_output,
                adapter_up_input.swapaxes(1, 2),
                adapter_up_output,
                adapter_down_input.swapaxes(1, 2),
                adapter_down_output,
            ],
        )
        place = jnp.repeat(ids, RANK) * RANK + jnp.arange(2 * RANK) % RANK
        hot = (place[:, None] == jnp.arange(count * RANK)[None, :]).astype(BF)
        norms = [
            v[None, :]
            for v in (first_norm_scale, first_norm_bias, second_norm_scale, second_norm_bias)
        ]
        (
            w_all,
            qkv,
            kp,
            normed_one,
            mixed,
            lows,
            res_p,
            res_c,
            grad_resid,
            grad_attn,
            low_o,
            packed,
        ) = forward_call(
            x_p,
            x_c,
            cot_p,
            cot_c,
            norms,
            (a_ext, b_ext, a_up, b_up, a_dn, b_dn),
            (frozen_query_key_value, frozen_output_weight, frozen_down_weight, frozen_up_weight),
            n_fs,
            n_shard,
        )
        grad_p, grad_c, t_a, t_b, t_a_up, t_b_up, t_a_dn, t_b_dn = back_call(
            grad_attn,
            mixed,
            low_o,
            lows,
            norms[0],
            a_ext,
            b_ext,
            hot,
            packed,
            qkv,
            kp,
            x_p,
            x_c,
            normed_one,
            grad_resid,
            w_all,
            n_fs,
            count,
        )
        tables = [other_pairs(t) for t in (t_a, t_b, t_a_up, t_b_up, t_a_dn, t_b_dn)]
        res_p, res_c, grad_p, grad_c, t_a, t_b, t_a_up, t_b_up, t_a_dn, t_b_dn = finish_call(
            [res_p, res_c, grad_p, grad_c], tables
        )
        return (
            res_p.reshape(prompt_input_rows.shape),
            res_c.reshape(continuation_input.shape),
            grad_p.reshape(prompt_input_rows.shape),
            grad_c.reshape(continuation_input.shape),
            t_a.swapaxes(2, 3),
            t_b,
            t_a_up.swapaxes(1, 2),
            t_b_up,
            t_a_dn.swapaxes(1, 2),
            t_b_dn,
        )

    return body


def solution(mesh):
    sizes = (mesh.shape["rep"], mesh.shape["grp"], mesh.shape["fs"])
    rows_in = P("rep", "fs", "grp", None)
    conts_in = P("rep", "fs", "grp", None, None)
    weight = P(("grp", "fs"), None)
    return jax.shard_map(
        make_body(sizes),
        mesh=mesh,
        in_specs=(
            rows_in,
            conts_in,
            P("rep", "fs"),
            P("rep", "fs", "grp"),
            P(),
            P(),
            P(),
            P(),
            weight,
            weight,
            weight,
            weight,
            P(),
            P(),
            P(),
            P(),
            P(),
            P(),
            rows_in,
            conts_in,
        ),
        out_specs=(
            rows_in,
            conts_in,
            rows_in,
            conts_in,
            P("fs", None, None, None),
            P("fs", None, None, None),
            P("fs", None, None),
            P("fs", None, None),
            P("fs", None, None),
            P("fs", None, None),
        ),
        check_vma=False,
    )
```

```python
import functools
import math

import jax
import jax.numpy as jnp
from jax import lax
from jax.experimental import pallas as pl
from jax.experimental.pallas import tpu as pltpu
from jax.sharding import PartitionSpec as P

HDIM = 128
RANK = 16
BLOCK = 512
PART = 256
AWAY = (32, 48)
ALONG = 16
SCALE = HDIM ** (-0.5)
NEG_FILL = -1e30
BF = jnp.bfloat16
F32 = jnp.float32
MESH = pl.DeviceIdType.MESH
ANY = pl.BlockSpec(memory_space=pl.ANY)
WHOLE = pl.BlockSpec(memory_space=pltpu.VMEM)
ROOM = 62 * 2**20


def mm(a, b):
    return jnp.dot(a, b, preferred_element_type=F32)


def mm_nt(a, b):
    return lax.dot_general(a, b, (((1,), (1,)), ((), ())), preferred_element_type=F32)


def mm_tn(a, b):
    return lax.dot_general(a, b, (((0,), (0,)), ((), ())), preferred_element_type=F32)


def norm_stats(values):
    center = values - jnp.mean(values, axis=-1, keepdims=True)
    spread = jnp.mean(center * center, axis=-1, keepdims=True)
    rstd = lax.rsqrt(spread + 1e-05)
    return center * rstd, rstd


def norm_back(values, gain, grad):
    hat, rstd = norm_stats(values)
    e = grad * gain
    return (
        e - jnp.mean(e, axis=-1, keepdims=True) - hat * jnp.mean(e * hat, axis=-1, keepdims=True)
    ) * rstd


def low_of(product, prompt_len):
    row = lax.broadcasted_iota(jnp.int32, product.shape, 0)
    col = lax.broadcasted_iota(jnp.int32, product.shape, 1)
    return jnp.where((row < prompt_len) == (col < RANK), product, 0.0).astype(BF)


class Gather:
    def __init__(self, n_fs, sources, dst, sems, lag=2):
        (self.zs, self.zr, self.ws, self.wr, self.ys, self.yr, self.xs, self.xr) = sems[:8]
        (self.cs, self.cr, self.ds, self.dr, self.loc) = sems[8:]
        self.nz, self.sources, self.dst = n_fs, sources, dst
        self.count, self.rows = dst.shape[0], dst.shape[2]
        self.lag, self.slots, self.last = lag, 2 * lag, n_fs + 2
        rep, grp = lax.axis_index("rep"), lax.axis_index("grp")
        self.z = lax.axis_index("fs")
        self.y, self.c, plane = grp // 2, grp % 2, rep % 2
        self.far_rep = rep + 1 - 2 * plane
        self.far_core = self.y * 2 + 1 - self.c
        self.far_row = (1 - self.y) * 2 + self.c
        self.own = grp * n_fs + self.z
        self.inner, self.outer, self.far = [], [], []
        for away in AWAY:
            stay = self.rows - away
            self.inner.append((pl.multiple_of(away * plane, 8), stay))
            self.outer.append((pl.multiple_of(stay * plane, 8), away))
            self.far.append((pl.multiple_of(stay * (1 - plane), 8), away))
        first, stay = self.inner[1]
        self.near = (first, stay - ALONG)
        self.along = (pl.multiple_of(first + stay - ALONG, 8), ALONG)

    @staticmethod
    def semaphores(n_fs, lag=2):
        slots, dma = 2 * lag, pltpu.SemaphoreType.DMA
        return (
            [dma((3 * slots, 2, n_fs)), dma((3 * slots, n_fs))]
            + [dma((3 * slots, n_fs))] * 2
            + [dma((slots, n_fs))] * 2
            + [dma((slots, 2 * n_fs))] * 6
            + [dma((slots,))]
        )

    def barrier(self):
        sem = pltpu.get_barrier_semaphore()

        def greet(**where):
            pl.semaphore_signal(sem, 1, device_id=where, device_id_type=MESH)

        greet(rep=self.far_rep)
        greet(grp=self.far_core)
        greet(grp=self.far_row)
        below, above = self.z > 0, self.z < self.nz - 1
        pl.when(below)(lambda: greet(fs=self.z - 1))
        pl.when(above)(lambda: greet(fs=self.z + 1))
        pl.semaphore_wait(sem, 3 + below.astype(jnp.int32) + above.astype(jnp.int32))

    def at_distance(self, d):
        if d < 0 or d >= self.nz:
            return []
        if d == 0:
            return [(None, self.z, 0)]
        return [(self.z >= d, self.z - d, 1), (self.z < self.nz - d, self.z + d, -1)]

    def crossing(self, d, ok, fs, way):
        if d < self.nz // 2:
            return [(ok, self.inner[1])]
        if d == self.nz - 1:
            return [(ok, self.near)]
        end = fs == (0 if way > 0 else self.nz - 1)
        inside = jnp.logical_not(end)
        return [(self.both(ok, inside), self.inner[1]), (self.both(ok, end), self.near)]

    @staticmethod
    def both(left, right):
        return right if left is None else jnp.logical_and(left, right)

    def shard(self, other, fs, core):
        row = 1 - self.y if other else self.y
        return (row * 2 + core) * self.nz + fs

    def send(self, j, shard, span, sems, src=None, **where):
        rows = pl.ds(*span)
        return pltpu.make_async_remote_copy(
            self.dst.at[j, shard, rows] if src is None else src(*span),
            self.dst.at[j, shard, rows],
            *sems,
            device_id=where,
            device_id_type=MESH,
        )

    def own_blocks(self, j):
        start = 0
        for count, ref in self.sources:
            ok = (j >= start) & (j < start + count) if len(self.sources) > 1 else None
            yield ok, functools.partial(ref, j - start)
            start += count

    def keeps(self, j, t):
        sem = self.loc.at[lax.rem(t, self.slots)]
        for ok, src in self.own_blocks(j):
            yield ok, pltpu.make_async_copy(src(0, self.rows), self.dst.at[j, self.own], sem)

    def sends(self, a, j, t):
        todo, nz = [], self.nz
        k, kz = lax.rem(t, self.slots), lax.rem(t, 3 * self.slots)

        def column(ok, fs, way, src):
            shard = self.shard(0, fs, self.c)
            if way >= 0:
                sems = (self.zs.at[kz, 0, fs], self.zr.at[kz, fs])
                up = self.send(j, shard, self.inner[0], sems, src, fs=self.z + 1)
                todo.append((self.both(ok, self.z < nz - 1), up))
            if way <= 0:
                sems = (self.zs.at[kz, 1, fs], self.zr.at[kz, fs])
                down = self.send(j, shard, self.inner[0], sems, src, fs=self.z - 1)
                todo.append((self.both(ok, self.z > 0), down))
            sems = (self.ys.at[k, fs], self.yr.at[k, fs])
            for ok_row, span in self.crossing(a, ok, fs, way):
                todo.append((ok_row, self.send(j, shard, span, sems, src, grp=self.far_row)))
            if way:
                sems = (self.xs.at[k, fs], self.xr.at[k, fs])
                todo.append((ok, self.send(j, shard, self.outer[0], sems, rep=self.far_rep)))
            sems = (self.cs.at[k, fs], self.cr.at[k, fs])
            span = self.inner[0] if way else (0, self.rows)
            todo.append((ok, self.send(j, shard, span, sems, src, grp=self.far_core)))

        if a == 0:
            for ok, src in self.own_blocks(j):
                column(ok, self.z, 0, src)
        else:
            for ok, fs, way in self.at_distance(a):
                column(ok, fs, way, None)
        for ok, fs, way in self.at_distance(a - 1):
            shard = self.shard(1, fs, self.c)
            sems = (self.xs.at[k, nz + fs], self.xr.at[k, nz + fs])
            todo.append((ok, self.send(j, shard, self.outer[1], sems, rep=self.far_rep)))
            sems = (self.cs.at[k, nz + fs], self.cr.at[k, nz + fs])
            todo.append((ok, self.send(j, shard, self.inner[1], sems, grp=self.far_core)))
            if nz // 2 <= a < nz:
                to = self.z + way
                ok = (fs == (0 if way > 0 else nz - 1)) & (to >= 0) & (to < nz)
                sems = (self.ws.at[kz, fs], self.wr.at[kz, fs])
                todo.append((ok, self.send(j, shard, self.along, sems, fs=to)))
        for other in (0, 1):
            for ok, fs, way in self.at_distance(a - 1 - other):
                if way or other:
                    i = other * nz + fs
                    sems = (self.ds.at[k, i], self.dr.at[k, i])
                    shard = self.shard(other, fs, self.c)
                    core = self.send(j, shard, self.far[other], sems, grp=self.far_core)
                    todo.append((ok, core))
        return todo

    def arrivals(self, a, j, t):
        todo, nz = [], self.nz
        k, kz = lax.rem(t, self.slots), lax.rem(t, 3 * self.slots)

        def expect(ok, shard, span, sem):
            ref = self.dst.at[j, shard, pl.ds(*span)]
            todo.append((ok, pltpu.make_async_copy(ref, ref, sem)))

        for ok, fs, way in self.at_distance(a):
            if way:
                expect(ok, self.shard(0, fs, self.c), self.inner[0], self.zr.at[kz, fs])
        for ok, fs, way in self.at_distance(a - 1):
            shard = self.shard(1, fs, self.c)
            for ok_row, span in self.crossing(a - 1, ok, fs, way):
                expect(ok_row, shard, span, self.yr.at[k, fs])
            if a - 1 >= nz // 2:
                end = self.both(ok, fs == (0 if way > 0 else nz - 1))
                expect(end, shard, self.along, self.wr.at[kz, fs])
        for other in (0, 1):
            inner, far = self.inner[other], self.far[other]
            for ok, fs, way in self.at_distance(a - 1 - other):
                i = other * nz + fs
                if way or other:
                    expect(ok, self.shard(other, fs, self.c), far, self.xr.at[k, i])
                span = inner if way or other else (0, self.rows)
                expect(ok, self.shard(other, fs, 1 - self.c), span, self.cr.at[k, i])
            for ok, fs, way in self.at_distance(a - 2 - other):
                if way or other:
                    i = other * nz + fs
                    expect(ok, self.shard(other, fs, 1 - self.c), far, self.dr.at[k, i])
        return todo

    def run(self, early=None, compute=None):
        lag = self.lag

        def act(ok, fn):
            if ok is None:
                fn()
            else:
                pl.when(ok)(fn)

        def finish(a, j, t):
            for ok, copy in self.sends(a - 1, j, t):
                act(ok, copy.wait_send)
            for ok, copy in self.arrivals(a, j, t):
                act(ok, copy.wait)
            if a == 1:
                for ok, copy in self.keeps(j, t):
                    act(ok, copy.wait)

        def begin(a, j, t):
            for ok, copy in self.sends(a, j, t):
                act(ok, copy.start)
            if a == 0:
                for ok, copy in self.keeps(j, t):
                    act(ok, copy.start)

        def tick(t, carry):
            for a in range(self.last, 0, -1):
                j = t - lag * a
                pl.when((j >= 0) & (j < self.count))(functools.partial(finish, a, j, t - lag))
            for a in range(self.last - 1, -1, -1):
                j = t - lag * a
                pl.when((j >= 0) & (j < self.count))(functools.partial(begin, a, j, t))
            if early is not None:
                early(t)
            if compute is not None:
                j = t - lag * self.last
                pl.when(j >= 0)(functools.partial(compute, j))
            return carry

        lax.fori_loop(0, self.count + lag * self.last + (compute is not None), tick, 0)


def head_columns(ref, rows, part, h, width):
    first = pl.multiple_of(part * width + h * HDIM, HDIM)
    return ref[rows, pl.ds(first, HDIM)]


def seen(shape, first):
    row = lax.broadcasted_iota(jnp.int32, shape, 0)
    return lax.broadcasted_iota(jnp.int32, shape, 1) <= first + row


def head_chances(qkv, kp, h, prompt_len, width, first):
    own, cont = slice(0, prompt_len), slice(prompt_len, None)
    q_p = head_columns(qkv, own, 0, h, width)
    q_c = head_columns(qkv, cont, 0, h, width)
    k_c = head_columns(qkv, cont, 1, h, width)
    v_c = head_columns(qkv, cont, 2, h, width)
    lanes = pl.ds(pl.multiple_of(h * HDIM, HDIM), HDIM)
    k_p = kp[:, :, lanes].reshape(-1, HDIM)
    lanes = pl.ds(pl.multiple_of(width + h * HDIM, HDIM), HDIM)
    v_p = kp[:, :, lanes].reshape(-1, HDIM)
    s_p = mm_nt(q_p, k_p) * SCALE
    s_p = jnp.where(seen(s_p.shape, first), s_p, NEG_FILL)
    e_p = jnp.exp(s_p - jnp.max(s_p, axis=-1, keepdims=True))
    c_p = e_p * (1.0 / jnp.sum(e_p, axis=-1, keepdims=True))
    s_1 = mm_nt(q_c, k_p) * SCALE
    s_2 = mm_nt(q_c, k_c) * SCALE
    s_2 = jnp.where(seen(s_2.shape, 0), s_2, NEG_FILL)
    peak = jnp.maximum(
        jnp.max(s_1, axis=-1, keepdims=True), jnp.max(s_2, axis=-1, keepdims=True)
    )
    e_1, e_2 = jnp.exp(s_1 - peak), jnp.exp(s_2 - peak)
    mass = jnp.sum(e_1, axis=-1, keepdims=True) + jnp.sum(e_2, axis=-1, keepdims=True)
    inv = 1.0 / mass
    return (q_p, q_c, k_p, k_c, v_p, v_c), (c_p, e_1 * inv, e_2 * inv)


def select_call(ids, tables):
    def kernel(ids, *refs):
        for src, dst in zip(refs[: len(tables)], refs[len(tables) :]):
            dst[...] = src[0]

    def spec_in(t):
        return pl.BlockSpec((1,) + t.shape[1:], lambda i, ids: (ids[i],) + (0,) * (t.ndim - 1))

    def spec_out(t):
        lead = t.ndim - 3
        return pl.BlockSpec(t.shape[1:], lambda i, ids: (0,) * lead + (i, 0))

    return pl.pallas_call(
        kernel,
        grid_spec=pltpu.PrefetchScalarGridSpec(
            num_scalar_prefetch=1,
            grid=(2,),
            in_specs=[spec_in(t) for t in tables],
            out_specs=[spec_out(t) for t in tables],
        ),
        out_shape=[
            jax.ShapeDtypeStruct(t.shape[1:-2] + (2 * RANK, t.shape[-1]), BF) for t in tables
        ],
        name="select",
    )(ids, *tables)


def columns_of(ref):
    return lambda j, first, size: ref.at[
        pl.ds(first, size), pl.ds(pl.multiple_of(j * PART, PART), PART)
    ]


def tiles_of(ref, shard_rows, parts):
    def tile(j, first, size):
        row = pl.multiple_of(lax.rem(j, parts) * shard_rows + first, 8)
        return ref.at[pl.ds(row, size), pl.ds(pl.multiple_of(j // parts * PART, PART), PART)]

    return tile


def pair_loads(blocks, first, wbuf, wsem, k):
    return [
        pltpu.make_async_copy(
            blocks.at[first + i], wbuf.at[k, :, :, pl.ds(i * PART, PART)], wsem.at[k, i]
        )
        for i in range(2)
    ]


PIECES = 8


def pack(out, unit, piece, value):
    value = value.astype(BF)
    for n in range(PIECES):
        out[n, :, unit * piece : (unit + 1) * piece] = value[:, n * piece : (n + 1) * piece]


def forward_call(x_p, x_c, cot_p, cot_c, norms, tables, weights, n_fs, n_shard):
    prompt_len, width = x_p.shape
    rows = prompt_len + x_c.shape[0]
    shard_rows, hidden = weights[3].shape
    parts = weights[2].shape[0] // shard_rows
    n_qkv, n_out, n_up = 3 * width // PART, width // PART, hidden // PART
    n_dn = n_out * parts
    before_up = n_qkv + n_out + n_dn
    count = before_up + n_up
    n_grp = n_shard // n_fs
    heads = width // HDIM
    per = width // BLOCK
    piece = width // PIECES
    lag = 2
    t_onward, t_low = 6, 12
    t_head = n_qkv + lag * (n_fs + 2) + 1
    t_out = t_head + heads
    t_norm = t_out + per

    def kernel(x_p, x_c, gain_one, bias_one, gain_two, bias_two, *refs):
        (a_ext, b_ext, a_up, b_up, a_dn, b_dn), refs = refs[:6], refs[6:]
        (cot_p, cot_c), src, refs = refs[:2], refs[2:6], refs[6:]
        (dst, qkv_out, kp_out, normed_out, mixed_out), refs = refs[:5], refs[5:]
        (lows, res_p, res_c, resid_back, grad_attn, low_o), refs = refs[:6], refs[6:]
        packed, refs = refs[0], refs[1:]
        (qkv, kp, group, low_group, normed_one, normed, mixed, cot, resid, out_acc), refs = refs[:10], refs[10:]
        (low_up, dlow_dn, low_dn, dlow_up, wbuf, dbuf), refs = refs[:6], refs[6:]
        (wsem, dsem, ksend, krecv, lsem), sems = refs[:5], refs[5:]
        own, rest = slice(0, prompt_len), slice(prompt_len, None)
        sources = [
            (n_qkv, columns_of(src[0])),
            (n_out, columns_of(src[1])),
            (n_dn, tiles_of(src[2], shard_rows, parts)),
            (n_up, columns_of(src[3])),
        ]
        engine = Gather(n_fs, sources, dst, sems, lag)
        engine.barrier()
        grp = lax.axis_index("grp")
        loads = [
            pltpu.make_async_copy(cot_p, cot.at[pl.ds(0, prompt_len)], lsem.at[0]),
            pltpu.make_async_copy(cot_c, cot.at[pl.ds(prompt_len, rows - prompt_len)], lsem.at[1]),
        ]
        stores = [
            pltpu.make_async_copy(qkv, qkv_out, lsem.at[2]),
            pltpu.make_async_copy(kp, kp_out, lsem.at[3]),
            pltpu.make_async_copy(normed_one, normed_out, lsem.at[4]),
            pltpu.make_async_copy(mixed, mixed_out, lsem.at[5]),
        ]

        def pass_on(n, whose, to):
            return pltpu.make_async_remote_copy(
                group.at[whose],
                group.at[whose],
                ksend.at[n],
                krecv.at[n],
                device_id={"grp": to},
                device_id_type=MESH,
            )

        def landed(n, whose):
            return pltpu.make_async_copy(group.at[whose], group.at[whose], krecv.at[n])

        to_row = pass_on(0, grp, engine.far_row)
        to_core = pass_on(1, grp, engine.far_core)
        onward = pass_on(2, engine.far_row, engine.far_core)
        diagonal = (1 - engine.y) * 2 + 1 - engine.c

        def early(t):
            @pl.when(t == 0)
            def _():
                for copy in loads:
                    copy.start()
                for x, part in ((x_p, own), (x_c, rest)):
                    hat, _ = norm_stats(x[...].astype(F32))
                    normed_one[part] = (hat * gain_one[...] + bias_one[...]).astype(BF)
                    if part == own:
                        group[grp] = normed_one[part]
                        to_row.start()
                        to_core.start()
                for n in range(3):
                    lows[n] = low_of(mm_nt(normed_one[...], a_ext[n]), prompt_len)
                for copy in loads:
                    copy.wait()
                dlow_dn[...] = low_of(mm_nt(cot[...], b_dn[...]), prompt_len)

            @pl.when(t == t_onward)
            def _():
                landed(0, engine.far_row).wait()
                onward.start()

            @pl.when(t == t_low)
            def _():
                landed(1, engine.far_core).wait()
                landed(2, diagonal).wait()
                to_row.wait_send()
                to_core.wait_send()
                onward.wait_send()
                for n in range(2):
                    low = mm_nt(group[...].reshape(-1, width), a_ext[1 + n, :RANK])
                    low_group[n] = low.astype(BF)

            @pl.when(t == t_head)
            def _():
                for n in range(3):
                    stores[n].start()

            @pl.when((t >= t_head) & (t < t_out))
            def _():
                h = t - t_head
                (_, _, _, _, v_p, v_c), (c_p, c_1, c_2) = head_chances(
                    qkv, kp, h, prompt_len, width, grp * prompt_len
                )
                lanes = pl.ds(pl.multiple_of(h * HDIM, HDIM), HDIM)
                mixed[own, lanes] = mm(c_p.astype(BF), v_p).astype(BF)
                mixed[rest, lanes] = (mm(c_1.astype(BF), v_p) + mm(c_2.astype(BF), v_c)).astype(BF)

            def load_out(b):
                return pair_loads(dst, n_qkv + 2 * b, wbuf, wsem, lax.rem(b, 2))

            @pl.when(t == t_out - 1)
            def _():
                for copy in load_out(0):
                    copy.start()

            @pl.when((t >= t_out) & (t < t_norm))
            def _():
                b = t - t_out

                @pl.when(b == 0)
                def _():
                    stores[3].start()
                    low_o[...] = low_of(mm_nt(mixed[...], a_ext[3]), prompt_len)

                for copy in load_out(b):
                    copy.wait()

                @pl.when(b + 1 < per)
                def _():
                    for copy in load_out(b + 1):
                        copy.start()

                cols = pl.ds(pl.multiple_of(b * BLOCK, BLOCK), BLOCK)
                w = wbuf[lax.rem(b, 2)].reshape(-1, BLOCK)
                branch = mm(mixed[...], w) + mm(low_o[...], b_ext[3, :, cols])
                resid[own, cols] = x_p[:, cols].astype(F32) + branch[own]
                resid[rest, cols] = x_c[:, cols].astype(F32) + branch[rest]

            @pl.when(t == t_norm)
            def _():
                hat, _ = norm_stats(resid[...])
                normed[...] = (hat * gain_two[...] + bias_two[...]).astype(BF)
                low_up[...] = low_of(mm_nt(normed[...], a_up[...]), prompt_len)
                out_acc[...] = resid[...]
                resid_back[...] = jnp.zeros_like(resid_back)
                low_dn[...] = jnp.zeros_like(low_dn)
                dlow_up[...] = jnp.zeros_like(dlow_up)

        def load(j):
            k, i = lax.rem(j // 2, 2), lax.rem(j, 2)
            into = wbuf.at[k, :, :, pl.ds(pl.multiple_of(i * PART, PART), PART)]
            return pltpu.make_async_copy(dst.at[j], into, wsem.at[k, i])

        def load_down(n):
            k = lax.rem(n, 2)
            return [
                pltpu.make_async_copy(
                    dst.at[pl.ds(n_qkv + n_out + b * parts, parts), n],
                    dbuf.at[k, :, :, pl.ds(b * PART, PART)],
                    dsem.at[k, b],
                )
                for b in range(n_out)
            ]

        def compute(j):
            n = j - before_up

            @pl.when((j < n_qkv) | ((n >= 0) & (n < n_up)))
            def _():
                load(j).start()

            @pl.when((n >= 0) & (n < n_up) & (lax.rem(j, 2) == 0))
            def _():
                for copy in load_down(n // 2):
                    copy.start()

            @pl.when((j > 0) & (j <= n_qkv) & (lax.rem(j, 2) == 0))
            def _():
                i = j // 2 - 1
                for first in (j - 2, j - 1):
                    load(first).wait()
                w = wbuf[lax.rem(i, 2)].reshape(-1, BLOCK)
                m = i // per
                inside = pl.ds(pl.multiple_of(lax.rem(i, per) * BLOCK, BLOCK), BLOCK)
                cols = pl.ds(pl.multiple_of(i * BLOCK, BLOCK), BLOCK)

                @pl.when(m == 0)
                def _():
                    extra = mm(lows[0], b_ext[0, :, inside])
                    qkv[:, cols] = (mm(normed_one[...], w) + extra).astype(BF)

                @pl.when(m > 0)
                def _():
                    extra = mm(lows[m, rest], b_ext[m, :, inside])
                    qkv[rest, cols] = (mm(normed_one[rest], w) + extra).astype(BF)
                    extra = mm(low_group[m - 1], b_ext[m, :RANK, inside])
                    shared = (mm(group[...].reshape(-1, width), w) + extra).astype(BF)
                    there = pl.ds(pl.multiple_of((i - per) * BLOCK, BLOCK), BLOCK)
                    kp[:, :, there] = shared.reshape(n_grp, prompt_len, BLOCK)

            @pl.when((n > 0) & (lax.rem(j, 2) == 0))
            def _():
                i = n // 2 - 1
                for first in (j - 2, j - 1):
                    load(first).wait()
                for copy in load_down(i):
                    copy.wait()
                cols = pl.ds(pl.multiple_of(i * BLOCK, BLOCK), BLOCK)
                w_up = wbuf[lax.rem(j // 2 - 1, 2)].reshape(-1, BLOCK)
                w_dn = dbuf[lax.rem(i, 2)].reshape(BLOCK, width)
                a_d, b_u = a_dn[:, cols], b_up[:, cols]
                pre = mm(normed[...], w_up) + mm(low_up[...], b_u)
                cdf = 0.5 * (1.0 + lax.erf(pre * math.sqrt(0.5)))
                act = (pre * cdf).astype(BF)
                slope = cdf + pre * jnp.exp(-0.5 * pre * pre) * (1.0 / math.sqrt(2.0 * math.pi))
                grad_act = mm_nt(cot[...], w_dn) + mm(dlow_dn[...], a_d)
                grad_pre = (grad_act * slope).astype(BF)
                out_acc[...] += mm(act, w_dn)
                resid_back[...] += mm_nt(grad_pre, w_up)
                low_dn[...] += mm_nt(act, a_d)
                dlow_up[...] += mm_nt(grad_pre, b_u)
                wide = hidden // width
                for base, grad in (
                    (0, mm_tn(low_up[...], grad_pre).astype(BF)),
                    (wide, mm_tn(dlow_dn[...], act).astype(BF)),
                ):
                    unit = pl.ds(pl.multiple_of((base + i // per) * piece, piece), piece)
                    for m in range(BLOCK // piece):
                        where = lax.rem(i, per) * (BLOCK // piece) + m
                        packed[where, :, unit] = grad[:, m * piece : (m + 1) * piece]

        engine.run(early, compute)
        dlow = low_of(dlow_up[...], prompt_len)
        pack(packed, 2 * (hidden // width), piece, mm_tn(dlow, normed[...]))
        grad = resid_back[...] + mm(dlow, a_up[...])
        grad = cot[...].astype(F32) + norm_back(resid[...], gain_two[...], grad)
        resid_back[...] = grad
        grad_attn[...] = grad.astype(BF)
        low = low_of(low_dn[...], prompt_len)
        result = (out_acc[...] + mm(low, b_dn[...])).astype(BF)
        res_p[...] = result[own]
        res_c[...] = result[rest]
        pack(packed, 2 * (hidden // width) + 1, piece, mm_tn(low, cot[...]))
        for copy in stores:
            copy.wait()

    like = jax.ShapeDtypeStruct
    two = 2 * RANK
    dma = pltpu.SemaphoreType.DMA
    share = (n_grp, prompt_len, 2 * width)
    return pl.pallas_call(
        kernel,
        out_shape=[
            like((count, n_shard, shard_rows, PART), BF),
            like((rows, 3 * width), BF),
            like(share, BF),
            like((rows, width), BF),
            like((rows, width), BF),
            like((3, rows, two), BF),
            like(x_p.shape, BF),
            like(x_c.shape, BF),
            like((rows, width), F32),
            like((rows, width), BF),
            like((rows, two), BF),
            like((PIECES, two, (2 * (hidden // width) + 2) * piece), BF),
        ],
        in_specs=[WHOLE] * 12 + [ANY] * 6,
        out_specs=[ANY] * 5 + [WHOLE] * 7,
        scratch_shapes=[
            pltpu.VMEM((rows, 3 * width), BF),
            pltpu.VMEM(share, BF),
            pltpu.VMEM((n_grp, prompt_len, width), BF),
            pltpu.VMEM((2, n_grp * prompt_len, RANK), BF),
            pltpu.VMEM((rows, width), BF),
            pltpu.VMEM((rows, width), BF),
            pltpu.VMEM((rows, width), BF),
            pltpu.VMEM((rows, width), BF),
            pltpu.VMEM((rows, width), F32),
            pltpu.VMEM((rows, width), F32),
            pltpu.VMEM((rows, two), BF),
            pltpu.VMEM((rows, two), BF),
            pltpu.VMEM((rows, two), F32),
            pltpu.VMEM((rows, two), F32),
            pltpu.VMEM((2, n_shard, shard_rows, BLOCK), BF),
            pltpu.VMEM((2, parts, shard_rows, width), BF),
            dma((2, 2)),
            dma((2, n_out)),
            dma((3,)),
            dma((3,)),
            dma((6,)),
        ]
        + Gather.semaphores(n_fs, lag),
        compiler_params=pltpu.CompilerParams(
            collective_id=0, has_side_effects=True, vmem_limit_bytes=ROOM
        ),
        name="forward",
    )(x_p, x_c, *norms, *tables, cot_p, cot_c, *weights)


class TableSum:
    def __init__(self, n_fs, hots, units, bufs, sems, stepwise):
        self.n_fs, self.hots, self.units, self.stepwise = n_fs, hots, units, stepwise
        self.out, self.got, self.dense, self.parts, self.sums = bufs
        (self.s1, self.r1, self.s2, self.r2, self.s3, self.r3) = sems
        rep, self.grp = lax.axis_index("rep"), lax.axis_index("grp")
        self.z = lax.axis_index("fs")
        plane = rep % 2
        y, c = self.grp // 2, self.grp % 2
        self.me = plane * 4 + self.grp
        self.peers = []
        for q in range(1, PIECES):
            x_to = 1 - plane if q // 4 else plane
            y_to = 1 - y if q // 2 % 2 else y
            c_to = 1 - c if q % 2 else c
            where = {"grp": y_to * 2 + c_to}
            if q // 4:
                where["rep"] = rep + 1 - 2 * plane
            self.peers.append((q, x_to * 4 + y_to * 2 + c_to, where))
        self.piece = self.out.shape[2] // units

    @staticmethod
    def scratch(n_fs, units, piece, count):
        two, wide = 2 * RANK, units * piece
        rows = count * RANK // n_fs
        bufs = [
            pltpu.VMEM((PIECES, two, wide), BF),
            pltpu.VMEM((PIECES, two, wide), BF),
            pltpu.VMEM((n_fs, rows, wide), BF),
            pltpu.VMEM((n_fs, rows, wide), BF),
            pltpu.VMEM((PIECES, rows, wide), BF),
        ]
        dma = pltpu.SemaphoreType.DMA
        return bufs, [dma((PIECES,))] * 2 + [dma((n_fs,))] * 2 + [dma((PIECES,))] * 2

    def pack(self, unit, value):
        pack(self.out, unit, self.piece, value)

    def exchange(self):
        return [
            pltpu.make_async_remote_copy(
                self.out.at[to],
                self.got.at[self.me],
                self.s1.at[q],
                self.r1.at[q],
                device_id=where,
                device_id_type=MESH,
            )
            for q, to, where in self.peers
        ]

    def along_fs(self):
        copies = []
        for d in range(1, self.n_fs):
            to = lax.rem(self.z + d, self.n_fs)
            copies.append(
                pltpu.make_async_remote_copy(
                    self.dense.at[to],
                    self.parts.at[self.z],
                    self.s2.at[d],
                    self.r2.at[d],
                    device_id={"fs": to},
                    device_id_type=MESH,
                )
            )
        return copies

    def hand(self, n, whose, q):
        return pltpu.make_async_remote_copy(
            self.sums.at[whose],
            self.sums.at[whose],
            self.s3.at[n],
            self.r3.at[n],
            device_id=self.peers[q - 1][2],
            device_id_type=MESH,
        )

    def hand_out(self):
        return [self.hand(q, self.me, q) for q, _, _ in self.peers]

    def relay(self, stage):
        far_row, far_rep, both = (self.peers[q - 1][1] for q in (2, 4, 6))
        steps = [
            [(4, self.me, 4), (2, self.me, 2), (1, self.me, 1)],
            [(6, far_rep, 2), (5, far_rep, 1), (3, far_row, 1)],
            [(7, both, 1)],
        ]
        return [self.hand(*step) for step in steps[stage]]

    def arrived(self, q):
        ref = self.sums.at[self.peers[q - 1][1]]
        pltpu.make_async_copy(ref, ref, self.r3.at[q]).wait()

    def first(self):
        for copy in self.exchange():
            copy.start()
        self.got[self.me] = self.out[self.me]

    def second(self):
        for q, whose, _ in self.peers:
            ref = self.got.at[whose]
            pltpu.make_async_copy(ref, ref, self.r1.at[q]).wait()
        for copy in self.exchange():
            copy.wait_send()
        wide = self.out.shape[2]
        hots = self.hots[...].reshape(PIECES * 2 * RANK, -1)
        dense = mm_tn(hots, self.got[...].reshape(PIECES * 2 * RANK, wide))
        self.dense[...] = dense.astype(BF).reshape(self.dense.shape)
        for copy in self.along_fs():
            copy.start()
        self.parts[self.z] = self.dense[self.z]

    def third(self):
        for d in range(1, self.n_fs):
            ref = self.parts.at[lax.rem(self.z + self.n_fs - d, self.n_fs)]
            pltpu.make_async_copy(ref, ref, self.r2.at[d]).wait()
        for copy in self.along_fs():
            copy.wait_send()
        total = self.parts[0].astype(F32)
        for n in range(1, self.n_fs):
            total = total + self.parts[n].astype(F32)
        self.sums[self.me] = total.astype(BF)
        if not self.stepwise:
            for copy in self.hand_out():
                copy.start()
            return
        for copy in self.relay(0):
            copy.start()

    def fourth(self):
        self.arrived(4)
        self.arrived(2)
        for copy in self.relay(1):
            copy.start()

    def fifth(self):
        self.arrived(6)
        for copy in self.relay(2):
            copy.start()

    def last(self, places):
        if self.stepwise:
            for q in (1, 3, 5, 7):
                self.arrived(q)
            sent = self.relay(0) + self.relay(1) + self.relay(2)
        else:
            for q, _, _ in self.peers:
                self.arrived(q)
            sent = self.hand_out()
        for copy in sent:
            copy.wait_send()
        for unit, place in enumerate(places):
            for k in range(PIECES):
                cols = slice(unit * self.piece, (unit + 1) * self.piece)
                for a in range(self.sums.shape[1] // RANK):
                    value = self.sums[k, a * RANK : (a + 1) * RANK, cols]
                    place(a, k * self.piece, value)


def back_call(
    grad_attn, mixed, low_o, lows, gain, a_ext, b_ext, hot, packed, qkv, kp, x_p, x_c, normed, grad_resid, w_all, n_fs, count
):
    rows, width = grad_attn.shape
    prompt_len, cont_len = x_p.shape[0], x_c.shape[0]
    heads = width // HDIM
    n_grp = kp.shape[0]
    n_shard, shard_rows = w_all.shape[1:3]
    per = width // BLOCK
    n_qkv = 3 * per
    piece = width // PIECES
    adapters = count // n_fs
    groups = 8
    group_heads = heads // groups
    half = group_heads * HDIM
    two = 2 * RANK
    first_units = packed.shape[2] // piece
    wide_units = first_units // 2 - 1
    hidden = wide_units * width
    last_units = 4

    def kernel(*refs):
        (grad_attn, mixed, low_o, lows, gain, a_ext, b_ext, hot), refs = refs[:8], refs[8:]
        packed, refs = refs[0], refs[1:]
        (qkv, kp, x_p, x_c, normed, grad_resid, w_all), refs = refs[:7], refs[7:]
        (out_p, out_c, t_a, t_b, t_a_up, t_b_up, t_a_dn, t_b_dn), refs = refs[:8], refs[8:]
        (grads, keep, late, x, normed_here, wbuf, gm, acc, dlow, dlow_o), refs = refs[:10], refs[10:]
        (far, far_core, far_row, hots), refs = refs[:4], refs[4:]
        bufs_one, bufs_mid, bufs_two, refs = (packed, *refs[:4]), refs[4:9], refs[9:14], refs[14:]
        sems_one, sems_mid, sems_two, refs = refs[:6], refs[6:12], refs[12:18], refs[18:]
        lsem, wsem, csend, crecv, rsend, rrecv, hsend, hrecv = refs
        grp = lax.axis_index("grp")
        y, c = grp // 2, grp % 2
        own, rest = slice(0, prompt_len), slice(prompt_len, None)
        one = TableSum(n_fs, hots, first_units, bufs_one, sems_one, True)
        mid = TableSum(n_fs, hots, last_units, bufs_mid, sems_mid, True)
        two_ = TableSum(n_fs, hots, last_units, bufs_two, sems_two, False)
        barrier = pltpu.get_barrier_semaphore()
        for _, _, where in one.peers:
            pl.semaphore_signal(barrier, 1, device_id=where, device_id_type=MESH)
        for d in range(1, n_fs):
            to = lax.rem(one.z + d, n_fs)
            pl.semaphore_signal(barrier, 1, device_id={"fs": to}, device_id_type=MESH)

        loads = [
            pltpu.make_async_copy(src, dst, lsem.at[n])
            for n, (src, dst) in enumerate(
                [
                    (qkv, grads),
                    (kp, keep),
                    (grad_resid, late),
                    (normed, normed_here),
                    (x_p, x.at[pl.ds(0, prompt_len)]),
                    (x_c, x.at[pl.ds(prompt_len, cont_len)]),
                ]
            )
        ]
        for copy in loads:
            copy.start()

        def load_w(i, k):
            for copy in pair_loads(w_all, 2 * i, wbuf, wsem, k):
                copy.start()

        def wait_w(i, k):
            for copy in pair_loads(w_all, 2 * i, wbuf, wsem, k):
                copy.wait()

        load_w(n_qkv, 0)
        pl.semaphore_wait(barrier, len(one.peers) + n_fs - 1)

        hots[one.me] = hot[...]
        hot_sends = [
            pltpu.make_async_remote_copy(
                hots.at[one.me],
                hots.at[one.me],
                hsend.at[q],
                hrecv.at[q],
                device_id=where,
                device_id_type=MESH,
            )
            for q, _, where in one.peers
        ]
        for copy in hot_sends:
            copy.start()
        one.first()
        dlow_o[...] = low_of(mm_nt(grad_attn[...], b_ext[3]), prompt_len)
        mid.pack(0, mm_tn(dlow_o[...], mixed[...]))
        mid.pack(1, mm_tn(low_o[...], grad_attn[...]))

        acc[...] = mm(dlow_o[...], a_ext[3])
        for n in range(per):
            wait_w(n_qkv + n, n % 2)
            if n + 1 < per:
                load_w(n_qkv + n + 1, (n + 1) % 2)
            w = wbuf[n % 2].reshape(-1, BLOCK)
            acc[...] += mm_nt(grad_attn[:, n * BLOCK : (n + 1) * BLOCK], w)
        gm[...] = acc[...].astype(BF)
        load_w(0, 0)
        load_w(1, 1)

        loads[0].wait()
        loads[1].wait()

        def head(part, n, carry):
            h = part * group_heads + n
            first = grp * prompt_len
            (q_p, q_c, k_p, k_c, v_p, v_c), (c_p, c_1, c_2) = head_chances(
                grads, keep, h, prompt_len, width, first
            )
            lanes = [
                pl.ds(pl.multiple_of(i * width + h * HDIM, HDIM), HDIM) for i in range(3)
            ]
            gm_p, gm_c = gm[own, lanes[0]], gm[rest, lanes[0]]
            d_p = mm_nt(gm_p, v_p)
            d_1, d_2 = mm_nt(gm_c, v_p), mm_nt(gm_c, v_c)
            s_p = (c_p * (d_p - jnp.sum(c_p * d_p, axis=-1, keepdims=True))).astype(BF)
            inner = jnp.sum(c_1 * d_1, axis=-1, keepdims=True) + jnp.sum(
                c_2 * d_2, axis=-1, keepdims=True
            )
            s_1 = (c_1 * (d_1 - inner)).astype(BF)
            s_2 = (c_2 * (d_2 - inner)).astype(BF)
            grads[own, lanes[0]] = (mm(s_p, k_p) * SCALE).astype(BF)
            grads[rest, lanes[0]] = ((mm(s_1, k_p) + mm(s_2, k_c)) * SCALE).astype(BF)
            grads[rest, lanes[1]] = (mm_tn(s_2, q_c) * SCALE).astype(BF)
            grads[rest, lanes[2]] = mm_tn(c_2.astype(BF), gm_c).astype(BF)
            g_k = ((mm_tn(s_p, q_p) + mm_tn(s_1, q_c)) * SCALE).astype(BF)
            g_v = (mm_tn(c_p.astype(BF), gm_p) + mm_tn(c_1.astype(BF), gm_c)).astype(BF)
            into = [pl.ds(pl.multiple_of(i * half + n * HDIM, HDIM), HDIM) for i in range(2)]
            far[part, :, :, into[0]] = g_k.reshape(n_grp, prompt_len, HDIM)
            far[part, :, :, into[1]] = g_v.reshape(n_grp, prompt_len, HDIM)
            return carry

        def to_core(part):
            return [
                pltpu.make_async_remote_copy(
                    far.at[part, row * 2 + 1 - c],
                    far_core.at[part, row],
                    csend.at[part, row],
                    crecv.at[part, row],
                    device_id={"grp": y * 2 + 1 - c},
                    device_id_type=MESH,
                )
                for row in range(2)
            ]

        def to_row(part):
            return pltpu.make_async_remote_copy(
                far.at[part, (1 - y) * 2 + c],
                far_row.at[part],
                rsend.at[part],
                rrecv.at[part],
                device_id={"grp": (1 - y) * 2 + c},
                device_id_type=MESH,
            )

        def add_core(part):
            for copy in to_core(part):
                copy.wait()
            for row in range(2):
                total = far[part, row * 2 + c].astype(F32) + far_core[part, row].astype(F32)
                far[part, row * 2 + c] = total.astype(BF)
            to_row(part).start()

        def add_row(part):
            to_row(part).wait()
            total = far[part, grp].astype(F32) + far_row[part].astype(F32)
            total = total.astype(BF)
            for i in range(2):
                cols = slice((i + 1) * width + part * half, (i + 1) * width + (part + 1) * half)
                grads[own, cols] = total[:, i * half : (i + 1) * half]

        def half_group(i, carry):
            part = i // 2

            @pl.when((lax.rem(i, 2) == 1) & (part > 0))
            def _():
                add_core(part - 1)

            first = lax.rem(i, 2) * (group_heads // 2)
            lax.fori_loop(first, first + group_heads // 2, functools.partial(head, part), 0)

            @pl.when(lax.rem(i, 2) == 1)
            def _():
                for copy in to_core(part):
                    copy.start()

            @pl.when(i == 1)
            def _():
                for copy in hot_sends:
                    copy.wait_send()
                for q, whose, _ in one.peers:
                    pltpu.make_async_copy(hots.at[whose], hots.at[whose], hrecv.at[q]).wait()
                one.second()

            return carry

        lax.fori_loop(0, 2 * groups, half_group, 0)

        def tables(i, into, first):
            part = grads[:, i * width : (i + 1) * width]
            low = low_of(mm_nt(part, b_ext[i]), prompt_len)
            into.pack(first, mm_tn(low, normed_here[...]))
            into.pack(first + 1, mm_tn(lows[i], part))
            dlow[i] = low

        def project(n, carry):
            k = lax.rem(n, 2)
            wait_w(n, k)
            part = grads[:, pl.ds(pl.multiple_of(n * BLOCK, BLOCK), BLOCK)]
            acc[...] += mm_nt(part, wbuf[k].reshape(-1, BLOCK))

            @pl.when(n + 2 < n_qkv)
            def _():
                load_w(n + 2, k)

            return carry

        loads[3].wait()
        add_core(groups - 1)
        tables(0, mid, 2)
        mid.first()
        acc[...] = mm(dlow[0], a_ext[0])
        lax.fori_loop(0, per, project, 0)
        for part in range(groups):
            add_row(part)
        tables(1, two_, 0)
        tables(2, two_, 2)
        two_.first()
        mid.second()
        one.third()
        acc[...] += mm(dlow[1], a_ext[1]) + mm(dlow[2], a_ext[2])

        def project_more(n, carry):
            pl.when(n == 2 * per + 1)(two_.second)
            return project(n, carry)

        lax.fori_loop(per, n_qkv, project_more, 0)
        mid.third()
        one.fourth()
        for copy in (loads[2], loads[4], loads[5]):
            copy.wait()
        back = late[...] + norm_back(x[...].astype(F32), gain[...], acc[...])
        back = back.astype(BF)
        out_p[...] = back[own]
        out_c[...] = back[rest]

        def whole(ref, first):
            def place(a, col, value):
                ref[a, :, first + col : first + col + piece] = value

            return place

        def one_map(ref, n):
            def place(a, col, value):
                ref[a, n, :, col : col + piece] = value

            return place

        two_.third()
        one.fifth()
        mid.fourth()
        mid.fifth()
        one.last(
            [whole(t_b_up, n * width) for n in range(wide_units)]
            + [whole(t_a_dn, n * width) for n in range(wide_units)]
            + [whole(t_a_up, 0), whole(t_b_dn, 0)]
        )
        mid.last([one_map(t_a, 3), one_map(t_b, 3), one_map(t_a, 0), one_map(t_b, 0)])
        two_.last([one_map(t_a, 1), one_map(t_b, 1), one_map(t_a, 2), one_map(t_b, 2)])

    like = jax.ShapeDtypeStruct
    bufs_one, sems_one = TableSum.scratch(n_fs, first_units, piece, count)
    bufs_mid, sems_mid = TableSum.scratch(n_fs, last_units, piece, count)
    bufs_two, sems_two = TableSum.scratch(n_fs, last_units, piece, count)
    dma = pltpu.SemaphoreType.DMA
    return pl.pallas_call(
        kernel,
        out_shape=[
            like(x_p.shape, BF),
            like(x_c.shape, BF),
            like((adapters, 4, RANK, width), BF),
            like((adapters, 4, RANK, width), BF),
            like((adapters, RANK, width), BF),
            like((adapters, RANK, hidden), BF),
            like((adapters, RANK, hidden), BF),
            like((adapters, RANK, width), BF),
        ],
        in_specs=[WHOLE] * 9 + [ANY] * 7,
        out_specs=[WHOLE] * 8,
        scratch_shapes=[
            pltpu.VMEM((rows, 3 * width), BF),
            pltpu.VMEM(kp.shape, BF),
            pltpu.VMEM((rows, width), F32),
            pltpu.VMEM((rows, width), BF),
            pltpu.VMEM((rows, width), BF),
            pltpu.VMEM((2, n_shard, shard_rows, BLOCK), BF),
            pltpu.VMEM((rows, width), BF),
            pltpu.VMEM((rows, width), F32),
            pltpu.VMEM((3, rows, two), BF),
            pltpu.VMEM((rows, two), BF),
            pltpu.VMEM((groups, n_grp, prompt_len, 2 * half), BF),
            pltpu.VMEM((groups, 2, prompt_len, 2 * half), BF),
            pltpu.VMEM((groups, prompt_len, 2 * half), BF),
            pltpu.VMEM((PIECES,) + hot.shape, BF),
        ]
        + bufs_one[1:]
        + bufs_mid
        + bufs_two
        + sems_one
        + sems_mid
        + sems_two
        + [dma((6,)), dma((2, 2)), dma((groups, 2)), dma((groups, 2)), dma((groups,)), dma((groups,))]
        + [dma((PIECES,)), dma((PIECES,))],
        compiler_params=pltpu.CompilerParams(
            collective_id=2, has_side_effects=True, vmem_limit_bytes=ROOM
        ),
        name="back",
    )(
        grad_attn, mixed, low_o, lows, gain, a_ext, b_ext, hot, packed,
        qkv, kp, x_p, x_c, normed, grad_resid, w_all,
    )


def finish_call(rows, tables):
    steps = (2, 4)

    def kernel(*refs):
        for src, dst in zip(refs[: len(refs) // 2], refs[len(refs) // 2 :]):
            dst[...] = src[...].astype(dst.dtype)

    def row_spec(v):
        return pl.BlockSpec((v.shape[0] // 8, v.shape[1]), lambda a, n: (a * 4 + n, 0))

    def table_spec(v):
        if v.ndim == 4:
            return pl.BlockSpec((1, 1) + v.shape[2:], lambda a, n: (a, n, 0, 0))
        return pl.BlockSpec((1, v.shape[1], v.shape[2] // 4), lambda a, n: (a, 0, n))

    specs = [row_spec(v) for v in rows] + [table_spec(v) for v in tables]
    return pl.pallas_call(
        kernel,
        grid=steps,
        in_specs=specs,
        out_specs=specs,
        out_shape=[jax.ShapeDtypeStruct(v.shape, BF) for v in rows]
        + [jax.ShapeDtypeStruct(v.shape, F32) for v in tables],
        name="finish",
    )(*rows, *tables)


def make_body(sizes):
    n_rep, n_grp, n_fs = sizes
    n_shard = n_grp * n_fs

    def other_pairs(v):
        step = 2
        while step < n_rep:
            far = lax.ppermute(v, "rep", [(i, i ^ step) for i in range(n_rep)])
            v = (v.astype(F32) + far.astype(F32)).astype(BF)
            step *= 2
        return v

    def body(
        prompt_input_rows,
        continuation_input,
        prompt_group_adapter,
        continuation_adapter,
        first_norm_scale,
        first_norm_bias,
        second_norm_scale,
        second_norm_bias,
        frozen_query_key_value,
        frozen_output_weight,
        frozen_up_weight,
        frozen_down_weight,
        adapter_attention_input,
        adapter_attention_output,
        adapter_up_input,
        adapter_up_output,
        adapter_down_input,
        adapter_down_output,
        prompt_cotangent,
        continuation_cotangent,
    ):
        prompt_len, width = prompt_input_rows.shape[2:]
        count = adapter_up_input.shape[0]
        hidden = frozen_up_weight.shape[1]
        shard_rows = frozen_query_key_value.shape[0]
        assert n_grp == 4 and hidden == n_shard * BLOCK and count // n_fs == 2
        assert frozen_down_weight.shape[0] == BLOCK and BLOCK % shard_rows == 0

        def flat(v):
            return v.reshape(v.shape[-2:])

        x_p, x_c = flat(prompt_input_rows), flat(continuation_input)
        cot_p, cot_c = flat(prompt_cotangent), flat(continuation_cotangent)
        ids = jnp.concatenate([prompt_group_adapter.reshape(1), continuation_adapter.reshape(1)])
        a_ext, b_ext, a_up, b_up, a_dn, b_dn = select_call(
            ids,
            [
                adapter_attention_input.swapaxes(2, 3),
                adapter_attention_output,
                adapter_up_input.swapaxes(1, 2),
                adapter_up_output,
                adapter_down_input.swapaxes(1, 2),
                adapter_down_output,
            ],
        )
        place = jnp.repeat(ids, RANK) * RANK + jnp.arange(2 * RANK) % RANK
        hot = (place[:, None] == jnp.arange(count * RANK)[None, :]).astype(BF)
        norms = [
            v[None, :]
            for v in (first_norm_scale, first_norm_bias, second_norm_scale, second_norm_bias)
        ]
        (
            w_all,
            qkv,
            kp,
            normed_one,
            mixed,
            lows,
            res_p,
            res_c,
            grad_resid,
            grad_attn,
            low_o,
            packed,
        ) = forward_call(
            x_p,
            x_c,
            cot_p,
            cot_c,
            norms,
            (a_ext, b_ext, a_up, b_up, a_dn, b_dn),
            (frozen_query_key_value, frozen_output_weight, frozen_down_weight, frozen_up_weight),
            n_fs,
            n_shard,
        )
        grad_p, grad_c, t_a, t_b, t_a_up, t_b_up, t_a_dn, t_b_dn = back_call(
            grad_attn,
            mixed,
            low_o,
            lows,
            norms[0],
            a_ext,
            b_ext,
            hot,
            packed,
            qkv,
            kp,
            x_p,
            x_c,
            normed_one,
            grad_resid,
            w_all,
            n_fs,
            count,
        )
        tables = [other_pairs(t) for t in (t_a, t_b, t_a_up, t_b_up, t_a_dn, t_b_dn)]
        res_p, res_c, grad_p, grad_c, t_a, t_b, t_a_up, t_b_up, t_a_dn, t_b_dn = finish_call(
            [res_p, res_c, grad_p, grad_c], tables
        )
        return (
            res_p.reshape(prompt_input_rows.shape),
            res_c.reshape(continuation_input.shape),
            grad_p.reshape(prompt_input_rows.shape),
            grad_c.reshape(continuation_input.shape),
            t_a.swapaxes(2, 3),
            t_b,
            t_a_up.swapaxes(1, 2),
            t_b_up,
            t_a_dn.swapaxes(1, 2),
            t_b_dn,
        )

    return body


def solution(mesh):
    sizes = (mesh.shape["rep"], mesh.shape["grp"], mesh.shape["fs"])
    rows_in = P("rep", "fs", "grp", None)
    conts_in = P("rep", "fs", "grp", None, None)
    weight = P(("grp", "fs"), None)
    return jax.shard_map(
        make_body(sizes),
        mesh=mesh,
        in_specs=(
            rows_in,
            conts_in,
            P("rep", "fs"),
            P("rep", "fs", "grp"),
            P(),
            P(),
            P(),
            P(),
            weight,
            weight,
            weight,
            weight,
            P(),
            P(),
            P(),
            P(),
            P(),
            P(),
            rows_in,
            conts_in,
        ),
        out_specs=(
            rows_in,
            conts_in,
            rows_in,
            conts_in,
            P("fs", None, None, None),
            P("fs", None, None, None),
            P("fs", None, None),
            P("fs", None, None),
            P("fs", None, None),
            P("fs", None, None),
        ),
        check_vma=False,
    )
```
